32 devices in a mesh: dp: 4 (over z), row: 2 (over x), col: 4 (over y, core).
Axes of the slice: x: 2, y: 2, z: 4, core: 2. Of those that a mesh axis runs over, the one named last changes fastest.
Arguments:
- tokens: bfloat16 [2, 8192, 768], P(None, ('dp', 'row', 'col')), may hold values from -6 to 6
- cotangent: bfloat16 [2, 8192, 768], P(None, ('dp', 'row', 'col')), may hold values from -6 to 6
- doc_ids: int32 [2, 4, 2048], P(None, 'dp', ('row', 'col')), may hold values from 0 to 3, never falling along the last dimension, each value on 1 to 1024 neighbouring positions
- proj_weight: bfloat16 [5, 768, 384], P(None, 'row', 'col'), may hold values from -0.21875 to 0.21875
- out_weight: bfloat16 [768, 768], P('row', 'col'), may hold values from -0.625 to 0.625
- inner_weight: bfloat16 [2, 384, 1536], P('row', None, 'col'), may hold values from -0.3125 to 0.3125
- outer_weight: bfloat16 [2, 1536, 384], P('row', 'col'), may hold values from -0.15625 to 0.15625
- depth_weight: bfloat16 [9, 768], replicated, may hold values from -2 to 2
- proj_bias: bfloat16 [4, 384], replicated, may hold values from -3 to 3
- kernel_weight: bfloat16 [384, 54], replicated, may hold values from -0.3125 to 0.3125
- kernel_bias: bfloat16 [54], replicated, may hold values from -3 to 3
- out_bias: bfloat16 [768], replicated, may hold values from -2 to 2
- norm1_gain: bfloat16 [768], replicated, may hold values from 0.5 to 1.5
- norm1_shift: bfloat16 [768], replicated, may hold values from -2 to 2
- inner_bias: bfloat16 [3072], replicated, may hold values from -2 to 2
- outer_bias: bfloat16 [768], replicated, may hold values from -2 to 2
- norm2_gain: bfloat16 [768], replicated, may hold values from 0.5 to 1.5
- norm2_shift: bfloat16 [768], replicated, may hold values from -2 to 2
Outputs:
- output: bfloat16 [2, 8192, 768], P(None, ('dp', 'row', 'col'))
- tokens_grad: float32 [2, 8192, 768], P(None, ('dp', 'row', 'col'))
- proj_weight_grad: float32 [5, 768, 384], P(None, 'row', 'col')
- out_weight_grad: float32 [768, 768], P('row', 'col')
- inner_weight_grad: float32 [2, 384, 1536], P('row', None, 'col')
- outer_weight_grad: float32 [2, 1536, 384], P('row', 'col')
- depth_weight_grad: float32 [9, 768], replicated
- proj_bias_grad: float32 [4, 384], replicated
- kernel_weight_grad: float32 [384, 54], replicated
- kernel_bias_grad: float32 [54], replicated
- out_bias_grad: float32 [768], replicated
- norm1_gain_grad: float32 [768], replicated
- norm1_shift_grad: float32 [768], replicated
- inner_bias_grad: float32 [3072], replicated
- outer_bias_grad: float32 [768], replicated
- norm2_gain_grad: float32 [768], replicated
- norm2_shift_grad: float32 [768], replicated
The draws below stay inside these ranges and needn't reach their ends.
Inputs may be any that keep to these rules, and one draw needn't show every extreme that they name: `doc_ids`: document numbers never fall along a sequence of 2048 tokens; each document has at most 1024 tokens, and one in every sequence has exactly that many.
All inputs are finite; a program needn't handle non-finite values.
Results may differ from the reference program's by a relative error of at most 0.018.
Values may be sent and summed in bfloat16 or wider, within the bound.
No kernel may reach another device: no remote copies, remote signals or barrier semaphores. Data moves between devices by JAX's collectives and lax.ppermute only.
A program may use at most 256 MiB of HBM per device.

```python
import math
import jax
import jax.numpy as jnp
import numpy as np
from jax import lax

D = 768
HEADS = 6
HEAD = 64
KERNEL = 9
FF = 3072
GROUPS = 2
MB = 2
SEQ = 2048
ATT = 384
N_DP = 4


def block_scale(rng, shape, pieces, smallest, top_value):
    level = 1.0
    for position, parts in pieces:
        draws = jax.random.uniform(jax.random.fold_in(jax.random.fold_in(rng, 6), position), (parts,), jnp.float32, smallest / len(pieces), top_value / len(pieces))
        level = level * jnp.repeat(jnp.exp(draws), shape[position] // parts).reshape((-1,) + (1,) * (len(shape) - 1 - position))
    return level


def split_up(count, total, limit, skew):
    loads = [(1 << 20) // math.isqrt(grade ** skew) + 1 for grade in range(2, count + 1)]
    rest, given = total - limit - (count - 1), [1] * (count - 1)
    while rest > 0:
        candidates = [i for i in range(count - 1) if given[i] < limit]
        pool, left = sum([loads[i] for i in candidates]), rest
        for i in candidates:
            addition = min(limit - given[i], max(1, left * loads[i] // pool), rest)
            given[i] = given[i] + addition
            rest = rest - addition
    return np.array([limit] + given)


def ragged(key, count, total, limit, slope):
    if count == 2:
        one = jax.random.randint(key, (), max(1, total - limit), min(limit, total - 1) + 1)
        return jnp.stack([one, total - one])
    sizes = jnp.asarray(split_up(count, total, limit, slope), jnp.int32)
    couples = (count - 1) // 2
    donor, taker = sizes[1:1 + 2 * couples:2], sizes[2:2 + 2 * couples:2]
    slack = jnp.minimum(donor - 1, limit - taker)
    passed = jax.random.randint(jax.random.fold_in(key, 1), (couples,), 0, 1 << 20) % (slack + 1)
    sizes = sizes.at[1:1 + 2 * couples:2].set(donor - passed).at[2:2 + 2 * couples:2].set(taker + passed)
    return sizes[jax.random.permutation(jax.random.fold_in(key, 2), count)]


def scatter_about(key, extent, deviation, reach, shards=(), kind=jnp.bfloat16):
    entries = jax.random.normal(key, extent, jnp.float32) * deviation
    if len(shards) > 0:
        entries = block_scale(key, extent, shards, -0.22, 0.18) * entries
    return jnp.clip(entries, min=-reach, max=reach).astype(kind)


def setup_inputs(seed: int = 0) -> dict:
    keys = jax.random.split(jax.random.key(seed), 19)
    return {
        "tokens": scatter_about(keys[0], (MB, N_DP * SEQ, D), 1.0, 6.0, ((1, 32),)),
        "cotangent": scatter_about(keys[1], (MB, N_DP * SEQ, D), 1.0, 6.0, ((1, 32),)),
        "doc_ids": jax.vmap(lambda own: jnp.searchsorted(jnp.cumsum(ragged(own, 4, SEQ, SEQ // 2, 1)), jnp.arange(SEQ), side="right"))(jax.random.split(keys[2], MB * N_DP)).reshape((MB, N_DP, SEQ)).astype(jnp.int32),
        "proj_weight": scatter_about(keys[3], (5, D, ATT), D ** -0.5, 0.21875, ((1, 2), (2, 4))),
        "out_weight": scatter_about(keys[4], (D, D), (D // 8) ** -0.5, 0.625, ((0, 2), (1, 4))),
        "inner_weight": scatter_about(keys[5], (GROUPS, D // GROUPS, FF // GROUPS), (D // GROUPS) ** -0.5, 0.3125, ((0, 2), (2, 4))),
        "outer_weight": scatter_about(keys[6], (GROUPS, FF // GROUPS, D // GROUPS), (FF // GROUPS) ** -0.5, 0.15625, ((0, 2), (1, 4))),
        "depth_weight": scatter_about(keys[7], (KERNEL, D), KERNEL ** -0.5, 2.0),
        "proj_bias": scatter_about(keys[8], (4, ATT), 0.5, 3.0),
        "kernel_weight": scatter_about(keys[9], (ATT, HEADS * KERNEL), ATT ** -0.5, 0.3125),
        "kernel_bias": scatter_about(keys[10], (HEADS * KERNEL,), 0.5, 3.0),
        "out_bias": scatter_about(keys[11], (D,), 0.3, 2.0),
        "norm1_gain": jnp.clip(1.0 + 0.1 * jax.random.normal(keys[12], (D,), jnp.float32), 0.5, 1.5).astype(jnp.bfloat16),
        "norm1_shift": scatter_about(keys[13], (D,), 0.3, 2.0),
        "inner_bias": scatter_about(keys[14], (FF,), 0.3, 2.0),
        "outer_bias": scatter_about(keys[15], (D,), 0.3, 2.0),
        "norm2_gain": jnp.clip(1.0 + 0.1 * jax.random.normal(keys[16], (D,), jnp.float32), 0.5, 1.5).astype(jnp.bfloat16),
        "norm2_shift": scatter_about(keys[17], (D,), 0.3, 2.0),
    }


@jax.custom_vjp
def low(v):
    return lax.optimization_barrier(v.astype(jnp.bfloat16)).astype(jnp.float32)

@jax.custom_vjp
def low_back(v):
    return v

def low_keep(v):
    return (low(v), None)

def low_pass(kept, grad):
    return (grad,)

def back_keep(v):
    return (v, None)

def back_low(kept, grad):
    return (low(grad),)
low.defvjp(low_keep, low_pass)
low_back.defvjp(back_keep, back_low)
PRECISE = lax.Precision.HIGHEST
EPSILON = 1e-12
MASKED = -1e+30

def rounded(values_in):
    return low(low_back(values_in))

def matmul(left_side, right_side):
    return jnp.dot(left_side, right_side, precision=PRECISE)

def norm_rows(values_in, norm_gain, norm_shift):
    row_mean = lax.optimization_barrier(jnp.mean(values_in, axis=-1, keepdims=True))
    centred = values_in - row_mean
    row_var = lax.optimization_barrier(jnp.mean(centred * centred, axis=-1, keepdims=True))
    return centred * lax.rsqrt(row_var + EPSILON) * norm_gain + norm_shift

def doc_taps(doc_row):
    length = doc_row.shape[0]
    margin = KERNEL // 2
    padded = jnp.pad(doc_row, (margin, margin), constant_values=-1)
    return jnp.stack([padded[offset:offset + length] == doc_row for offset in range(KERNEL)], axis=1)

def conv_softmax(logits, tap_mask):
    allowed = tap_mask[:, None, :]
    masked = jnp.where(allowed, logits, MASKED)
    row_top = lax.optimization_barrier(jnp.max(masked, axis=-1, keepdims=True))
    exp_terms = jnp.where(allowed, jnp.exp(masked - row_top), 0.0)
    return exp_terms / lax.optimization_barrier(jnp.sum(exp_terms, axis=-1, keepdims=True))

def attention(query_low, key_low, value_low, doc_row):
    length = query_low.shape[0]
    block_len = min(512, length)
    query_blocks = query_low.reshape(length // block_len, block_len, HEADS, HEAD)
    key_heads = key_low.reshape(length, HEADS, HEAD)
    value_heads = value_low.reshape(length, HEADS, HEAD)
    score_scale = HEAD ** (-0.5)

    def one_block(block_item):
        query_block, doc_block = block_item
        raw_scores = jnp.einsum('qhd,khd->hqk', query_block, key_heads, precision=PRECISE)
        scores = low_back(raw_scores * score_scale)
        same_doc = (doc_block[:, None] == doc_row[None, :])[None]
        masked = jnp.where(same_doc, scores, MASKED)
        row_top = lax.optimization_barrier(jnp.max(masked, axis=-1, keepdims=True))
        exp_terms = jnp.exp(masked - row_top)
        probs_low = low(exp_terms / lax.optimization_barrier(jnp.sum(exp_terms, axis=-1, keepdims=True)))
        return jnp.einsum('hqk,khd->qhd', probs_low, value_heads, precision=PRECISE)
    blocks_out = lax.map(jax.checkpoint(one_block), (query_blocks, doc_row.reshape(length // block_len, block_len)))
    return blocks_out.reshape(length, ATT)

def sequence_layer(tokens_seq, doc_row, params):
    proj_weight, out_weight, inner_weight, outer_weight, depth_weight, proj_bias, kernel_weight, kernel_bias, out_bias, norm1_gain, norm1_shift, inner_bias, outer_bias, norm2_gain, norm2_shift = params
    length = tokens_seq.shape[0]
    margin = KERNEL // 2
    tap_mask = doc_taps(doc_row)
    padded = jnp.pad(tokens_seq, ((margin, margin), (0, 0)))
    depthwise = low(sum((depth_weight[offset] * jnp.where(tap_mask[:, offset:offset + 1], padded[offset:offset + length], 0.0) for offset in range(KERNEL))))
    query_low = rounded(matmul(tokens_seq, proj_weight[0]) + proj_bias[0])
    key_low = rounded(matmul(tokens_seq, proj_weight[1]))
    value_low = rounded(matmul(tokens_seq, proj_weight[2]) + proj_bias[1])
    conv_value = rounded(matmul(tokens_seq, proj_weight[3]) + proj_bias[2])
    key_conv = low_back(matmul(depthwise, proj_weight[4]) + proj_bias[3])
    conv_attn = low(query_low * key_conv)
    logits = low_back(matmul(conv_attn, kernel_weight) + kernel_bias).reshape(length, HEADS, KERNEL)
    conv_weights = conv_softmax(logits, tap_mask)
    conv_padded = jnp.pad(conv_value, ((margin, margin), (0, 0))).reshape(length + 2 * margin, HEADS, HEAD)
    conv_context = sum((conv_weights[:, :, offset:offset + 1] * conv_padded[offset:offset + length] for offset in range(KERNEL)))
    attended = attention(query_low, key_low, value_low, doc_row)
    context = rounded(jnp.concatenate([attended, conv_context.reshape(length, ATT)], axis=1))
    attn_out = low_back(matmul(context, out_weight) + out_bias)
    hidden = norm_rows(tokens_seq + attn_out, norm1_gain, norm1_shift)
    grouped = low(hidden).reshape(length, GROUPS, D // GROUPS)
    inner_pre = low_back(jnp.einsum('tga,gab->tgb', grouped, inner_weight, precision=PRECISE).reshape(length, FF) + inner_bias)
    active = low(jax.nn.gelu(inner_pre, approximate=False)).reshape(length, GROUPS, FF // GROUPS)
    ffn_out = low_back(jnp.einsum('tga,gab->tgb', active, outer_weight, precision=PRECISE).reshape(length, D) + outer_bias)
    return norm_rows(hidden + ffn_out, norm2_gain, norm2_shift)

def reference(tokens, cotangent, doc_ids, proj_weight, out_weight, inner_weight, outer_weight, depth_weight, proj_bias, kernel_weight, kernel_bias, out_bias, norm1_gain, norm1_shift, inner_bias, outer_bias, norm2_gain, norm2_shift):
    params = tuple((weight_item.astype(jnp.float32) for weight_item in (proj_weight, out_weight, inner_weight, outer_weight, depth_weight, proj_bias, kernel_weight, kernel_bias, out_bias, norm1_gain, norm1_shift, inner_bias, outer_bias, norm2_gain, norm2_shift)))
    seq_count = MB * N_DP
    inputs = tokens.astype(jnp.float32).reshape(seq_count, SEQ, D)
    doc_rows = doc_ids.reshape(seq_count, SEQ)
    layer_fn = jax.checkpoint(sequence_layer)

    def forward(inputs_all, params_all):

        def scan_step(scan_carry, seq_item):
            return (scan_carry, layer_fn(seq_item[0], seq_item[1], params_all))
        return lax.scan(scan_step, jnp.zeros((), jnp.float32), (inputs_all, doc_rows))[1]
    output, pullback = jax.vjp(forward, inputs, params)
    grad_inputs, grad_params = pullback(cotangent.astype(jnp.float32).reshape(seq_count, SEQ, D))
    return (output.astype(jnp.bfloat16).reshape(MB, N_DP * SEQ, D), grad_inputs.reshape(MB, N_DP * SEQ, D), grad_params[0], grad_params[1], grad_params[2], grad_params[3], grad_params[4], grad_params[5], grad_params[6], grad_params[7], grad_params[8], grad_params[9], grad_params[10], grad_params[11], grad_params[12], grad_params[13], grad_params[14])
```

```python
import jax
import jax.numpy as jnp
from jax import lax
from jax.sharding import PartitionSpec as P

HEADS = 6
HEAD = 64
KERNEL = 9
FF = 3072
ATT = 384
PARTS = 5

EPSILON = 1e-12
MASKED = -1e30
LOW = jnp.bfloat16
WIDE = jnp.float32


def swap(block, axis, step):
    count = lax.axis_size(axis)
    return lax.ppermute(block, axis, [(i, i ^ step) for i in range(count)])


def shift(block, axis, step):
    count = lax.axis_size(axis)
    return lax.ppermute(block, axis, [(i, (i + step) % count) for i in range(count)])


def steps_of(axis):
    steps = []
    step = 1
    while step < lax.axis_size(axis):
        steps.append(step)
        step *= 2
    return steps


def pick(block, index):
    return lax.dynamic_index_in_dim(block, index, 0, keepdims=False)


def norm_rows(values_in, norm_gain, norm_shift):
    row_mean = jnp.mean(values_in, axis=-1, keepdims=True)
    centred = values_in - row_mean
    row_var = jnp.mean(centred * centred, axis=-1, keepdims=True)
    return centred * lax.rsqrt(row_var + EPSILON) * norm_gain + norm_shift


def conv_softmax(logits, tap_mask):
    allowed = tap_mask[:, None, :]
    masked = jnp.where(allowed, logits, MASKED)
    row_top = jnp.max(masked, axis=-1, keepdims=True)
    exp_terms = jnp.where(allowed, jnp.exp(masked - row_top), 0.0)
    return exp_terms / jnp.sum(exp_terms, axis=-1, keepdims=True)


def gelu_exact(values_in):
    return jax.nn.gelu(values_in, approximate=False)


def gather_grid(slab):
    half = slab.shape[0] // 2
    far = [step for step in steps_of("col") if step > 1]
    first = {(0, 0): slab[:half]}
    second = {(0, 0): slab[half:]}

    def grow_row(held):
        keys = list(held)
        moved = swap(jnp.stack([held[key] for key in keys]), "row", 1)
        for place, key in enumerate(keys):
            held[(key[0] ^ 1, key[1])] = moved[place]

    def grow_col(held, step):
        keys = list(held)
        moved = swap(jnp.stack([held[key] for key in keys]), "col", step)
        for place, key in enumerate(keys):
            held[(key[0], key[1] ^ step)] = moved[place]

    grow_row(first)
    grow_col(second, far[0])
    grow_col(first, far[0])
    grow_row(second)
    for step in far[1:]:
        grow_col(first, step)
        grow_col(second, step)
    grow_col(first, 1)
    grow_col(second, 1)
    return [
        [
            jnp.concatenate([first[(dr, dc)], second[(dr, dc)]], axis=0)
            for dc in range(lax.axis_size("col"))
        ]
        for dr in range(lax.axis_size("row"))
    ]


def to_absolute(grid):
    row_count = len(grid)
    col_count = len(grid[0])
    stacked = jnp.stack([jnp.stack(line) for line in grid])
    row_here = lax.axis_index("row")
    col_here = lax.axis_index("col")
    return jnp.stack(
        [
            jnp.stack(
                [
                    pick(pick(stacked, row_here ^ dr), col_here ^ dc)
                    for dc in range(col_count)
                ]
            )
            for dr in range(row_count)
        ]
    )


def scatter_grid(slabs):
    slabs = slabs.astype(LOW)
    half = slabs.shape[2] // 2
    far = [step for step in steps_of("col") if step > 1]

    def add(kept, moved):
        return (kept.astype(WIDE) + moved.astype(WIDE)).astype(LOW)

    row_count, col_count = slabs.shape[:2]
    held = {(dr, dc): slabs[dr, dc] for dr in range(row_count) for dc in range(col_count)}

    def fold(held, axis, step, chosen):
        keys = [key for key in held if not chosen(key)]
        gone = [(key[0] ^ step, key[1]) if axis == "row" else (key[0], key[1] ^ step) for key in keys]
        moved = swap(jnp.stack([held[key] for key in gone]), axis, step)
        return {key: add(held[key], moved[place]) for place, key in enumerate(keys)}

    held = fold(held, "col", 1, lambda key: key[1] & 1)
    first = {key: held[key][:half] for key in held}
    second = {key: held[key][half:] for key in held}
    for step in far[1:]:
        first = fold(first, "col", step, lambda key: key[1] & step)
        second = fold(second, "col", step, lambda key: key[1] & step)
    first = fold(first, "row", 1, lambda key: key[0] & 1)
    second = fold(second, "col", far[0], lambda key: key[1] & far[0])
    first = fold(first, "col", far[0], lambda key: key[1] & far[0])
    second = fold(second, "row", 1, lambda key: key[0] & 1)
    return jnp.concatenate([first[(0, 0)], second[(0, 0)]], axis=0)


def data_sum(part):
    index = lax.axis_index("dp")
    steps = steps_of("dp")
    sent = part.dtype
    for step in steps:
        bit = (index // step) % 2
        halves = part.reshape((2, part.shape[0] // 2) + part.shape[1:])
        moved = swap(pick(halves, 1 - bit), "dp", step)
        part = (pick(halves, bit).astype(WIDE) + moved.astype(WIDE)).astype(sent)
    for step in reversed(steps):
        bit = (index // step) % 2
        moved = swap(part, "dp", step)
        both = jnp.stack([part, moved])
        part = jnp.concatenate([pick(both, bit), pick(both, 1 - bit)], axis=0)
    return part


def local(
    tokens,
    cotangent,
    doc_ids,
    proj_weight,
    out_weight,
    inner_weight,
    outer_weight,
    depth_weight,
    proj_bias,
    kernel_weight,
    kernel_bias,
    out_bias,
    norm1_gain,
    norm1_shift,
    inner_bias,
    outer_bias,
    norm2_gain,
    norm2_shift,
):
    block_len = tokens.shape[1]
    model_width = tokens.shape[2]
    margin = KERNEL // 2
    row_count = lax.axis_size("row")
    col_count = lax.axis_size("col")
    row_here = lax.axis_index("row")
    col_here = lax.axis_index("col")
    tokens_here = 2 * block_len
    score_scale = HEAD ** (-0.5)
    depth_gain = depth_weight.astype(WIDE)
    bias_proj = proj_bias.astype(WIDE)
    bias_kernel = kernel_bias.astype(WIDE)
    bias_out = out_bias.astype(WIDE)
    gain_first = norm1_gain.astype(WIDE)
    shift_first = norm1_shift.astype(WIDE)
    bias_inner = inner_bias.astype(WIDE)
    bias_outer = outer_bias.astype(WIDE)
    gain_second = norm2_gain.astype(WIDE)
    shift_second = norm2_shift.astype(WIDE)

    slab_proj = jnp.transpose(proj_weight, (0, 2, 1)).reshape(-1, proj_weight.shape[1])
    slab_rest = jnp.concatenate([out_weight.T, inner_weight[0].T, outer_weight[0]], axis=0)
    proj_abs = to_absolute(gather_grid(slab_proj))
    rest_abs = to_absolute(gather_grid(slab_rest))
    lanes = slab_proj.shape[1]
    proj_t = proj_abs.reshape(row_count, col_count, PARTS, -1, lanes)
    cut_out = out_weight.shape[1]
    cut_inner = cut_out + inner_weight.shape[2]
    out_t = rest_abs[:, :, :cut_out]
    inner_t = rest_abs[:, :, cut_out:cut_inner]
    outer_full = rest_abs[:, :, cut_inner:]

    def trade(pair):
        return jnp.stack([pick(pair, row_here), swap(pick(pair, 1 - row_here), "row", 1)])

    own = trade(tokens)
    cot = trade(cotangent).reshape(tokens_here, model_width)

    def rims(last, first):
        wrap_low = col_here == 0
        wrap_high = col_here == col_count - 1
        low = shift(last, "col", 1)
        high = shift(first, "col", -1)
        low = jnp.where(wrap_low, low[::-1], low)
        high = jnp.where(wrap_high, high[::-1], high)
        return low, high

    low_rim, high_rim = rims(own[:, block_len - margin :], own[:, :margin])
    extended = jnp.concatenate([low_rim, own, high_rim], axis=1)
    own_rows = own.reshape(tokens_here, model_width)

    docs = trade(doc_ids[:, 0])[None]
    for step in reversed(steps_of("col")):
        docs = jnp.concatenate([docs, swap(docs, "col", step)], axis=0)
    order = [0]
    for step in reversed(steps_of("col")):
        order = order + [entry ^ step for entry in order]
    ordered = jnp.stack([docs[order.index(dc)] for dc in range(col_count)])
    doc_seq = jnp.concatenate(
        [
            pick(pick(ordered, col_here ^ dc), row_here ^ dr)
            for dr in range(row_count)
            for dc in range(col_count)
        ]
    )
    doc_keys = ordered.reshape(-1)
    doc_padded = jnp.pad(doc_seq, (margin, margin), constant_values=-1)
    starts = [
        ((row_here ^ slot) * col_count + col_here) * block_len for slot in range(2)
    ]
    doc_ext = jnp.stack(
        [lax.dynamic_slice_in_dim(doc_padded, start, block_len + 2 * margin) for start in starts]
    )
    doc_own = doc_ext[:, margin : margin + block_len]
    tap_mask = jnp.stack(
        [doc_ext[:, offset : offset + block_len] == doc_own for offset in range(KERNEL)], axis=2
    ).reshape(tokens_here, KERNEL)
    doc_rows = doc_own.reshape(tokens_here)

    def taps_of(ext):
        width = ext.shape[2:]
        return [
            ext[:, offset : offset + block_len].reshape((tokens_here,) + width)
            for offset in range(KERNEL)
        ]

    shifted = [
        jnp.where(tap_mask[:, offset : offset + 1], piece.astype(WIDE), 0.0)
        for offset, piece in enumerate(taps_of(extended))
    ]
    depth_low = sum((depth_gain[offset] * shifted[offset] for offset in range(KERNEL))).astype(LOW)
    split_depth = depth_low.reshape(tokens_here, row_count, -1)
    split_tokens = own_rows.reshape(tokens_here, row_count, -1)
    mixed_proj = jnp.einsum(
        "tra,rcjba->jtcb", split_tokens, proj_t[:, :, :3], preferred_element_type=WIDE
    ).reshape(3, tokens_here, ATT)
    query_low = (mixed_proj[0] + bias_proj[0]).astype(LOW)
    key_low = mixed_proj[1].astype(LOW)
    value_low = (mixed_proj[2] + bias_proj[1]).astype(LOW)
    conv_ext = (
        jnp.einsum(
            "stra,rcba->stcb",
            extended.reshape(2, block_len + 2 * margin, row_count, -1),
            proj_t[:, :, 3],
            preferred_element_type=WIDE,
        ).reshape(2, block_len + 2 * margin, ATT)
        + bias_proj[2]
    ).astype(LOW)
    conv_taps = [piece.reshape(tokens_here, HEADS, HEAD) for piece in taps_of(conv_ext)]
    key_conv = (
        jnp.einsum(
            "tra,rcba->tcb", split_depth, proj_t[:, :, 4], preferred_element_type=WIDE
        ).reshape(tokens_here, ATT)
        + bias_proj[3]
    )
    conv_attn = (query_low.astype(WIDE) * key_conv).astype(LOW)
    logits = (
        jnp.dot(conv_attn, kernel_weight, preferred_element_type=WIDE) + bias_kernel
    ).reshape(tokens_here, HEADS, KERNEL)
    conv_weights = conv_softmax(logits, tap_mask)
    conv_context = sum(
        (conv_weights[:, :, offset : offset + 1] * conv_taps[offset] for offset in range(KERNEL))
    )

    pair = jnp.concatenate([key_low, value_low], axis=1)[None]
    for step in reversed(steps_of("col")):
        pair = jnp.concatenate([pair, swap(pair, "col", step)], axis=0)
    pair = jnp.concatenate([pair[order.index(dc)] for dc in range(col_count)], axis=0)
    keys_all = pair[:, :ATT]
    values_all = pair[:, ATT:]

    same_doc = doc_rows[:, None] == doc_keys[None, :]
    head_outs = []
    row_tops = []
    row_totals = []
    for head_index in range(HEADS):
        columns = slice(head_index * HEAD, (head_index + 1) * HEAD)
        raw_scores = (
            jnp.einsum(
                "qd,kd->qk", query_low[:, columns], keys_all[:, columns], preferred_element_type=WIDE
            )
            * score_scale
        )
        masked = jnp.where(same_doc, raw_scores, MASKED)
        row_top = jnp.max(masked, axis=-1, keepdims=True)
        exp_terms = jnp.exp(masked - row_top)
        row_total = jnp.sum(exp_terms, axis=-1, keepdims=True)
        probs_low = (exp_terms / row_total).astype(LOW)
        head_outs.append(jnp.dot(probs_low, values_all[:, columns], preferred_element_type=WIDE))
        row_tops.append(row_top)
        row_totals.append(row_total)
    attended = jnp.concatenate(head_outs, axis=1)
    context = jnp.concatenate([attended, conv_context.reshape(tokens_here, ATT)], axis=1).astype(LOW)
    split_context = context.reshape(tokens_here, row_count, -1)
    attn_out = (
        jnp.einsum(
            "tra,rcba->tcb", split_context, out_t, preferred_element_type=WIDE
        ).reshape(tokens_here, model_width)
        + bias_out
    )
    resid_first = own_rows.astype(WIDE) + attn_out
    hidden = norm_rows(resid_first, gain_first, shift_first)
    hidden_low = hidden.astype(LOW).reshape(tokens_here, row_count, -1)
    inner_pre = (
        jnp.einsum(
            "tra,rcba->trcb", hidden_low, inner_t, preferred_element_type=WIDE
        ).reshape(tokens_here, FF)
        + bias_inner
    )
    active = gelu_exact(inner_pre).astype(LOW)
    split_active = active.reshape(tokens_here, row_count, col_count, -1)
    ffn_out = (
        jnp.einsum(
            "trca,rcab->trb", split_active, outer_full, preferred_element_type=WIDE
        ).reshape(tokens_here, model_width)
        + bias_outer
    )
    resid_second = hidden + ffn_out
    output = norm_rows(resid_second, gain_second, shift_second).astype(LOW)

    norm2_back = jax.vjp(norm_rows, resid_second, gain_second, shift_second)[1]
    g_resid2, g_gain2, g_shift2 = norm2_back(cot.astype(WIDE))
    g_ffn = g_resid2.astype(LOW)
    split_gffn = g_ffn.reshape(tokens_here, row_count, -1)
    d_outer_w = jnp.einsum("trca,trb->rcab", split_active, split_gffn, preferred_element_type=WIDE)
    g_active = jnp.einsum(
        "trb,rcab->trca", split_gffn, outer_full, preferred_element_type=WIDE
    ).reshape(tokens_here, FF)
    gelu_back = jax.vjp(gelu_exact, inner_pre)[1]
    g_inner = gelu_back(g_active)[0].astype(LOW)
    split_ginner = g_inner.reshape(tokens_here, row_count, col_count, -1)
    d_inner_w = jnp.einsum("tra,trcb->rcba", hidden_low, split_ginner, preferred_element_type=WIDE)
    g_hidden = g_resid2 + jnp.einsum(
        "trcb,rcba->tra", split_ginner, inner_t, preferred_element_type=WIDE
    ).reshape(tokens_here, model_width)
    norm1_back = jax.vjp(norm_rows, resid_first, gain_first, shift_first)[1]
    g_resid1, g_gain1, g_shift1 = norm1_back(g_hidden)
    g_attn = g_resid1.astype(LOW)
    split_gattn = g_attn.reshape(tokens_here, col_count, -1)
    d_out_w = jnp.einsum("tra,tcb->rcba", split_context, split_gattn, preferred_element_type=WIDE)
    g_context = (
        jnp.einsum("tcb,rcba->tra", split_gattn, out_t, preferred_element_type=WIDE)
        .reshape(tokens_here, model_width)
        .astype(LOW)
    )
    g_attention = g_context[:, :ATT]
    g_conv = g_context[:, ATT:].astype(WIDE).reshape(tokens_here, HEADS, HEAD)
    g_conv_w = jnp.stack([jnp.sum(g_conv * piece, axis=-1) for piece in conv_taps], axis=-1)
    softmax_back = jax.vjp(lambda logit_values: conv_softmax(logit_values, tap_mask), logits)[1]
    g_logits = softmax_back(g_conv_w)[0].reshape(tokens_here, HEADS * KERNEL).astype(LOW)
    d_kernel_w = jnp.dot(conv_attn.T, g_logits, preferred_element_type=WIDE)
    g_conv_attn = jnp.dot(g_logits, kernel_weight.T, preferred_element_type=WIDE)

    def spread(pieces):
        return sum(
            (
                jnp.pad(
                    piece.reshape(2, block_len, -1),
                    ((0, 0), (offset, 2 * margin - offset), (0, 0)),
                )
                for offset, piece in enumerate(pieces)
            )
        )

    g_ext_value = spread(
        [conv_weights[:, :, offset : offset + 1] * g_conv for offset in range(KERNEL)]
    )
    g_key_conv = (g_conv_attn * query_low.astype(WIDE)).astype(LOW)
    split_gkc = g_key_conv.reshape(tokens_here, col_count, -1)
    d_point_w = jnp.einsum("tra,tcb->rcba", split_depth, split_gkc, preferred_element_type=WIDE)
    g_depth_in = jnp.einsum(
        "tcb,rcba->tra", split_gkc, proj_t[:, :, 4], preferred_element_type=WIDE
    ).reshape(tokens_here, model_width)
    d_depth = jnp.stack([jnp.sum(g_depth_in * piece, axis=0) for piece in shifted])
    g_ext_tokens = spread(
        [
            jnp.where(tap_mask[:, offset : offset + 1], g_depth_in * depth_gain[offset], 0.0)
            for offset in range(KERNEL)
        ]
    )
    query_terms = []
    key_terms = []
    value_terms = []
    for head_index in range(HEADS):
        columns = slice(head_index * HEAD, (head_index + 1) * HEAD)
        raw_scores = (
            jnp.einsum(
                "qd,kd->qk", query_low[:, columns], keys_all[:, columns], preferred_element_type=WIDE
            )
            * score_scale
        )
        masked = jnp.where(same_doc, raw_scores, MASKED)
        probs_full = jnp.exp(masked - row_tops[head_index]) / row_totals[head_index]
        g_probs = jnp.einsum(
            "qd,kd->qk", g_attention[:, columns], values_all[:, columns], preferred_element_type=WIDE
        )
        row_delta = jnp.sum(probs_full * g_probs, axis=-1, keepdims=True)
        g_scores = (probs_full * (g_probs - row_delta)).astype(LOW)
        query_terms.append(
            jnp.dot(g_scores, keys_all[:, columns], preferred_element_type=WIDE) * score_scale
        )
        probs_low = probs_full.astype(LOW)
        key_terms.append(
            jnp.einsum("qk,qd->kd", g_scores, query_low[:, columns], preferred_element_type=WIDE)
            * score_scale
        )
        value_terms.append(
            jnp.einsum("qk,qd->kd", probs_low, g_attention[:, columns], preferred_element_type=WIDE)
        )
    pair_grads = jnp.concatenate(key_terms + value_terms, axis=1).astype(LOW)
    pair_grads = pair_grads.reshape(col_count, tokens_here, 2 * ATT)
    held = {dc: pair_grads[dc] for dc in range(col_count)}
    for step in steps_of("col"):
        keys = [dc for dc in held if not dc & step]
        moved = swap(jnp.stack([held[dc ^ step] for dc in keys]), "col", step)
        held = {
            dc: (held[dc].astype(WIDE) + moved[place].astype(WIDE)).astype(LOW)
            for place, dc in enumerate(keys)
        }
    g_key = held[0][:, :ATT]
    g_value = held[0][:, ATT:]

    ext_grads = jnp.concatenate([g_ext_value, g_ext_tokens], axis=2)
    from_after, from_before = (
        shift(ext_grads[:, :margin].astype(LOW), "col", -1),
        shift(ext_grads[:, margin + block_len :].astype(LOW), "col", 1),
    )
    from_after = jnp.where(col_here == col_count - 1, from_after[::-1], from_after)
    from_before = jnp.where(col_here == 0, from_before[::-1], from_before)
    rim_total = jnp.pad(
        from_before.astype(WIDE), ((0, 0), (0, block_len - margin), (0, 0))
    ) + jnp.pad(from_after.astype(WIDE), ((0, 0), (block_len - margin, 0), (0, 0)))
    ext_total = (ext_grads[:, margin : margin + block_len] + rim_total).reshape(tokens_here, -1)
    g_value_conv = ext_total[:, :ATT].astype(LOW)
    g_tokens_depth = ext_total[:, ATT:]
    g_query = (jnp.concatenate(query_terms, axis=1) + g_conv_attn * key_conv).astype(LOW)
    g_mixed = jnp.stack([g_query, g_key, g_value, g_value_conv]).reshape(
        4, tokens_here, col_count, -1
    )
    d_proj_tokens = jnp.einsum(
        "tra,jtcb->rcjba", split_tokens, g_mixed, preferred_element_type=WIDE
    )
    d_proj = jnp.concatenate([d_proj_tokens, d_point_w[:, :, None]], axis=2)
    token_grad = (
        g_resid1
        + jnp.einsum(
            "jtcb,rcjba->tra", g_mixed, proj_t[:, :, :4], preferred_element_type=WIDE
        ).reshape(tokens_here, model_width)
        + g_tokens_depth
    )
    d_proj_bias = jnp.stack(
        [
            jnp.sum(g_query.astype(WIDE), axis=0),
            jnp.sum(g_value.astype(WIDE), axis=0),
            jnp.sum(g_value_conv.astype(WIDE), axis=0),
            jnp.sum(g_key_conv.astype(WIDE), axis=0),
        ]
    )
    smalls = [
        d_depth,
        d_proj_bias,
        d_kernel_w,
        jnp.sum(g_logits.astype(WIDE), axis=0),
        jnp.sum(g_attn.astype(WIDE), axis=0),
        g_gain1,
        g_shift1,
        jnp.sum(g_inner.astype(WIDE), axis=0),
        jnp.sum(g_ffn.astype(WIDE), axis=0),
        g_gain2,
        g_shift2,
    ]
    flat = jnp.concatenate([item.reshape(-1) for item in smalls])
    total_len = flat.shape[0]
    flat = jnp.pad(flat, (0, -total_len % 1024)).reshape(-1, 128)
    for axis in ("col", "row", "dp"):
        for step in steps_of(axis):
            flat = flat + swap(flat, axis, step)
    flat = flat.reshape(-1)
    finals = []
    start = 0
    for item in smalls:
        finals.append(flat[start : start + item.size].reshape(item.shape))
        start += item.size

    def to_relative(slabs):
        return jnp.stack(
            [
                jnp.stack(
                    [pick(pick(slabs, row_here ^ dr), col_here ^ dc) for dc in range(col_count)]
                )
                for dr in range(row_count)
            ]
        )

    grads_rest = jnp.concatenate([d_out_w, d_inner_w, d_outer_w], axis=2).astype(LOW)
    rest_sum = data_sum(scatter_grid(to_relative(grads_rest))).astype(WIDE)
    grads_proj = d_proj.reshape(row_count, col_count, -1, lanes).astype(LOW)
    proj_sum = data_sum(scatter_grid(to_relative(grads_proj))).astype(WIDE)

    def give_back(rows):
        pair_rows = rows.reshape(2, block_len, model_width)
        both = jnp.stack([pair_rows[0], swap(pair_rows[1].astype(LOW), "row", 1).astype(rows.dtype)])
        return jnp.where(row_here == 0, both, both[::-1])

    return (
        give_back(output),
        give_back(token_grad),
        jnp.transpose(proj_sum.reshape(PARTS, -1, lanes), (0, 2, 1)),
        rest_sum[:cut_out].T,
        rest_sum[cut_out:cut_inner].T[None],
        rest_sum[cut_inner:][None],
        *finals,
    )


def solution(mesh):
    return jax.shard_map(
        local,
        mesh=mesh,
        in_specs=(
            P(None, ("dp", "row", "col"), None),
            P(None, ("dp", "row", "col"), None),
            P(None, "dp", ("row", "col")),
            P(None, "row", "col"),
            P("row", "col"),
            P("row", None, "col"),
            P("row", "col", None),
        )
        + (P(),) * 11,
        out_specs=(
            P(None, ("dp", "row", "col"), None),
            P(None, ("dp", "row", "col"), None),
            P(None, "row", "col"),
            P("row", "col"),
            P("row", None, "col"),
            P("row", "col", None),
        )
        + (P(),) * 11,
        check_vma=False,
    )
```

```python
import functools

import jax
import jax.numpy as jnp
from jax import lax
from jax.experimental import pallas as pl
from jax.experimental.pallas import tpu as pltpu
from jax.sharding import PartitionSpec as P

HEADS = 6
HEAD = 64
KERNEL = 9
FF = 3072
ATT = 384
PAIRS = HEADS // 2
LANE = 128
RIM = 8

EPSILON = 1e-12
MASKED = -1e30
LOW = jnp.bfloat16
WIDE = jnp.float32


def swap(block, axis, step):
    count = lax.axis_size(axis)
    return lax.ppermute(block, axis, [(i, i ^ step) for i in range(count)])


def shift(block, axis, step):
    count = lax.axis_size(axis)
    return lax.ppermute(block, axis, [(i, (i + step) % count) for i in range(count)])


def steps_of(axis):
    steps = []
    step = 1
    while step < lax.axis_size(axis):
        steps.append(step)
        step *= 2
    return steps


def pick(block, index):
    return lax.dynamic_index_in_dim(block, index, 0, keepdims=False)


NT = (((1,), (1,)), ((), ()))
NN = (((1,), (0,)), ((), ()))
TN = (((0,), (0,)), ((), ()))


def mm(left, right, how):
    return lax.dot_general(left, right, how, preferred_element_type=WIDE)


def kernel_call(body, outs, scratch=(), smem=1, cost=None):
    def run(*args):
        specs = [
            pl.BlockSpec(memory_space=pltpu.SMEM if place < smem else pltpu.VMEM)
            for place in range(len(args))
        ]
        return pl.pallas_call(
            body,
            in_specs=specs,
            out_specs=[pl.BlockSpec(memory_space=pltpu.VMEM)] * len(outs),
            out_shape=[jax.ShapeDtypeStruct(shape, kind) for shape, kind in outs],
            scratch_shapes=[pltpu.VMEM(shape, kind) for shape, kind in scratch],
            cost_estimate=cost,
        )(*args)

    return run


def place_of(entry, kind):
    if kind == "col":
        entry = (entry & 1) * 2 + (entry // 2) % 2 + (entry // 4) * 4
    return entry % 2, (entry // 2) * 2


def stages_of(kind):
    far = [("col", step) for step in steps_of("col") if step > 1]
    row = [("row", 1)]
    return row + far if kind == "row" else far[:1] + row + far[1:]


def gather(slab, kind):
    stack = slab[None]
    for axis, step in stages_of(kind):
        stack = jnp.concatenate([stack, swap(stack, axis, step)], axis=0)
    return stack, swap(stack, "col", 1)


def add_low(kept, moved):
    return (kept.astype(WIDE) + moved.astype(WIDE)).astype(LOW)


def scatter(kept, sent, kind):
    stack = add_low(kept, swap(sent, "col", 1))
    for axis, step in reversed(stages_of(kind)):
        half = stack.shape[0] // 2
        stack = add_low(stack[:half], swap(stack[half:], axis, step))
    return stack[0]


def data_sum(part):
    index = lax.axis_index("dp")
    steps = steps_of("dp")
    sent = part.dtype
    for step in steps:
        bit = (index // step) % 2
        halves = part.reshape((2, part.shape[0] // 2) + part.shape[1:])
        moved = swap(pick(halves, 1 - bit), "dp", step)
        part = (pick(halves, bit).astype(WIDE) + moved.astype(WIDE)).astype(sent)
    for step in reversed(steps):
        bit = (index // step) % 2
        moved = swap(part, "dp", step)
        both = jnp.stack([part, moved])
        part = jnp.concatenate([pick(both, bit), pick(both, 1 - bit)], axis=0)
    return part


def grid_sum(flat):
    for axis in ("col", "row", "dp"):
        for step in steps_of(axis):
            flat = flat + swap(flat, axis, step)
    return flat


def assemble(here, stacks, kind, full, parts, size, start):
    for core, stack in enumerate(stacks):

        def one(entry, carry):
            dr, dc = place_of(entry, kind)
            row = here[0] ^ dr
            col = here[1] ^ (dc + core)
            for part in range(parts):
                full[part, row, pl.ds(pl.multiple_of(col * size, 16), size), :] = stack[
                    entry, start + part * size : start + (part + 1) * size, :
                ]
            return carry

        lax.fori_loop(0, stack.shape[0], one, 0)


def cut(here, full, outs, kind, parts, size, start):
    for core, out in enumerate(outs):

        def one(entry, carry):
            dr, dc = place_of(entry, kind)
            row = here[0] ^ dr
            col = here[1] ^ (dc + core)
            for part in range(parts):
                out[entry, start + part * size : start + (part + 1) * size, :] = full[
                    part, row, pl.ds(pl.multiple_of(col * size, 16), size), :
                ]
            return carry

        lax.fori_loop(0, out.shape[0], one, 0)


def two(left, right):
    return jnp.concatenate([left, right], axis=1)


def half_pair(value):
    return value[:, : value.shape[1] // 2], value[:, value.shape[1] // 2 :]


def project_kernel(here, own, other, w_own, w_far, bias, query, *rest):
    pairs, w_full = rest[:PAIRS], rest[PAIRS]
    size = w_own.shape[1] // 3
    block_len = own.shape[0]
    assemble(here, (w_own, w_far), "row", w_full, 3, size, 0)
    for slot, source in enumerate((own, other)):
        left, right = half_pair(source[...])
        rows = pl.ds(slot * block_len, block_len)

        def product(part):
            return mm(left, w_full[part, 0], NT) + mm(right, w_full[part, 1], NT)

        query[rows, :] = (product(0) + bias[0:1, :]).astype(LOW)
        key_low = product(1).astype(LOW)
        value_low = (product(2) + bias[1:2, :]).astype(LOW)
        for index, pair in enumerate(pairs):
            lanes = slice(index * LANE, (index + 1) * LANE)
            pair[rows, :] = two(key_low[:, lanes], value_low[:, lanes])


def tile_lanes(mask, times):
    return jnp.concatenate([mask] * times, axis=1)


def split_low(values):
    high = values.astype(LOW)
    return high, (values - high.astype(WIDE)).astype(LOW)


def fill_wide(wide, slot, low_rim, source, high_rim):
    block_len = source.shape[0]
    wide[slot, 0:RIM, :] = low_rim[slot].astype(WIDE)
    wide[slot, RIM : RIM + block_len, :] = source[...].astype(WIDE)
    wide[slot, RIM + block_len : RIM + block_len + RIM, :] = high_rim[slot].astype(WIDE)


def same_doc(docs, slot, offset, block_len):
    start = RIM - KERNEL // 2 + offset
    return docs[slot, start : start + block_len, :] == docs[slot, RIM : RIM + block_len, :]


def spread_heads():
    head = lax.broadcasted_iota(jnp.int32, (2 * LANE, ATT), 0) % LANE
    lane = lax.broadcasted_iota(jnp.int32, (2 * LANE, ATT), 1)
    return jnp.where(lane // HEAD == head, 1.0, 0.0).astype(LOW)


def branch_kernel(
    here,
    own,
    other,
    low_rim,
    high_rim,
    docs,
    w_own,
    w_far,
    depth_gain,
    bias,
    tap_weight,
    tap_bias,
    query,
    context,
    depth_low,
    value_wide,
    key_conv,
    conv_attn,
    conv_weights,
    w_full,
    wide,
):
    size = w_own.shape[1] // 2
    block_len = own.shape[0]
    start = RIM - KERNEL // 2
    assemble(here, (w_own, w_far), "col", w_full, 2, size, 0)
    spread = spread_heads()
    for slot, source in enumerate((own, other)):
        rows = slice(slot * block_len, (slot + 1) * block_len)
        fill_wide(wide, slot, low_rim, source, high_rim)
        for block in range(wide.shape[2] // LANE):
            lanes = slice(block * LANE, (block + 1) * LANE)
            total = jnp.zeros((block_len, LANE), WIDE)
            for offset in range(KERNEL):
                piece = wide[slot, start + offset : start + offset + block_len, lanes]
                piece = jnp.where(same_doc(docs, slot, offset, block_len), piece, 0.0)
                total = total + piece * depth_gain[offset : offset + 1, lanes]
            depth_low[rows, lanes] = total.astype(LOW)
        left, right = half_pair(wide[slot].astype(LOW))
        value = (mm(left, w_full[0, 0], NT) + mm(right, w_full[0, 1], NT) + bias[2:3, :]).astype(LOW)
        value_wide[slot] = value.astype(WIDE)
        left, right = half_pair(depth_low[rows, :])
        key_here = mm(left, w_full[1, 0], NT) + mm(right, w_full[1, 1], NT) + bias[3:4, :]
        key_conv[rows, :] = key_here
        attn = (query[rows, :].astype(WIDE) * key_here).astype(LOW)
        conv_attn[rows, :] = attn
        conv_weights[rows, :] = mm(attn, tap_weight[...], NN) + tap_bias[...]
        top = jnp.full((block_len, LANE), MASKED, WIDE)
        for offset in range(KERNEL):
            lanes = slice(offset * LANE, (offset + 1) * LANE)
            top = jnp.maximum(
                top,
                jnp.where(
                    same_doc(docs, slot, offset, block_len), conv_weights[rows, lanes], MASKED
                ),
            )
        total = jnp.zeros((block_len, LANE), WIDE)
        for offset in range(KERNEL):
            lanes = slice(offset * LANE, (offset + 1) * LANE)
            mask = same_doc(docs, slot, offset, block_len)
            term = jnp.where(
                mask, jnp.exp(jnp.where(mask, conv_weights[rows, lanes], MASKED) - top), 0.0
            )
            conv_weights[rows, lanes] = term
            total = total + term
        scale = 1.0 / total
        mixed = jnp.zeros((block_len, ATT), WIDE)
        for offset in range(KERNEL):
            lanes = slice(offset * LANE, (offset + 1) * LANE)
            weight = conv_weights[rows, lanes] * scale
            conv_weights[rows, lanes] = weight
            wide_weight = mm(two(*split_low(weight)), spread, NN)
            mixed = mixed + wide_weight * value_wide[slot, start + offset : start + offset + block_len, :]
        context[rows, :] = mixed.astype(LOW)


def head_queries(values, head):
    lane = lax.broadcasted_iota(jnp.int32, values.shape, 1)
    return jnp.where(lane // HEAD == head, values, jnp.zeros_like(values))


def blocks_overlap(bounds, slot, block):
    return (bounds[block, 0] <= bounds[slot, 1]) & (bounds[block, 1] >= bounds[slot, 0])


def attend_kernel(bounds, query, kv_own, kv_far, doc_query, doc_key, out, stats, scores, top, total, mixed):
    entries, tokens_here, _ = kv_own.shape
    block_len = tokens_here // 2
    score_scale = HEAD ** (-0.5)
    for slot in range(2):
        rows = slice(slot * block_len, (slot + 1) * block_len)
        scaled = query[rows, :] * jnp.asarray(score_scale, LOW)
        queries = [head_queries(scaled, head) for head in range(2)]
        doc_here = doc_query[slot : slot + 1, :]
        top[...] = jnp.full(top.shape, MASKED, WIDE)
        total[...] = jnp.zeros(total.shape, WIDE)
        mixed[...] = jnp.zeros(mixed.shape, WIDE)

        def each(body):
            for core, stack in enumerate((kv_own, kv_far)):

                def one(step, carry):
                    block = core * entries * 2 + step

                    @pl.when(blocks_overlap(bounds, slot, block))
                    def _():
                        keys = pl.ds(pl.multiple_of((step % 2) * block_len, 16), block_len)
                        body(stack, step // 2, keys, block)

                    return carry

                lax.fori_loop(0, entries * 2, one, 0)

        def first(stack, entry, keys, block):
            key_rows = stack[entry, keys, :LANE]
            doc_rows = doc_key[block]
            allowed = tile_lanes(doc_rows, block_len // LANE) == doc_here
            for head in range(2):
                score = jnp.where(allowed, mm(key_rows, queries[head], NT), MASKED)
                scores[block, head] = score
                top[head] = jnp.maximum(top[head], jnp.max(score, axis=0, keepdims=True))

        each(first)

        def second(stack, entry, keys, block):
            value_rows = stack[entry, keys, LANE:]
            for head in range(2):
                term = jnp.exp(scores[block, head] - top[head, 0:1, :])
                total[head] = total[head] + jnp.sum(term, axis=0, keepdims=True)
                mixed[head] = mixed[head] + mm(value_rows, term.astype(LOW), TN)

        each(second)
        parts = []
        for head in range(2):
            scale = 1.0 / total[head, 0:1, :]
            parts.append(mixed[head, head * HEAD : (head + 1) * HEAD, :] * scale)
            stats[slot, head : head + 1, :] = top[head, 0:1, :] + jnp.log(total[head, 0:1, :])
        out[rows, :] = jnp.concatenate(parts, axis=0).T.astype(LOW)


def attend_back_kernel(
    bounds,
    query,
    kv_own,
    kv_far,
    doc_query,
    doc_key,
    attended,
    grad,
    stats,
    grad_query,
    grad_own,
    grad_far,
    delta,
    grad_kv,
):
    entries, tokens_here, _ = kv_own.shape
    block_len = tokens_here // 2
    score_scale = HEAD ** (-0.5)
    head_row = lax.broadcasted_iota(jnp.int32, (8, LANE), 0)
    head_lane = lax.broadcasted_iota(jnp.int32, (8, LANE), 1) // HEAD
    chosen = jnp.where(head_row == head_lane, 1.0, 0.0).astype(LOW)
    for slot in range(2):
        rows = slice(slot * block_len, (slot + 1) * block_len)
        both = attended[rows, :].astype(WIDE) * grad[rows, :].astype(WIDE)
        high, low = split_low(both)
        delta[slot] = mm(chosen, high, NT) + mm(chosen, low, NT)
    grad_query[...] = jnp.zeros(grad_query.shape, WIDE)

    for core, (stack, out) in enumerate(((kv_own, grad_own), (kv_far, grad_far))):

        def one(step, carry):
            block = core * entries * 2 + step
            keys = pl.ds(pl.multiple_of((step % 2) * block_len, 16), block_len)
            entry = step // 2
            grad_kv[...] = jnp.zeros(grad_kv.shape, WIDE)
            for slot in range(2):

                @pl.when(blocks_overlap(bounds, slot, block))
                def _():
                    rows = slice(slot * block_len, (slot + 1) * block_len)
                    key_rows = stack[entry, keys, :LANE]
                    value_rows = stack[entry, keys, LANE:]
                    scaled = query[rows, :] * jnp.asarray(score_scale, LOW)
                    allowed = tile_lanes(doc_key[block], block_len // LANE) == doc_query[slot : slot + 1, :]
                    for head in range(2):
                        query_here = head_queries(scaled, head)
                        grad_here = head_queries(grad[rows, :], head)
                        score = mm(key_rows, query_here, NT)
                        probs = jnp.where(
                            allowed, jnp.exp(score - stats[slot, head : head + 1, :]), 0.0
                        )
                        g_probs = mm(value_rows, grad_here, NT)
                        g_score = (probs * (g_probs - delta[slot, head : head + 1, :])).astype(LOW)
                        key_here = head_queries(key_rows, head)
                        grad_query[rows, :] += mm(g_score, key_here, TN)
                        grad_kv[:, :LANE] += mm(g_score, query_here, NN)
                        grad_kv[:, LANE:] += mm(probs.astype(LOW), grad_here, NN)

            out[entry, keys, :] = grad_kv[...].astype(LOW)
            return carry

        lax.fori_loop(0, entries * 2, one, 0)
    grad_query[...] = grad_query[...] * score_scale


def norm_stats(values):
    mean = jnp.mean(values, axis=-1, keepdims=True)
    centred = values - mean
    spread = jnp.mean(centred * centred, axis=-1, keepdims=True)
    scale = lax.rsqrt(spread + EPSILON)
    return centred * scale, scale


def norm_back(normal, scale, grad):
    return scale * (
        grad
        - jnp.mean(grad, axis=-1, keepdims=True)
        - normal * jnp.mean(grad * normal, axis=-1, keepdims=True)
    )


def column_sum(values):
    return jnp.sum(values, axis=0, keepdims=True)


def middle_kernel(
    here,
    own,
    other,
    cot_own,
    cot_other,
    att_0,
    att_1,
    att_2,
    conv_context,
    inner_own,
    inner_far,
    tail_own,
    tail_far,
    vectors,
    inner_bias,
    out_own,
    out_other,
    resid_grad,
    g_att_0,
    g_att_1,
    g_att_2,
    g_conv,
    d_inner_own,
    d_inner_far,
    d_tail_own,
    d_tail_far,
    vector_grads,
    inner_bias_grad,
    w_out,
    context,
    normal_1,
    scale_1,
    hidden_low,
    active,
    slope,
    ffn_sum,
    grad_2,
    ffn_grad,
    attn_grad,
    d_out,
):
    block_len = own.shape[0]
    tokens_here = 2 * block_len
    inner_size = inner_own.shape[1]
    out_size = tail_own.shape[1] - inner_size
    half_width = inner_own.shape[2]
    cols = inner_own.shape[0]
    assemble(here, (tail_own, tail_far), "col", w_out, 1, out_size, inner_size)
    bias_out, gain_1, shift_1 = vectors[0:1, :], vectors[1:2, :], vectors[2:3, :]
    bias_outer, gain_2, shift_2 = vectors[3:4, :], vectors[4:5, :], vectors[5:6, :]
    context[0] = jnp.concatenate([att_0[...], att_1[...], att_2[...]], axis=1)
    context[1] = conv_context[...]
    sources = ((own, cot_own, out_own), (other, cot_other, out_other))
    for slot, (source, _, _) in enumerate(sources):
        rows = slice(slot * block_len, (slot + 1) * block_len)
        attn = (
            mm(context[0, rows, :], w_out[0, 0], NT)
            + mm(context[1, rows, :], w_out[0, 1], NT)
            + bias_out
        )
        normal, scale = norm_stats(source[...].astype(WIDE) + attn)
        normal_1[rows, :] = normal
        scale_1[rows, :] = jnp.broadcast_to(scale, (block_len, LANE))
        hidden = normal * gain_1 + shift_1
        left, right = half_pair(hidden.astype(LOW))
        hidden_low[0, rows, :] = left
        hidden_low[1, rows, :] = right
    ffn_sum[...] = jnp.zeros(ffn_sum.shape, WIDE)

    def each(body):
        for core, (inner, tail) in enumerate(((inner_own, tail_own), (inner_far, tail_far))):

            def one(entry, carry):
                dr, dc = place_of(entry, "row")
                entry_tail = (entry % 2) * 2 + (entry // 2) % 2 + (entry // 4) * 4
                group = here[0] ^ dr
                spot = group * (2 * cols // 2) + (here[1] ^ (dc + core))
                body(core, entry, entry_tail, group, spot, inner, tail)
                return carry

            lax.fori_loop(0, cols, one, 0)

    def forward(core, entry, entry_tail, group, spot, inner, tail):
        for slot in range(2):
            rows = slice(slot * block_len, (slot + 1) * block_len)
            pre = mm(hidden_low[group, rows, :], inner[entry], NT) + inner_bias[spot]
            half = 0.5 * (1.0 + lax.erf(pre * (0.5**0.5)))
            low = (pre * half).astype(LOW)
            active[core * cols + entry, rows, :] = low
            slope[core * cols + entry, rows, :] = half + pre * jnp.exp(-0.5 * pre * pre) * (
                0.3989422804014327
            )
            ffn_sum[group, rows, :] += mm(low, tail[entry_tail, :inner_size, :], NN)

    each(forward)
    vector_grads[...] = jnp.zeros(vector_grads.shape, WIDE)
    for slot, (_, cot, out) in enumerate(sources):
        rows = slice(slot * block_len, (slot + 1) * block_len)
        hidden = normal_1[rows, :] * gain_1 + shift_1
        resid = hidden + (two(ffn_sum[0, rows, :], ffn_sum[1, rows, :]) + bias_outer)
        normal, scale = norm_stats(resid)
        out[...] = (normal * gain_2 + shift_2).astype(LOW)
        cot_wide = cot[...].astype(WIDE)
        vector_grads[0:1, :] += column_sum(cot_wide * normal)
        vector_grads[1:2, :] += column_sum(cot_wide)
        grad = norm_back(normal, scale, cot_wide * gain_2)
        grad_2[rows, :] = grad
        low = grad.astype(LOW)
        vector_grads[2:3, :] += column_sum(low.astype(WIDE))
        left, right = half_pair(low)
        ffn_grad[0, rows, :] = left
        ffn_grad[1, rows, :] = right
    ffn_sum[...] = jnp.zeros(ffn_sum.shape, WIDE)

    def backward(core, entry, entry_tail, group, spot, inner, tail):
        d_inner = (d_inner_own, d_inner_far)[core]
        d_tail = (d_tail_own, d_tail_far)[core]
        where = core * cols + entry
        lows = []
        for slot in range(2):
            rows = slice(slot * block_len, (slot + 1) * block_len)
            g_active = mm(ffn_grad[group, rows, :], tail[entry_tail, :inner_size, :], NT)
            low = (g_active * slope[where, rows, :]).astype(LOW)
            lows.append(low)
            ffn_sum[group, rows, :] += mm(low, inner[entry], NN)
        g_inner = jnp.concatenate(lows, axis=0)
        inner_bias_grad[spot] = column_sum(g_inner.astype(WIDE))
        d_inner[entry] = mm(g_inner, hidden_low[group], TN).astype(LOW)
        d_tail[entry_tail, :inner_size, :] = mm(active[where], ffn_grad[group], TN).astype(LOW)

    each(backward)
    for slot in range(2):
        rows = slice(slot * block_len, (slot + 1) * block_len)
        grad = grad_2[rows, :] + two(ffn_sum[0, rows, :], ffn_sum[1, rows, :])
        normal = normal_1[rows, :]
        vector_grads[3:4, :] += column_sum(grad * normal)
        vector_grads[4:5, :] += column_sum(grad)
        grad = norm_back(normal, scale_1[rows, 0:1], grad * gain_1)
        resid_grad[rows, :] = grad
        low = grad.astype(LOW)
        vector_grads[5:6, :] += column_sum(low.astype(WIDE))
        attn_grad[rows, :] = low
        g_att = mm(low, w_out[0, 0], NN).astype(LOW)
        for index, out in enumerate((g_att_0, g_att_1, g_att_2)):
            out[rows, :] = g_att[:, index * LANE : (index + 1) * LANE]
        g_conv[rows, :] = mm(low, w_out[0, 1], NN).astype(LOW)
    for half in range(2):
        d_out[0, half] = mm(attn_grad[...], context[half], TN).astype(LOW)
    cut(here, d_out, (d_tail_own, d_tail_far), "col", 1, out_size, inner_size)


def branch_back_kernel(
    own,
    other,
    low_rim,
    high_rim,
    docs,
    w_full,
    depth_gain,
    tap_weight,
    query,
    g_conv,
    value_wide,
    key_conv,
    conv_attn,
    conv_weights,
    g_key_conv,
    g_query,
    d_tap_weight,
    d_tap_bias,
    d_depth,
    g_ext_value,
    g_ext_tokens,
    wide,
    weight_grad,
    low_grad,
):
    block_len = own.shape[0]
    start = RIM - KERNEL // 2
    spread = spread_heads()
    d_tap_weight[...] = jnp.zeros(d_tap_weight.shape, WIDE)
    d_tap_bias[...] = jnp.zeros(d_tap_bias.shape, WIDE)
    d_depth[...] = jnp.zeros(d_depth.shape, WIDE)
    g_ext_value[...] = jnp.zeros(g_ext_value.shape, WIDE)
    g_ext_tokens[...] = jnp.zeros(g_ext_tokens.shape, WIDE)
    for slot, source in enumerate((own, other)):
        rows = slice(slot * block_len, (slot + 1) * block_len)
        fill_wide(wide, slot, low_rim, source, high_rim)
        grad = g_conv[rows, :].astype(WIDE)
        mean = jnp.zeros((block_len, LANE), WIDE)
        for offset in range(KERNEL):
            lanes = slice(offset * LANE, (offset + 1) * LANE)
            place = slice(start + offset, start + offset + block_len)
            high, low = split_low(grad * value_wide[slot, place, :])
            back = mm(high, spread[:LANE], NT) + mm(low, spread[:LANE], NT)
            weight_grad[:, lanes] = back
            mean = mean + conv_weights[rows, lanes] * back
        for offset in range(KERNEL):
            lanes = slice(offset * LANE, (offset + 1) * LANE)
            place = slice(start + offset, start + offset + block_len)
            weight = conv_weights[rows, lanes]
            low_grad[:, lanes] = (weight * (weight_grad[:, lanes] - mean)).astype(LOW)
            g_ext_value[slot, place, :] += mm(two(*split_low(weight)), spread, NN) * grad
        d_tap_weight[...] += mm(conv_attn[rows, :], low_grad[...], TN)
        d_tap_bias[...] += column_sum(low_grad[...].astype(WIDE))
        g_attn = mm(low_grad[...], tap_weight[...], NT)
        g_key = (g_attn * query[rows, :].astype(WIDE)).astype(LOW)
        g_key_conv[rows, :] = g_key
        g_query[rows, :] = g_attn * key_conv[rows, :]
        for half in range(2):
            g_depth = mm(g_key, w_full[1, half], NN)
            for block in range(g_depth.shape[1] // LANE):
                column = half * g_depth.shape[1] + block * LANE
                lanes = slice(column, column + LANE)
                piece = g_depth[:, block * LANE : (block + 1) * LANE]
                for offset in range(KERNEL):
                    place = slice(start + offset, start + offset + block_len)
                    masked = jnp.where(same_doc(docs, slot, offset, block_len), piece, 0.0)
                    d_depth[offset : offset + 1, lanes] += column_sum(masked * wide[slot, place, lanes])
                    g_ext_tokens[slot, place, lanes] += masked * depth_gain[offset : offset + 1, lanes]


def branch_weights_kernel(
    here,
    own,
    other,
    w_full,
    depth_low,
    g_key_conv,
    g_ext_value,
    g_ext_tokens,
    after,
    before,
    resid_grad,
    d_own,
    d_far,
    token_grad,
    bias_grad,
    ext,
    d_full,
    tokens,
    value_grad,
):
    block_len = own.shape[0]
    size = d_own.shape[1] // 2
    for slot, source in enumerate((own, other)):
        rows = slice(slot * block_len, (slot + 1) * block_len)
        tokens[rows, :] = source[...]
        for grads, lanes in ((g_ext_value, slice(0, ATT)), (g_ext_tokens, slice(ATT, ext.shape[1]))):
            ext[:, lanes] = grads[slot, RIM : RIM + block_len, :]
        ext[0:RIM, :] += before[slot].astype(WIDE)
        ext[block_len - RIM :, :] += after[slot].astype(WIDE)
        low = ext[:, :ATT].astype(LOW)
        value_grad[rows, :] = low
        token_grad[rows, :] = (
            resid_grad[rows, :]
            + ext[:, ATT:]
            + two(mm(low, w_full[0, 0], NN), mm(low, w_full[0, 1], NN))
        )
    bias_grad[0:1, :] = column_sum(value_grad[...].astype(WIDE))
    bias_grad[1:2, :] = column_sum(g_key_conv[...].astype(WIDE))
    for half in range(2):
        lanes = slice(half * d_own.shape[2], (half + 1) * d_own.shape[2])
        d_full[0, half] = mm(value_grad[...], tokens[:, lanes], TN).astype(LOW)
        d_full[1, half] = mm(g_key_conv[...], depth_low[:, lanes], TN).astype(LOW)
    cut(here, d_full, (d_own, d_far), "col", 2, size, 0)


def query_weights_kernel(
    here, own, other, w_full, grad_0, grad_1, grad_2, g_query, token_in, d_own, d_far, token_grad, bias_grad, d_full, tokens
):
    block_len = own.shape[0]
    size = d_own.shape[1]
    low = (jnp.concatenate([grad_0[...], grad_1[...], grad_2[...]], axis=1) + g_query[...]).astype(LOW)
    bias_grad[...] = column_sum(low.astype(WIDE))
    for slot, source in enumerate((own, other)):
        tokens[slot * block_len : (slot + 1) * block_len, :] = source[...]
    token_grad[...] = token_in[...] + two(mm(low, w_full[0, 0], NN), mm(low, w_full[0, 1], NN))
    for half in range(2):
        lanes = slice(half * d_own.shape[2], (half + 1) * d_own.shape[2])
        d_full[0, half] = mm(low, tokens[:, lanes], TN).astype(LOW)
    cut(here, d_full, (d_own, d_far), "col", 1, size, 0)


def pair_weights_kernel(
    here, own, other, w_full, pair_0, pair_1, pair_2, token_in, d_own, d_far, token_own, token_other, bias_grad, d_full, tokens
):
    block_len = own.shape[0]
    size = d_own.shape[1] // 2
    pairs = (pair_0, pair_1, pair_2)
    for slot, source in enumerate((own, other)):
        tokens[slot * block_len : (slot + 1) * block_len, :] = source[...]
    lows = [
        jnp.concatenate([pair[:, part * LANE : (part + 1) * LANE] for pair in pairs], axis=1)
        for part in range(2)
    ]
    bias_grad[...] = column_sum(lows[1].astype(WIDE))
    for part in range(2):
        for half in range(2):
            lanes = slice(half * d_own.shape[2], (half + 1) * d_own.shape[2])
            d_full[part, half] = mm(lows[part], tokens[:, lanes], TN).astype(LOW)
    cut(here, d_full, (d_own, d_far), "row", 2, size, 0)
    for slot, out in enumerate((token_own, token_other)):
        rows = slice(slot * block_len, (slot + 1) * block_len)
        total = token_in[rows, :]
        for part in range(2):
            total = total + two(
                mm(lows[part][rows], w_full[part + 1, 0], NN), mm(lows[part][rows], w_full[part + 1, 1], NN)
            )
        out[...] = total.astype(out.dtype)


def local(
    tokens,
    cotangent,
    doc_ids,
    proj_weight,
    out_weight,
    inner_weight,
    outer_weight,
    depth_weight,
    proj_bias,
    kernel_weight,
    kernel_bias,
    out_bias,
    norm1_gain,
    norm1_shift,
    inner_bias,
    outer_bias,
    norm2_gain,
    norm2_shift,
):
    block_len = tokens.shape[1]
    model_width = tokens.shape[2]
    margin = KERNEL // 2
    col_count = lax.axis_size("col")
    row_count = lax.axis_size("row")
    row_here = lax.axis_index("row")
    col_here = lax.axis_index("col")
    here = jnp.stack([row_here, col_here]).astype(jnp.int32)
    tokens_here = 2 * block_len
    entries = col_count // 2 * row_count
    pair_entries = col_count // 2
    cut_proj = proj_weight.shape[2]
    cut_out = out_weight.shape[1]
    cut_inner = inner_weight.shape[2]
    lanes = proj_weight.shape[1]

    proj_t = jnp.transpose(proj_weight, (0, 2, 1))
    first_own, first_far = gather(proj_t[:3].reshape(-1, lanes), "row")

    def trade(pair):
        return pick(pair, row_here), swap(pick(pair, 1 - row_here), "row", 1)

    own, other = trade(tokens)
    branch_own, branch_far = gather(proj_t[3:].reshape(-1, lanes), "col")

    def wrapped(block, step):
        moved = shift(block, "col", step)
        edge = 0 if step > 0 else col_count - 1
        return jnp.where(col_here == edge, moved[::-1], moved)

    low_rim = wrapped(jnp.stack([own[block_len - RIM :], other[block_len - RIM :]]), 1)
    high_rim = wrapped(jnp.stack([own[:RIM], other[:RIM]]), -1)

    docs = jnp.stack(trade(doc_ids[:, 0]))[None]
    far_steps = [step for step in steps_of("col") if step > 1]
    for step in far_steps + [1]:
        docs = jnp.concatenate([docs, swap(docs, "col", step)], axis=0)
    relative = [0]
    for step in far_steps + [1]:
        relative = relative + [entry ^ step for entry in relative]
    doc_blocks = docs.reshape(-1, block_len)
    bounds = jnp.stack([doc_blocks[:, 0], doc_blocks[:, -1]], axis=1)
    doc_key = jnp.broadcast_to(doc_blocks[:, :, None], doc_blocks.shape + (LANE,))
    ordered = jnp.stack([docs[relative.index(dc)] for dc in range(col_count)])

    def doc_rim(slot, step):
        position = (row_here ^ slot) * col_count + col_here + step
        inside = (position >= 0) & (position < row_count * col_count)
        position = jnp.clip(position, 0, row_count * col_count - 1)
        dr = (position // col_count) ^ row_here
        dc = (position % col_count) ^ col_here
        return jnp.where(inside, pick(pick(ordered, dc), dr), -1)

    doc_ext = jnp.stack(
        [
            jnp.concatenate(
                [doc_rim(slot, -1)[block_len - RIM :], docs[0, slot], doc_rim(slot, 1)[:RIM]]
            )
            for slot in range(2)
        ]
    )
    doc_rows = jnp.broadcast_to(doc_ext[:, :, None], doc_ext.shape + (LANE,))

    inner_own, inner_far = gather(inner_weight[0].T, "row")
    tail_own, tail_far = gather(jnp.concatenate([outer_weight[0], out_weight.T], axis=0), "col")
    cot_own, cot_other = trade(cotangent)

    wide_bias = proj_bias.astype(WIDE)
    tap_weight = jnp.pad(
        kernel_weight.reshape(ATT, HEADS, KERNEL).transpose(0, 2, 1),
        ((0, 0), (0, 0), (0, LANE - HEADS)),
    ).reshape(ATT, KERNEL * LANE)
    tap_bias = (
        jnp.pad(kernel_bias.reshape(HEADS, KERNEL).T, ((0, 0), (0, LANE - HEADS)))
        .reshape(1, KERNEL * LANE)
        .astype(WIDE)
    )
    depth_gain = jnp.pad(depth_weight.astype(WIDE), ((0, 16 - KERNEL), (0, 0)))
    vectors = jnp.stack(
        [out_bias, norm1_gain, norm1_shift, outer_bias, norm2_gain, norm2_shift, norm2_shift, norm2_shift]
    ).astype(WIDE)

    query, *pairs = kernel_call(
        project_kernel,
        [((tokens_here, ATT), LOW)]
        + [((tokens_here, 2 * LANE), LOW)] * PAIRS
        + [((3, row_count, ATT, lanes), LOW)],
    )(here, own, other, first_own, first_far, wide_bias)
    w_first = pairs.pop()

    def gather_pair(pair):
        stack = pair[None]
        for step in far_steps:
            stack = jnp.concatenate([stack, swap(stack, "col", step)], axis=0)
        return stack, swap(stack, "col", 1)

    gathered = [gather_pair(pair) for pair in pairs]

    ext_len = block_len + 2 * RIM
    conv_context, depth_low, value_wide, key_conv, conv_attn, conv_weights, w_branch = kernel_call(
        branch_kernel,
        [
            ((tokens_here, ATT), LOW),
            ((tokens_here, model_width), LOW),
            ((2, ext_len, ATT), WIDE),
            ((tokens_here, ATT), WIDE),
            ((tokens_here, ATT), LOW),
            ((tokens_here, KERNEL * LANE), WIDE),
            ((2, row_count, ATT, lanes), LOW),
        ],
        [((2, ext_len, model_width), WIDE)],
    )(
        here,
        own,
        other,
        low_rim,
        high_rim,
        doc_rows,
        branch_own,
        branch_far,
        depth_gain,
        wide_bias,
        tap_weight,
        tap_bias,
        query,
    )

    doc_query = doc_blocks[:2]
    attended = []
    stats = []
    for index in range(PAIRS):
        out, stat = kernel_call(
            attend_kernel,
            [((tokens_here, LANE), LOW), ((2, 8, block_len), WIDE)],
            [
                ((2 * col_count, 2, block_len, block_len), WIDE),
                ((2, 1, block_len), WIDE),
                ((2, 1, block_len), WIDE),
                ((2, LANE, block_len), WIDE),
            ],
        )(bounds, query[:, index * LANE : (index + 1) * LANE], *gathered[index], doc_query, doc_key)
        attended.append(out)
        stats.append(stat)

    (
        out_own,
        out_other,
        resid_grad,
        *g_att,
        g_conv,
        d_inner_own,
        d_inner_far,
        d_tail_own,
        d_tail_far,
        vector_grads,
        inner_bias_grad,
    ) = kernel_call(
        middle_kernel,
        [
            ((block_len, model_width), LOW),
            ((block_len, model_width), LOW),
            ((tokens_here, model_width), WIDE),
        ]
        + [((tokens_here, LANE), LOW)] * PAIRS
        + [((tokens_here, ATT), LOW)]
        + [((entries, cut_inner, lanes), LOW)] * 2
        + [((entries, cut_inner + cut_out, lanes), LOW)] * 2
        + [((8, model_width), WIDE), ((2 * entries, 1, cut_inner), WIDE)],
        [
            ((1, row_count, model_width, lanes), LOW),
            ((row_count, tokens_here, lanes), LOW),
            ((tokens_here, model_width), WIDE),
            ((tokens_here, LANE), WIDE),
            ((row_count, tokens_here, lanes), LOW),
            ((2 * entries, tokens_here, cut_inner), LOW),
            ((2 * entries, tokens_here, cut_inner), WIDE),
            ((row_count, tokens_here, lanes), WIDE),
            ((tokens_here, model_width), WIDE),
            ((row_count, tokens_here, lanes), LOW),
            ((tokens_here, model_width), LOW),
            ((1, row_count, model_width, lanes), LOW),
        ],
    )(
        here,
        own,
        other,
        cot_own,
        cot_other,
        *attended,
        conv_context,
        inner_own,
        inner_far,
        tail_own,
        tail_far,
        vectors,
        inner_bias.astype(WIDE).reshape(2 * entries, 1, cut_inner),
    )

    inner_sum = data_sum(scatter(d_inner_own, d_inner_far, "row")).astype(WIDE)
    tail_sum = data_sum(scatter(d_tail_own, d_tail_far, "col")).astype(WIDE)

    (
        g_key_conv,
        g_query,
        d_tap_weight,
        d_tap_bias,
        d_depth,
        g_ext_value,
        g_ext_tokens,
    ) = kernel_call(
        branch_back_kernel,
        [
            ((tokens_here, ATT), LOW),
            ((tokens_here, ATT), WIDE),
            ((ATT, KERNEL * LANE), WIDE),
            ((1, KERNEL * LANE), WIDE),
            ((16, model_width), WIDE),
            ((2, ext_len, ATT), WIDE),
            ((2, ext_len, model_width), WIDE),
        ],
        [
            ((2, ext_len, model_width), WIDE),
            ((block_len, KERNEL * LANE), WIDE),
            ((block_len, KERNEL * LANE), LOW),
        ],
        smem=0,
    )(
        own,
        other,
        low_rim,
        high_rim,
        doc_rows,
        w_branch,
        depth_gain,
        tap_weight,
        query,
        g_conv,
        value_wide,
        key_conv,
        conv_attn,
        conv_weights,
    )

    def rim_of(start):
        return jnp.concatenate(
            [g_ext_value[:, start : start + RIM], g_ext_tokens[:, start : start + RIM]], axis=2
        ).astype(LOW)

    after = wrapped(rim_of(0), -1)
    before = wrapped(rim_of(RIM + block_len), 1)

    query_grads = []
    pair_grads = []
    for index in range(PAIRS):
        grad_query, grad_own, grad_far = kernel_call(
            attend_back_kernel,
            [
                ((tokens_here, LANE), WIDE),
                ((pair_entries, tokens_here, 2 * LANE), LOW),
                ((pair_entries, tokens_here, 2 * LANE), LOW),
            ],
            [((2, 8, block_len), WIDE), ((block_len, 2 * LANE), WIDE)],
        )(
            bounds,
            query[:, index * LANE : (index + 1) * LANE],
            *gathered[index],
            doc_query,
            doc_key,
            attended[index],
            g_att[index],
            stats[index],
        )
        query_grads.append(grad_query)
        stack = add_low(grad_own, swap(grad_far, "col", 1))
        for step in reversed(far_steps):
            half = stack.shape[0] // 2
            stack = add_low(stack[:half], swap(stack[half:], "col", step))
        pair_grads.append(stack[0])

    d_branch_own, d_branch_far, token_grad, branch_bias = kernel_call(
        branch_weights_kernel,
        [((entries, 2 * cut_proj, lanes), LOW)] * 2
        + [((tokens_here, model_width), WIDE), ((8, ATT), WIDE)],
        [
            ((block_len, ATT + model_width), WIDE),
            ((2, row_count, ATT, lanes), LOW),
            ((tokens_here, model_width), LOW),
            ((tokens_here, ATT), LOW),
        ],
    )(
        here,
        own,
        other,
        w_branch,
        depth_low,
        g_key_conv,
        g_ext_value,
        g_ext_tokens,
        after,
        before,
        resid_grad,
    )
    branch_sum = data_sum(scatter(d_branch_own, d_branch_far, "col")).astype(WIDE)

    d_query_own, d_query_far, token_grad, query_bias = kernel_call(
        query_weights_kernel,
        [((entries, cut_proj, lanes), LOW)] * 2
        + [((tokens_here, model_width), WIDE), ((1, ATT), WIDE)],
        [((1, row_count, ATT, lanes), LOW), ((tokens_here, model_width), LOW)],
    )(here, own, other, w_first, *query_grads, g_query, token_grad)
    query_sum = data_sum(scatter(d_query_own, d_query_far, "col")).astype(WIDE)

    d_pair_own, d_pair_far, token_own, token_other, value_bias = kernel_call(
        pair_weights_kernel,
        [((entries, 2 * cut_proj, lanes), LOW)] * 2
        + [((block_len, model_width), WIDE), ((block_len, model_width), LOW), ((1, ATT), WIDE)],
        [((2, row_count, ATT, lanes), LOW), ((tokens_here, model_width), LOW)],
    )(here, own, other, w_first, *pair_grads, token_grad)
    pair_sum = data_sum(scatter(d_pair_own, d_pair_far, "row")).astype(WIDE)

    def tap_layout(grads):
        return grads.reshape(-1, KERNEL, LANE)[:, :, :HEADS].transpose(0, 2, 1).reshape(-1, HEADS * KERNEL)

    early = [vector_grads[:6], inner_bias_grad]
    late = [
        d_depth[:KERNEL],
        tap_layout(d_tap_weight),
        tap_layout(d_tap_bias),
        branch_bias[:2],
        query_bias,
        value_bias,
    ]

    def small_sum(items):
        flat = jnp.concatenate([item.reshape(-1) for item in items])
        flat = jnp.pad(flat, (0, -flat.shape[0] % 1024)).reshape(-1, LANE)
        flat = grid_sum(flat).reshape(-1)
        finals = []
        start = 0
        for item in items:
            finals.append(flat[start : start + item.size].reshape(item.shape))
            start += item.size
        return finals

    vector_sum, inner_bias_sum = small_sum(early)
    depth_sum, tap_weight_sum, tap_bias_sum, branch_bias_sum, query_bias_sum, value_bias_sum = small_sum(late)

    def give_back(here_rows, there_rows):
        moved = swap(there_rows, "row", 1).astype(here_rows.dtype)
        return jnp.where(
            row_here == 0, jnp.stack([here_rows, moved]), jnp.stack([moved, here_rows])
        )

    proj_sum = jnp.concatenate([query_sum, pair_sum, branch_sum], axis=0)
    return (
        give_back(out_own, out_other),
        give_back(token_own, token_other),
        jnp.transpose(proj_sum.reshape(5, cut_proj, lanes), (0, 2, 1)),
        tail_sum[cut_inner:].T,
        inner_sum.T[None],
        tail_sum[:cut_inner][None],
        depth_sum,
        jnp.concatenate([query_bias_sum, value_bias_sum, branch_bias_sum], axis=0),
        tap_weight_sum,
        tap_bias_sum[0],
        vector_sum[5],
        vector_sum[3],
        vector_sum[4],
        inner_bias_sum.reshape(-1),
        vector_sum[2],
        vector_sum[0],
        vector_sum[1],
    )


def solution(mesh):
    return jax.shard_map(
        local,
        mesh=mesh,
        in_specs=(
            P(None, ("dp", "row", "col"), None),
            P(None, ("dp", "row", "col"), None),
            P(None, "dp", ("row", "col")),
            P(None, "row", "col"),
            P("row", "col"),
            P("row", None, "col"),
            P("row", "col", None),
        )
        + (P(),) * 11,
        out_specs=(
            P(None, ("dp", "row", "col"), None),
            P(None, ("dp", "row", "col"), None),
            P(None, "row", "col"),
            P("row", "col"),
            P("row", None, "col"),
            P("row", "col", None),
        )
        + (P(),) * 11,
        check_vma=False,
    )
```

```python
import functools

import jax
import jax.numpy as jnp
from jax import lax
from jax.experimental import pallas as pl
from jax.experimental.pallas import tpu as pltpu
from jax.sharding import PartitionSpec as P

HEADS = 6
HEAD = 64
KERNEL = 9
FF = 3072
ATT = 384
PAIRS = HEADS // 2
LANE = 128
RIM = 8
DOC_ROWS = 16

EPSILON = 1e-12
MASKED = -1e30
LOW = jnp.bfloat16
WIDE = jnp.float32


def swap(block, axis, step):
    count = lax.axis_size(axis)
    return lax.ppermute(block, axis, [(i, i ^ step) for i in range(count)])


def shift(block, axis, step):
    count = lax.axis_size(axis)
    return lax.ppermute(block, axis, [(i, (i + step) % count) for i in range(count)])


def steps_of(axis):
    steps = []
    step = 1
    while step < lax.axis_size(axis):
        steps.append(step)
        step *= 2
    return steps


def pick(block, index):
    return lax.dynamic_index_in_dim(block, index, 0, keepdims=False)


NT = (((1,), (1,)), ((), ()))
NN = (((1,), (0,)), ((), ()))
TN = (((0,), (0,)), ((), ()))


def mm(left, right, how):
    return lax.dot_general(left, right, how, preferred_element_type=WIDE)


def kernel_call(body, outs, scratch=(), smem=1, cost=5):
    def run(*args):
        specs = [
            pl.BlockSpec(memory_space=pltpu.SMEM if place < smem else pltpu.VMEM)
            for place in range(len(args))
        ]
        return pl.pallas_call(
            body,
            in_specs=specs,
            out_specs=[pl.BlockSpec(memory_space=pltpu.VMEM)] * len(outs),
            out_shape=[jax.ShapeDtypeStruct(shape, kind) for shape, kind in outs],
            scratch_shapes=[pltpu.VMEM(shape, kind) for shape, kind in scratch],
            cost_estimate=pl.CostEstimate(
                flops=int(cost * 1e9), bytes_accessed=int(cost * 3.6e6), transcendentals=0
            ),
        )(*args)

    return run


def place_of(entry, kind):
    if kind == "col":
        entry = (entry & 1) * 2 + (entry // 2) % 2 + (entry // 4) * 4
    return entry % 2, (entry // 2) * 2


def stages_of(kind):
    far = [("col", step) for step in steps_of("col") if step > 1]
    row = [("row", 1)]
    return row + far if kind == "row" else far[:1] + row + far[1:]


def after(value, *marks):
    return lax.optimization_barrier((value,) + marks)[0]


def grow(stack, axis, step):
    return jnp.concatenate([stack, swap(stack, axis, step)], axis=0)


def add_low(kept, moved):
    return (kept.astype(WIDE) + moved.astype(WIDE)).astype(LOW)


def join(kept, moved):
    half = kept.shape[0] // 2
    return add_low(kept[:half], moved[:half]), add_low(kept[half:], moved[half:])


class DataSum:
    def __init__(self, part):
        self.index = lax.axis_index("dp")
        steps = steps_of("dp")
        self.todo = [(True, step) for step in steps] + [(False, step) for step in reversed(steps)]
        self.part = part
        self.start()

    def start(self):
        down, step = self.todo[0]
        self.bit = (self.index // step) % 2
        if down:
            self.halves = self.part.reshape((2, self.part.shape[0] // 2) + self.part.shape[1:])
            self.moved = swap(pick(self.halves, 1 - self.bit), "dp", step)
        else:
            self.moved = swap(self.part, "dp", step)

    def finish(self, *marks):
        moved = after(self.moved, *marks) if marks else self.moved
        down, _ = self.todo.pop(0)
        if down:
            self.part = add_low(pick(self.halves, self.bit), moved)
        else:
            self.part = jnp.where(
                self.bit == 0,
                jnp.concatenate([self.part, moved], axis=0),
                jnp.concatenate([moved, self.part], axis=0),
            )
        if self.todo:
            self.start()
        return self.part

    def rest(self):
        while self.todo:
            self.finish()
        return self.part


def grid_sum(flat):
    for axis in ("col", "row", "dp"):
        for step in steps_of(axis):
            flat = flat + swap(flat, axis, step)
    return flat


def assemble_pieces(here, pieces, full, parts, size):
    for (dr, dc), piece in pieces:
        row = here[0] ^ dr
        col = here[1] ^ dc
        for part in range(parts):
            full[part, row, pl.ds(pl.multiple_of(col * size, 16), size), :] = piece[
                part * size : (part + 1) * size, :
            ]


def assemble(here, stacks, kind, full, parts, size, start):
    for core, stack in enumerate(stacks):

        def one(entry, carry):
            dr, dc = place_of(entry, kind)
            row = here[0] ^ dr
            col = here[1] ^ (dc + core)
            for part in range(parts):
                full[part, row, pl.ds(pl.multiple_of(col * size, 16), size), :] = stack[
                    entry, start + part * size : start + (part + 1) * size, :
                ]
            return carry

        lax.fori_loop(0, stack.shape[0], one, 0)


def cut(here, full, outs, kind, parts, size, start):
    for core, out in enumerate(outs):

        def one(entry, carry):
            dr, dc = place_of(entry, kind)
            row = here[0] ^ dr
            col = here[1] ^ (dc + core)
            for part in range(parts):
                out[entry, start + part * size : start + (part + 1) * size, :] = full[
                    part, row, pl.ds(pl.multiple_of(col * size, 16), size), :
                ]
            return carry

        lax.fori_loop(0, out.shape[0], one, 0)


def two(left, right):
    return jnp.concatenate([left, right], axis=1)


def half_pair(value):
    return value[:, : value.shape[1] // 2], value[:, value.shape[1] // 2 :]


def project_kernel(keys, here, own, other, bias, *rest):
    weights, rest = rest[: len(keys)], rest[len(keys) :]
    query, pairs, w_full = rest[0], rest[1 : 1 + PAIRS], rest[1 + PAIRS]
    size = (weights[0].shape[0] - DOC_ROWS) // 3
    block_len = own.shape[0]
    assemble_pieces(here, list(zip(keys, weights)), w_full, 3, size)
    for slot, source in enumerate((own, other)):
        left, right = half_pair(source[...])
        rows = pl.ds(slot * block_len, block_len)

        def product(part):
            return mm(left, w_full[part, 0], NT) + mm(right, w_full[part, 1], NT)

        query[rows, :] = (product(0) + bias[0:1, :]).astype(LOW)
        key_low = product(1).astype(LOW)
        value_low = (product(2) + bias[1:2, :]).astype(LOW)
        for index, pair in enumerate(pairs):
            lanes = slice(index * LANE, (index + 1) * LANE)
            pair[rows, :] = two(key_low[:, lanes], value_low[:, lanes])


def tile_lanes(mask, times):
    return jnp.concatenate([mask] * times, axis=1)


def split_low(values):
    high = values.astype(LOW)
    return high, (values - high.astype(WIDE)).astype(LOW)


def fill_wide(wide, slot, low_rim, source, high_rim):
    block_len = source.shape[0]
    wide[slot, 0:RIM, :] = low_rim[slot].astype(WIDE)
    wide[slot, RIM : RIM + block_len, :] = source[...].astype(WIDE)
    wide[slot, RIM + block_len : RIM + block_len + RIM, :] = high_rim[slot].astype(WIDE)


def same_doc(docs, slot, offset, block_len):
    start = RIM - KERNEL // 2 + offset
    return docs[slot, start : start + block_len, :] == docs[slot, RIM : RIM + block_len, :]


def spread_heads():
    head = lax.broadcasted_iota(jnp.int32, (2 * LANE, ATT), 0) % LANE
    lane = lax.broadcasted_iota(jnp.int32, (2 * LANE, ATT), 1)
    return jnp.where(lane // HEAD == head, 1.0, 0.0).astype(LOW)


def branch_kernel(
    keys, here, own, other, low_rim, high_rim, docs, depth_gain, bias, tap_weight, tap_bias, query, *rest
):
    weights, rest = rest[: len(keys)], rest[len(keys) :]
    context, depth_low, value_wide, key_conv, conv_attn, conv_weights, w_full, wide = rest
    size = weights[0].shape[0] // 2
    block_len = own.shape[0]
    start = RIM - KERNEL // 2
    assemble_pieces(here, list(zip(keys, weights)), w_full, 2, size)
    spread = spread_heads()
    for slot, source in enumerate((own, other)):
        rows = slice(slot * block_len, (slot + 1) * block_len)
        fill_wide(wide, slot, low_rim, source, high_rim)
        for block in range(wide.shape[2] // LANE):
            lanes = slice(block * LANE, (block + 1) * LANE)
            total = jnp.zeros((block_len, LANE), WIDE)
            for offset in range(KERNEL):
                piece = wide[slot, start + offset : start + offset + block_len, lanes]
                piece = jnp.where(same_doc(docs, slot, offset, block_len), piece, 0.0)
                total = total + piece * depth_gain[offset : offset + 1, lanes]
            depth_low[rows, lanes] = total.astype(LOW)
        left, right = half_pair(wide[slot].astype(LOW))
        value = (mm(left, w_full[0, 0], NT) + mm(right, w_full[0, 1], NT) + bias[2:3, :]).astype(LOW)
        value_wide[slot] = value.astype(WIDE)
        left, right = half_pair(depth_low[rows, :])
        key_here = mm(left, w_full[1, 0], NT) + mm(right, w_full[1, 1], NT) + bias[3:4, :]
        key_conv[rows, :] = key_here
        attn = (query[rows, :].astype(WIDE) * key_here).astype(LOW)
        conv_attn[rows, :] = attn
        conv_weights[rows, :] = mm(attn, tap_weight[...], NN) + tap_bias[...]
        top = jnp.full((block_len, LANE), MASKED, WIDE)
        for offset in range(KERNEL):
            lanes = slice(offset * LANE, (offset + 1) * LANE)
            top = jnp.maximum(
                top,
                jnp.where(
                    same_doc(docs, slot, offset, block_len), conv_weights[rows, lanes], MASKED
                ),
            )
        total = jnp.zeros((block_len, LANE), WIDE)
        for offset in range(KERNEL):
            lanes = slice(offset * LANE, (offset + 1) * LANE)
            mask = same_doc(docs, slot, offset, block_len)
            term = jnp.where(
                mask, jnp.exp(jnp.where(mask, conv_weights[rows, lanes], MASKED) - top), 0.0
            )
            conv_weights[rows, lanes] = term
            total = total + term
        scale = 1.0 / total
        mixed = jnp.zeros((block_len, ATT), WIDE)
        for offset in range(KERNEL):
            lanes = slice(offset * LANE, (offset + 1) * LANE)
            weight = conv_weights[rows, lanes] * scale
            conv_weights[rows, lanes] = weight
            wide_weight = mm(two(*split_low(weight)), spread, NN)
            mixed = mixed + wide_weight * value_wide[slot, start + offset : start + offset + block_len, :]
        context[rows, :] = mixed.astype(LOW)


def head_queries(values, head):
    lane = lax.broadcasted_iota(jnp.int32, values.shape, 1)
    return jnp.where(lane // HEAD == head, values, jnp.zeros_like(values))


def blocks_overlap(bounds, slot, block):
    return (bounds[block, 0] <= bounds[slot, 1]) & (bounds[block, 1] >= bounds[slot, 0])


def attend_kernel(count, bounds, query, doc_query, doc_key, *rest):
    stacks, rest = rest[:count], rest[count:]
    out, stats, scores, top, total, mixed = rest
    tokens_here = query.shape[0]
    block_len = tokens_here // 2
    score_scale = HEAD ** (-0.5)
    for slot in range(2):
        rows = slice(slot * block_len, (slot + 1) * block_len)
        scaled = query[rows, :] * jnp.asarray(score_scale, LOW)
        queries = [head_queries(scaled, head) for head in range(2)]
        doc_here = doc_query[slot : slot + 1, :]
        top[...] = jnp.full(top.shape, MASKED, WIDE)
        total[...] = jnp.zeros(total.shape, WIDE)
        mixed[...] = jnp.zeros(mixed.shape, WIDE)

        def each(body):
            for place, stack in enumerate(stacks):

                def one(step, carry):
                    block = place * 2 + step

                    @pl.when(blocks_overlap(bounds, slot, block))
                    def _():
                        keys = pl.ds(pl.multiple_of(step * block_len, 16), block_len)
                        body(stack, keys, block)

                    return carry

                lax.fori_loop(0, 2, one, 0)

        def first(stack, keys, block):
            key_rows = stack[keys, :LANE]
            doc_rows = doc_key[block]
            allowed = tile_lanes(doc_rows, block_len // LANE) == doc_here
            for head in range(2):
                score = jnp.where(allowed, mm(key_rows, queries[head], NT), MASKED)
                scores[block, head] = score
                top[head] = jnp.maximum(top[head], jnp.max(score, axis=0, keepdims=True))

        each(first)

        def second(stack, keys, block):
            value_rows = stack[keys, LANE:]
            for head in range(2):
                term = jnp.exp(scores[block, head] - top[head, 0:1, :])
                total[head] = total[head] + jnp.sum(term, axis=0, keepdims=True)
                mixed[head] = mixed[head] + mm(value_rows, term.astype(LOW), TN)

        each(second)
        parts = []
        for head in range(2):
            scale = 1.0 / total[head, 0:1, :]
            parts.append(mixed[head, head * HEAD : (head + 1) * HEAD, :] * scale)
            stats[slot, head : head + 1, :] = top[head, 0:1, :] + jnp.log(total[head, 0:1, :])
        out[rows, :] = jnp.concatenate(parts, axis=0).T.astype(LOW)


def attend_back_kernel(count, bounds, query, doc_query, doc_key, attended, grad, stats, *rest):
    stacks, rest = rest[:count], rest[count:]
    grad_query, grad_own, grad_far, delta, grad_kv = rest
    tokens_here = query.shape[0]
    block_len = tokens_here // 2
    score_scale = HEAD ** (-0.5)
    head_row = lax.broadcasted_iota(jnp.int32, (8, LANE), 0)
    head_lane = lax.broadcasted_iota(jnp.int32, (8, LANE), 1) // HEAD
    chosen = jnp.where(head_row == head_lane, 1.0, 0.0).astype(LOW)
    for slot in range(2):
        rows = slice(slot * block_len, (slot + 1) * block_len)
        both = attended[rows, :].astype(WIDE) * grad[rows, :].astype(WIDE)
        high, low = split_low(both)
        delta[slot] = mm(chosen, high, NT) + mm(chosen, low, NT)
    grad_query[...] = jnp.zeros(grad_query.shape, WIDE)

    for place, stack in enumerate(stacks):
        out = (grad_own, grad_far)[2 * place // count]
        entry = place % (count // 2)

        def one(step, carry):
            block = place * 2 + step
            keys = pl.ds(pl.multiple_of(step * block_len, 16), block_len)
            grad_kv[...] = jnp.zeros(grad_kv.shape, WIDE)
            for slot in range(2):

                @pl.when(blocks_overlap(bounds, slot, block))
                def _():
                    rows = slice(slot * block_len, (slot + 1) * block_len)
                    key_rows = stack[keys, :LANE]
                    value_rows = stack[keys, LANE:]
                    scaled = query[rows, :] * jnp.asarray(score_scale, LOW)
                    allowed = tile_lanes(doc_key[block], block_len // LANE) == doc_query[slot : slot + 1, :]
                    for head in range(2):
                        query_here = head_queries(scaled, head)
                        grad_here = head_queries(grad[rows, :], head)
                        score = mm(key_rows, query_here, NT)
                        probs = jnp.where(
                            allowed, jnp.exp(score - stats[slot, head : head + 1, :]), 0.0
                        )
                        g_probs = mm(value_rows, grad_here, NT)
                        g_score = (probs * (g_probs - delta[slot, head : head + 1, :])).astype(LOW)
                        key_here = head_queries(key_rows, head)
                        grad_query[rows, :] += mm(g_score, key_here, TN)
                        grad_kv[:, :LANE] += mm(g_score, query_here, NN)
                        grad_kv[:, LANE:] += mm(probs.astype(LOW), grad_here, NN)

            out[entry, keys, :] = grad_kv[...].astype(LOW)
            return carry

        lax.fori_loop(0, 2, one, 0)
    grad_query[...] = grad_query[...] * score_scale


def norm_stats(values):
    mean = jnp.mean(values, axis=-1, keepdims=True)
    centred = values - mean
    spread = jnp.mean(centred * centred, axis=-1, keepdims=True)
    scale = lax.rsqrt(spread + EPSILON)
    return centred * scale, scale


def norm_back(normal, scale, grad):
    return scale * (
        grad
        - jnp.mean(grad, axis=-1, keepdims=True)
        - normal * jnp.mean(grad * normal, axis=-1, keepdims=True)
    )


def column_sum(values):
    return jnp.sum(values, axis=0, keepdims=True)


def middle_kernel(
    here,
    own,
    other,
    cot_own,
    cot_other,
    att_0,
    att_1,
    att_2,
    conv_context,
    inner_own,
    inner_far,
    tail_own,
    tail_far,
    vectors,
    inner_bias,
    out_own,
    out_other,
    resid_grad,
    g_att_0,
    g_att_1,
    g_att_2,
    g_conv,
    d_inner_own,
    d_inner_far,
    d_tail_own,
    d_tail_far,
    vector_grads,
    inner_bias_grad,
    w_out,
    context,
    normal_1,
    scale_1,
    hidden_low,
    active,
    slope,
    ffn_sum,
    grad_2,
    ffn_grad,
    attn_grad,
    d_out,
):
    block_len = own.shape[0]
    tokens_here = 2 * block_len
    inner_size = inner_own.shape[1]
    out_size = tail_own.shape[1] - inner_size
    half_width = inner_own.shape[2]
    cols = inner_own.shape[0]
    assemble(here, (tail_own, tail_far), "col", w_out, 1, out_size, inner_size)
    bias_out, gain_1, shift_1 = vectors[0:1, :], vectors[1:2, :], vectors[2:3, :]
    bias_outer, gain_2, shift_2 = vectors[3:4, :], vectors[4:5, :], vectors[5:6, :]
    context[0] = jnp.concatenate([att_0[...], att_1[...], att_2[...]], axis=1)
    context[1] = conv_context[...]
    sources = ((own, cot_own, out_own), (other, cot_other, out_other))
    for slot, (source, _, _) in enumerate(sources):
        rows = slice(slot * block_len, (slot + 1) * block_len)
        attn = (
            mm(context[0, rows, :], w_out[0, 0], NT)
            + mm(context[1, rows, :], w_out[0, 1], NT)
            + bias_out
        )
        normal, scale = norm_stats(source[...].astype(WIDE) + attn)
        normal_1[rows, :] = normal
        scale_1[rows, :] = jnp.broadcast_to(scale, (block_len, LANE))
        hidden = normal * gain_1 + shift_1
        left, right = half_pair(hidden.astype(LOW))
        hidden_low[0, rows, :] = left
        hidden_low[1, rows, :] = right
    ffn_sum[...] = jnp.zeros(ffn_sum.shape, WIDE)

    def each(body):
        for core, (inner, tail) in enumerate(((inner_own, tail_own), (inner_far, tail_far))):

            def one(entry, carry):
                dr, dc = place_of(entry, "row")
                entry_tail = (entry % 2) * 2 + (entry // 2) % 2 + (entry // 4) * 4
                group = here[0] ^ dr
                spot = group * (2 * cols // 2) + (here[1] ^ (dc + core))
                body(core, entry, entry_tail, group, spot, inner, tail)
                return carry

            lax.fori_loop(0, cols, one, 0)

    def forward(core, entry, entry_tail, group, spot, inner, tail):
        for slot in range(2):
            rows = slice(slot * block_len, (slot + 1) * block_len)
            pre = mm(hidden_low[group, rows, :], inner[entry], NT) + inner_bias[spot]
            half = 0.5 * (1.0 + lax.erf(pre * (0.5**0.5)))
            low = (pre * half).astype(LOW)
            active[core * cols + entry, rows, :] = low
            slope[core * cols + entry, rows, :] = half + pre * jnp.exp(-0.5 * pre * pre) * (
                0.3989422804014327
            )
            ffn_sum[group, rows, :] += mm(low, tail[entry_tail, :inner_size, :], NN)

    each(forward)
    vector_grads[...] = jnp.zeros(vector_grads.shape, WIDE)
    for slot, (_, cot, out) in enumerate(sources):
        rows = slice(slot * block_len, (slot + 1) * block_len)
        hidden = normal_1[rows, :] * gain_1 + shift_1
        resid = hidden + (two(ffn_sum[0, rows, :], ffn_sum[1, rows, :]) + bias_outer)
        normal, scale = norm_stats(resid)
        out[...] = (normal * gain_2 + shift_2).astype(LOW)
        cot_wide = cot[...].astype(WIDE)
        vector_grads[0:1, :] += column_sum(cot_wide * normal)
        vector_grads[1:2, :] += column_sum(cot_wide)
        grad = norm_back(normal, scale, cot_wide * gain_2)
        grad_2[rows, :] = grad
        low = grad.astype(LOW)
        vector_grads[2:3, :] += column_sum(low.astype(WIDE))
        left, right = half_pair(low)
        ffn_grad[0, rows, :] = left
        ffn_grad[1, rows, :] = right
    ffn_sum[...] = jnp.zeros(ffn_sum.shape, WIDE)

    def backward(core, entry, entry_tail, group, spot, inner, tail):
        d_inner = (d_inner_own, d_inner_far)[core]
        d_tail = (d_tail_own, d_tail_far)[core]
        where = core * cols + entry
        lows = []
        for slot in range(2):
            rows = slice(slot * block_len, (slot + 1) * block_len)
            g_active = mm(ffn_grad[group, rows, :], tail[entry_tail, :inner_size, :], NT)
            low = (g_active * slope[where, rows, :]).astype(LOW)
            lows.append(low)
            ffn_sum[group, rows, :] += mm(low, inner[entry], NN)
        g_inner = jnp.concatenate(lows, axis=0)
        inner_bias_grad[spot] = column_sum(g_inner.astype(WIDE))
        d_inner[entry] = mm(g_inner, hidden_low[group], TN).astype(LOW)
        d_tail[entry_tail, :inner_size, :] = mm(active[where], ffn_grad[group], TN).astype(LOW)

    each(backward)
    for slot in range(2):
        rows = slice(slot * block_len, (slot + 1) * block_len)
        grad = grad_2[rows, :] + two(ffn_sum[0, rows, :], ffn_sum[1, rows, :])
        normal = normal_1[rows, :]
        vector_grads[3:4, :] += column_sum(grad * normal)
        vector_grads[4:5, :] += column_sum(grad)
        grad = norm_back(normal, scale_1[rows, 0:1], grad * gain_1)
        resid_grad[rows, :] = grad
        low = grad.astype(LOW)
        vector_grads[5:6, :] += column_sum(low.astype(WIDE))
        attn_grad[rows, :] = low
        g_att = mm(low, w_out[0, 0], NN).astype(LOW)
        for index, out in enumerate((g_att_0, g_att_1, g_att_2)):
            out[rows, :] = g_att[:, index * LANE : (index + 1) * LANE]
        g_conv[rows, :] = mm(low, w_out[0, 1], NN).astype(LOW)
    for half in range(2):
        d_out[0, half] = mm(attn_grad[...], context[half], TN).astype(LOW)
    cut(here, d_out, (d_tail_own, d_tail_far), "col", 1, out_size, inner_size)


def branch_back_kernel(
    own,
    other,
    low_rim,
    high_rim,
    docs,
    w_full,
    depth_gain,
    tap_weight,
    query,
    g_conv,
    value_wide,
    key_conv,
    conv_attn,
    conv_weights,
    g_key_conv,
    g_query,
    d_tap_weight,
    d_tap_bias,
    d_depth,
    bias_grad,
    g_ext_value,
    g_ext_tokens,
    wide,
    weight_grad,
    low_grad,
):
    block_len = own.shape[0]
    start = RIM - KERNEL // 2
    spread = spread_heads()
    d_tap_weight[...] = jnp.zeros(d_tap_weight.shape, WIDE)
    d_tap_bias[...] = jnp.zeros(d_tap_bias.shape, WIDE)
    d_depth[...] = jnp.zeros(d_depth.shape, WIDE)
    bias_grad[...] = jnp.zeros(bias_grad.shape, WIDE)
    g_ext_value[...] = jnp.zeros(g_ext_value.shape, WIDE)
    g_ext_tokens[...] = jnp.zeros(g_ext_tokens.shape, WIDE)
    for slot, source in enumerate((own, other)):
        rows = slice(slot * block_len, (slot + 1) * block_len)
        fill_wide(wide, slot, low_rim, source, high_rim)
        grad = g_conv[rows, :].astype(WIDE)
        mean = jnp.zeros((block_len, LANE), WIDE)
        for offset in range(KERNEL):
            lanes = slice(offset * LANE, (offset + 1) * LANE)
            place = slice(start + offset, start + offset + block_len)
            high, low = split_low(grad * value_wide[slot, place, :])
            back = mm(high, spread[:LANE], NT) + mm(low, spread[:LANE], NT)
            weight_grad[:, lanes] = back
            mean = mean + conv_weights[rows, lanes] * back
        for offset in range(KERNEL):
            lanes = slice(offset * LANE, (offset + 1) * LANE)
            place = slice(start + offset, start + offset + block_len)
            weight = conv_weights[rows, lanes]
            low_grad[:, lanes] = (weight * (weight_grad[:, lanes] - mean)).astype(LOW)
            g_ext_value[slot, place, :] += mm(two(*split_low(weight)), spread, NN) * grad
        d_tap_weight[...] += mm(conv_attn[rows, :], low_grad[...], TN)
        d_tap_bias[...] += column_sum(low_grad[...].astype(WIDE))
        g_attn = mm(low_grad[...], tap_weight[...], NT)
        g_key = (g_attn * query[rows, :].astype(WIDE)).astype(LOW)
        g_key_conv[rows, :] = g_key
        bias_grad[0:1, :] += column_sum(g_ext_value[slot])
        bias_grad[1:2, :] += column_sum(g_key.astype(WIDE))
        g_query[rows, :] = g_attn * key_conv[rows, :]
        for half in range(2):
            g_depth = mm(g_key, w_full[1, half], NN)
            for block in range(g_depth.shape[1] // LANE):
                column = half * g_depth.shape[1] + block * LANE
                lanes = slice(column, column + LANE)
                piece = g_depth[:, block * LANE : (block + 1) * LANE]
                for offset in range(KERNEL):
                    place = slice(start + offset, start + offset + block_len)
                    masked = jnp.where(same_doc(docs, slot, offset, block_len), piece, 0.0)
                    d_depth[offset : offset + 1, lanes] += column_sum(masked * wide[slot, place, lanes])
                    g_ext_tokens[slot, place, lanes] += masked * depth_gain[offset : offset + 1, lanes]


def branch_weights_kernel(
    here,
    own,
    other,
    w_full,
    depth_low,
    g_key_conv,
    g_ext_value,
    g_ext_tokens,
    after,
    before,
    resid_grad,
    d_own,
    d_far,
    token_grad,
    ext,
    d_full,
    tokens,
    value_grad,
):
    block_len = own.shape[0]
    size = d_own.shape[1] // 2
    for slot, source in enumerate((own, other)):
        rows = slice(slot * block_len, (slot + 1) * block_len)
        tokens[rows, :] = source[...]
        for grads, lanes in ((g_ext_value, slice(0, ATT)), (g_ext_tokens, slice(ATT, ext.shape[1]))):
            ext[:, lanes] = grads[slot, RIM : RIM + block_len, :]
        ext[0:RIM, :] += before[slot].astype(WIDE)
        ext[block_len - RIM :, :] += after[slot].astype(WIDE)
        low = ext[:, :ATT].astype(LOW)
        value_grad[rows, :] = low
        token_grad[rows, :] = (
            resid_grad[rows, :]
            + ext[:, ATT:]
            + two(mm(low, w_full[0, 0], NN), mm(low, w_full[0, 1], NN))
        )
    for half in range(2):
        lanes = slice(half * d_own.shape[2], (half + 1) * d_own.shape[2])
        d_full[0, half] = mm(value_grad[...], tokens[:, lanes], TN).astype(LOW)
        d_full[1, half] = mm(g_key_conv[...], depth_low[:, lanes], TN).astype(LOW)
    cut(here, d_full, (d_own, d_far), "col", 2, size, 0)


def first_weights_kernel(
    here,
    own,
    other,
    grad_0,
    grad_1,
    grad_2,
    g_query,
    pair_0,
    pair_1,
    pair_2,
    d_own,
    d_far,
    lows,
    bias_grad,
    d_full,
    tokens,
):
    block_len = own.shape[0]
    size = d_own.shape[1] // 3
    pairs = (pair_0, pair_1, pair_2)
    for slot, source in enumerate((own, other)):
        tokens[slot * block_len : (slot + 1) * block_len, :] = source[...]
    lows[0] = (
        jnp.concatenate([grad_0[...], grad_1[...], grad_2[...]], axis=1) + g_query[...]
    ).astype(LOW)
    for part in range(2):
        lows[1 + part] = jnp.concatenate(
            [pair[:, part * LANE : (part + 1) * LANE] for pair in pairs], axis=1
        )
    bias_grad[0:1, :] = column_sum(lows[0].astype(WIDE))
    bias_grad[1:2, :] = column_sum(lows[2].astype(WIDE))
    for part in range(3):
        for half in range(2):
            lanes = slice(half * d_own.shape[2], (half + 1) * d_own.shape[2])
            d_full[part, half] = mm(lows[part], tokens[:, lanes], TN).astype(LOW)
    cut(here, d_full, (d_own, d_far), "row", 3, size, 0)


def token_kernel(w_full, lows, token_in, token_own, token_other):
    block_len = token_own.shape[0]
    for slot, out in enumerate((token_own, token_other)):
        rows = slice(slot * block_len, (slot + 1) * block_len)
        total = token_in[rows, :]
        for part in range(3):
            low = lows[part, rows, :]
            total = total + two(mm(low, w_full[part, 0], NN), mm(low, w_full[part, 1], NN))
        out[...] = total.astype(out.dtype)


def local(
    tokens,
    cotangent,
    doc_ids,
    proj_weight,
    out_weight,
    inner_weight,
    outer_weight,
    depth_weight,
    proj_bias,
    kernel_weight,
    kernel_bias,
    out_bias,
    norm1_gain,
    norm1_shift,
    inner_bias,
    outer_bias,
    norm2_gain,
    norm2_shift,
):
    block_len = tokens.shape[1]
    model_width = tokens.shape[2]
    margin = KERNEL // 2
    col_count = lax.axis_size("col")
    row_count = lax.axis_size("row")
    row_here = lax.axis_index("row")
    col_here = lax.axis_index("col")
    here = jnp.stack([row_here, col_here]).astype(jnp.int32)
    tokens_here = 2 * block_len
    entries = col_count // 2 * row_count
    pair_entries = col_count // 2
    cut_proj = proj_weight.shape[2]
    cut_out = out_weight.shape[1]
    cut_inner = inner_weight.shape[2]
    lanes = proj_weight.shape[1]

    far_steps = [step for step in steps_of("col") if step > 1]

    proj_t = jnp.transpose(proj_weight, (0, 2, 1))
    doc_slab = jnp.pad(
        doc_ids[:, 0].astype(LOW), ((0, DOC_ROWS - doc_ids.shape[0]), (0, lanes - block_len))
    )
    first = {(0, 0): jnp.concatenate([proj_t[:3].reshape(-1, lanes), doc_slab], axis=0)}
    branch = {(0, 0): proj_t[3:].reshape(-1, lanes)}

    def spread_row(held, *marks):
        for dr, dc in list(held):
            held[(1, dc)] = swap(after(held[(dr, dc)], *marks), "row", 1)

    def spread_col(held, step):
        for dr, dc in list(held):
            held[(dr, dc ^ step)] = swap(held[(dr, dc)], "col", step)

    def trade(pair, *marks):
        sent = pick(pair, 1 - row_here)
        if marks:
            sent = after(sent, *marks)
        return pick(pair, row_here), swap(sent, "row", 1)

    spread_row(first)
    first_row = first[(1, 0)]
    for step in far_steps:
        spread_col(first, step)
    own, other = trade(tokens, first_row)
    for dr, dc in list(first):
        first[(dr, dc ^ 1)] = swap(first[(dr, dc)], "col", 1)
    branch[(0, 0)] = after(branch[(0, 0)], first[(0, far_steps[0])])
    for step in far_steps:
        spread_col(branch, step)
    spread_row(branch, other)
    for dr, dc in list(branch):
        branch[(dr, dc ^ 1)] = swap(branch[(dr, dc)], "col", 1)

    def wrapped(block, step):
        moved = shift(block, "col", step)
        edge = 0 if step > 0 else col_count - 1
        return jnp.where(col_here == edge, moved[::-1], moved)

    low_rim = wrapped(jnp.stack([own[block_len - RIM :], other[block_len - RIM :]]), 1)
    high_rim = wrapped(jnp.stack([own[:RIM], other[:RIM]]), -1)

    inner = grow(after(inner_weight[0].T, other, branch[(1, 0)])[None], "row", 1)
    inner_row = inner
    tail = grow(
        after(
            jnp.concatenate([outer_weight[0], out_weight.T], axis=0), first[(1, far_steps[-1])]
        )[None],
        "col",
        far_steps[0],
    )

    wide_bias = proj_bias.astype(WIDE)
    tap_weight = jnp.pad(
        kernel_weight.reshape(ATT, HEADS, KERNEL).transpose(0, 2, 1),
        ((0, 0), (0, 0), (0, LANE - HEADS)),
    ).reshape(ATT, KERNEL * LANE)
    tap_bias = (
        jnp.pad(kernel_bias.reshape(HEADS, KERNEL).T, ((0, 0), (0, LANE - HEADS)))
        .reshape(1, KERNEL * LANE)
        .astype(WIDE)
    )
    depth_gain = jnp.pad(depth_weight.astype(WIDE), ((0, 16 - KERNEL), (0, 0)))
    vectors = jnp.stack(
        [out_bias, norm1_gain, norm1_shift, outer_bias, norm2_gain, norm2_shift, norm2_shift, norm2_shift]
    ).astype(WIDE)

    first_keys = sorted(first, key=lambda key: (key[1] & 1, key[1], key[0]))
    query, *pairs = kernel_call(
        functools.partial(project_kernel, first_keys),
        [((tokens_here, ATT), LOW)]
        + [((tokens_here, 2 * LANE), LOW)] * PAIRS
        + [((3, row_count, ATT, lanes), LOW)],
    )(here, own, other, wide_bias, *[first[key] for key in first_keys])
    w_first = pairs.pop()

    gathered = []
    for pair in pairs:
        pieces = [pair]
        for step in far_steps:
            pieces = pieces + [swap(piece, "col", step) for piece in pieces]
        gathered.append(pieces)
    far_pair = gathered[0][1]
    for pieces in gathered:
        pieces.extend([swap(piece, "col", 1) for piece in list(pieces)])
    tail = grow(after(tail, inner_row, query), "row", 1)
    inner = after(inner, far_pair)
    for step in far_steps:
        inner = grow(inner, "col", step)
    for step in far_steps[1:]:
        tail = grow(tail, "col", step)
    inner_own, inner_far = inner, swap(inner, "col", 1)
    tail_own, tail_far = tail, swap(tail, "col", 1)
    cot_own, cot_other = trade(cotangent, inner_row, query)

    doc_blocks = jnp.stack(
        [
            lax.dynamic_slice(first[key], (3 * cut_proj + row_here, 0), (1, block_len))[0]
            for key in first_keys
        ]
    ).astype(jnp.int32)
    bounds = jnp.stack([doc_blocks[:, 0], doc_blocks[:, -1]], axis=1)
    doc_key = jnp.broadcast_to(doc_blocks[:, :, None], doc_blocks.shape + (LANE,))

    def doc_rim(slot, step):
        position = (row_here ^ slot) * col_count + col_here + step
        inside = (position >= 0) & (position < row_count * col_count)
        position = jnp.clip(position, 0, row_count * col_count - 1)
        dr = (position // col_count) ^ row_here
        dc = (position % col_count) ^ col_here
        return jnp.where(inside, pick(doc_blocks, (dc % 2) * entries + (dc // 2) * 2 + dr), -1)

    doc_ext = jnp.stack(
        [
            jnp.concatenate(
                [doc_rim(slot, -1)[block_len - RIM :], doc_blocks[slot], doc_rim(slot, 1)[:RIM]]
            )
            for slot in range(2)
        ]
    )
    doc_rows = jnp.broadcast_to(doc_ext[:, :, None], doc_ext.shape + (LANE,))

    ext_len = block_len + 2 * RIM
    branch_keys = list(branch)
    conv_context, depth_low, value_wide, key_conv, conv_attn, conv_weights, w_branch = kernel_call(
        functools.partial(branch_kernel, branch_keys),
        [
            ((tokens_here, ATT), LOW),
            ((tokens_here, model_width), LOW),
            ((2, ext_len, ATT), WIDE),
            ((tokens_here, ATT), WIDE),
            ((tokens_here, ATT), LOW),
            ((tokens_here, KERNEL * LANE), WIDE),
            ((2, row_count, ATT, lanes), LOW),
        ],
        [((2, ext_len, model_width), WIDE)],
        cost=11,
    )(
        here,
        own,
        other,
        low_rim,
        high_rim,
        doc_rows,
        depth_gain,
        wide_bias,
        tap_weight,
        tap_bias,
        query,
        *[branch[key] for key in branch_keys],
    )

    doc_query = doc_blocks[:2]
    attended = []
    stats = []
    for index in range(PAIRS):
        query_pair = query[:, index * LANE : (index + 1) * LANE]
        if index == 0:
            query_pair = after(query_pair, conv_context)
        out, stat = kernel_call(
            functools.partial(attend_kernel, col_count),
            [((tokens_here, LANE), LOW), ((2, 8, block_len), WIDE)],
            [
                ((2 * col_count, 2, block_len, block_len), WIDE),
                ((2, 1, block_len), WIDE),
                ((2, 1, block_len), WIDE),
                ((2, LANE, block_len), WIDE),
            ],
            cost=8,
        )(bounds, query_pair, doc_query, doc_key, *gathered[index])
        attended.append(out)
        stats.append(stat)

    (
        out_own,
        out_other,
        resid_grad,
        *g_att,
        g_conv,
        d_inner_own,
        d_inner_far,
        d_tail_own,
        d_tail_far,
        vector_grads,
        inner_bias_grad,
    ) = kernel_call(
        middle_kernel,
        [
            ((block_len, model_width), LOW),
            ((block_len, model_width), LOW),
            ((tokens_here, model_width), WIDE),
        ]
        + [((tokens_here, LANE), LOW)] * PAIRS
        + [((tokens_here, ATT), LOW)]
        + [((entries, cut_inner, lanes), LOW)] * 2
        + [((entries, cut_inner + cut_out, lanes), LOW)] * 2
        + [((8, model_width), WIDE), ((2 * entries, 1, cut_inner), WIDE)],
        [
            ((1, row_count, model_width, lanes), LOW),
            ((row_count, tokens_here, lanes), LOW),
            ((tokens_here, model_width), WIDE),
            ((tokens_here, LANE), WIDE),
            ((row_count, tokens_here, lanes), LOW),
            ((2 * entries, tokens_here, cut_inner), LOW),
            ((2 * entries, tokens_here, cut_inner), WIDE),
            ((row_count, tokens_here, lanes), WIDE),
            ((tokens_here, model_width), WIDE),
            ((row_count, tokens_here, lanes), LOW),
            ((tokens_here, model_width), LOW),
            ((1, row_count, model_width, lanes), LOW),
        ],
        cost=30,
    )(
        here,
        own,
        other,
        cot_own,
        cot_other,
        *attended,
        conv_context,
        inner_own,
        inner_far,
        tail_own,
        tail_far,
        vectors,
        inner_bias.astype(WIDE).reshape(2 * entries, 1, cut_inner),
    )

    row_stages = [("row", 1)] + [("col", step) for step in far_steps]
    col_stages = [("col", far_steps[0]), ("row", 1)] + [("col", step) for step in far_steps[1:]]
    row_stages.reverse()
    col_stages.reverse()

    class GridSum:
        def __init__(self, kept, sent, stages):
            self.kept = kept
            self.moved = swap(sent, "col", 1)
            self.todo = list(stages)

        def finish(self, *marks):
            moved = after(self.moved, *marks) if marks else self.moved
            if not self.todo:
                self.kept = add_low(self.kept, moved)
                return self.kept
            self.kept, sent = join(self.kept, moved)
            axis, step = self.todo.pop(0)
            self.moved = swap(sent, axis, step)
            return sent

        def rest(self, *marks):
            while self.todo:
                self.finish(*marks)
            return self.finish(*marks)[0]

    inner_sum = GridSum(d_inner_own, d_inner_far, row_stages)
    tail_sum = GridSum(d_tail_own, d_tail_far, col_stages)
    query_grads = []
    pair_sums = []
    marks = []
    for index in range(PAIRS):
        query_pair = query[:, index * LANE : (index + 1) * LANE]
        if marks:
            query_pair = after(query_pair, *marks)
        grad_query, grad_own, grad_far = kernel_call(
            functools.partial(attend_back_kernel, col_count),
            [
                ((tokens_here, LANE), WIDE),
                ((pair_entries, tokens_here, 2 * LANE), LOW),
                ((pair_entries, tokens_here, 2 * LANE), LOW),
            ],
            [((2, 8, block_len), WIDE), ((block_len, 2 * LANE), WIDE)],
            cost=13,
        )(
            bounds,
            query_pair,
            doc_query,
            doc_key,
            attended[index],
            g_att[index],
            stats[index],
            *gathered[index],
        )
        query_grads.append(grad_query)
        pair_sums.append(GridSum(grad_own, grad_far, [("col", step) for step in reversed(far_steps)]))
        marks = [grad_query]
        if len(inner_sum.todo) > 0:
            marks += [inner_sum.finish(grad_query), tail_sum.finish(grad_query)]
        if index > 0:
            marks.append(pair_sums[index - 1].finish(grad_query))
    marks.append(pair_sums[-1].finish())
    wide_part = jnp.concatenate([inner_sum.rest(grad_query), tail_sum.rest(grad_query)], axis=0)
    wide_sum = DataSum(wide_part)

    (
        g_key_conv,
        g_query,
        d_tap_weight,
        d_tap_bias,
        d_depth,
        branch_bias,
        g_ext_value,
        g_ext_tokens,
    ) = kernel_call(
        branch_back_kernel,
        [
            ((tokens_here, ATT), LOW),
            ((tokens_here, ATT), WIDE),
            ((ATT, KERNEL * LANE), WIDE),
            ((1, KERNEL * LANE), WIDE),
            ((16, model_width), WIDE),
            ((8, ATT), WIDE),
            ((2, ext_len, ATT), WIDE),
            ((2, ext_len, model_width), WIDE),
        ],
        [
            ((2, ext_len, model_width), WIDE),
            ((block_len, KERNEL * LANE), WIDE),
            ((block_len, KERNEL * LANE), LOW),
        ],
        smem=0,
        cost=16,
    )(
        own,
        other,
        low_rim,
        high_rim,
        doc_rows,
        w_branch,
        depth_gain,
        tap_weight,
        query,
        after(g_conv, wide_part, *marks),
        value_wide,
        key_conv,
        conv_attn,
        conv_weights,
    )
    pair_grads = [part.rest(g_query) for part in pair_sums]
    wide_stage = wide_sum.finish(g_query)

    def rim_of(start):
        return jnp.concatenate(
            [g_ext_value[:, start : start + RIM], g_ext_tokens[:, start : start + RIM]], axis=2
        ).astype(LOW)

    from_after = wrapped(rim_of(0), -1)
    from_before = wrapped(rim_of(RIM + block_len), 1)

    d_first_own, d_first_far, lows, first_bias = kernel_call(
        first_weights_kernel,
        [((entries, 3 * cut_proj, lanes), LOW)] * 2
        + [((3, tokens_here, ATT), LOW), ((8, ATT), WIDE)],
        [((3, row_count, ATT, lanes), LOW), ((tokens_here, model_width), LOW)],
        cost=6,
    )(here, own, other, *query_grads, after(g_query, wide_stage), *pair_grads)
    first_sum = GridSum(d_first_own, d_first_far, row_stages)
    wide_stage = wide_sum.finish(first_bias)

    d_branch_own, d_branch_far, token_grad = kernel_call(
        branch_weights_kernel,
        [((entries, 2 * cut_proj, lanes), LOW)] * 2 + [((tokens_here, model_width), WIDE)],
        [
            ((block_len, ATT + model_width), WIDE),
            ((2, row_count, ATT, lanes), LOW),
            ((tokens_here, model_width), LOW),
            ((tokens_here, ATT), LOW),
        ],
        cost=6,
    )(
        here,
        own,
        other,
        w_branch,
        depth_low,
        after(g_key_conv, lows, wide_stage),
        g_ext_value,
        g_ext_tokens,
        from_after,
        from_before,
        resid_grad,
    )
    branch_sum = GridSum(d_branch_own, d_branch_far, col_stages)
    wide_stage = wide_sum.finish(token_grad)
    first_stage = first_sum.finish(token_grad)
    branch_stage = branch_sum.finish()
    token_own, token_other = kernel_call(
        token_kernel,
        [((block_len, model_width), WIDE), ((block_len, model_width), LOW)],
        smem=0,
        cost=6,
    )(w_first, lows, after(token_grad, wide_stage, first_stage, branch_stage))
    wide_sum.finish(token_own)
    wide_sum = wide_sum.rest().astype(WIDE)
    first_part = first_sum.rest(token_own)
    branch_part = branch_sum.rest(token_own)
    proj_sum = DataSum(jnp.concatenate([first_part, branch_part], axis=0)).rest().astype(WIDE)

    def tap_layout(grads):
        return grads.reshape(-1, KERNEL, LANE)[:, :, :HEADS].transpose(0, 2, 1).reshape(-1, HEADS * KERNEL)

    items = [
        vector_grads[:6],
        inner_bias_grad,
        d_depth[:KERNEL],
        tap_layout(d_tap_weight),
        tap_layout(d_tap_bias),
        branch_bias[:2],
        first_bias[:2],
    ]
    flat = jnp.concatenate([item.reshape(-1) for item in items])
    flat = jnp.pad(flat, (0, -flat.shape[0] % 1024)).reshape(-1, LANE)
    flat = grid_sum(flat).reshape(-1)
    finals = []
    start = 0
    for item in items:
        finals.append(flat[start : start + item.size].reshape(item.shape))
        start += item.size
    vector_sum, inner_bias_sum, depth_sum, tap_weight_sum, tap_bias_sum, branch_bias_sum, first_bias_sum = finals

    def give_back(here_rows, there_rows):
        moved = swap(there_rows, "row", 1).astype(here_rows.dtype)
        return jnp.where(
            row_here == 0, jnp.stack([here_rows, moved]), jnp.stack([moved, here_rows])
        )

    return (
        give_back(out_own, out_other),
        give_back(token_own, token_other),
        jnp.transpose(proj_sum.reshape(5, cut_proj, lanes), (0, 2, 1)),
        wide_sum[2 * cut_inner :].T,
        wide_sum[:cut_inner].T[None],
        wide_sum[cut_inner : 2 * cut_inner][None],
        depth_sum,
        jnp.concatenate([first_bias_sum, branch_bias_sum], axis=0),
        tap_weight_sum,
        tap_bias_sum[0],
        vector_sum[5],
        vector_sum[3],
        vector_sum[4],
        inner_bias_sum.reshape(-1),
        vector_sum[2],
        vector_sum[0],
        vector_sum[1],
    )


def solution(mesh):
    return jax.shard_map(
        local,
        mesh=mesh,
        in_specs=(
            P(None, ("dp", "row", "col"), None),
            P(None, ("dp", "row", "col"), None),
            P(None, "dp", ("row", "col")),
            P(None, "row", "col"),
            P("row", "col"),
            P("row", None, "col"),
            P("row", "col", None),
        )
        + (P(),) * 11,
        out_specs=(
            P(None, ("dp", "row", "col"), None),
            P(None, ("dp", "row", "col"), None),
            P(None, "row", "col"),
            P("row", "col"),
            P("row", None, "col"),
            P("row", "col", None),
        )
        + (P(),) * 11,
        check_vma=False,
    )
```

```python
import functools

import jax
import jax.numpy as jnp
from jax import lax
from jax.experimental import pallas as pl
from jax.experimental.pallas import tpu as pltpu
from jax.sharding import PartitionSpec as P

HEADS = 6
HEAD = 64
KERNEL = 9
FF = 3072
ATT = 384
PAIRS = HEADS // 2
LANE = 128
RIM = 8
DOC_ROWS = 16

EPSILON = 1e-12
MASKED = -1e30
LOW = jnp.bfloat16
WIDE = jnp.float32


def swap(block, axis, step):
    count = lax.axis_size(axis)
    return lax.ppermute(block, axis, [(i, i ^ step) for i in range(count)])


def shift(block, axis, step):
    count = lax.axis_size(axis)
    return lax.ppermute(block, axis, [(i, (i + step) % count) for i in range(count)])


def steps_of(axis):
    steps = []
    step = 1
    while step < lax.axis_size(axis):
        steps.append(step)
        step *= 2
    return steps


def pick(block, index):
    return lax.dynamic_index_in_dim(block, index, 0, keepdims=False)


NT = (((1,), (1,)), ((), ()))
NN = (((1,), (0,)), ((), ()))
TN = (((0,), (0,)), ((), ()))
NT_ROWS = (((0,), (1,)), ((), ()))


def mm(left, right, how):
    return lax.dot_general(left, right, how, preferred_element_type=WIDE)


def kernel_call(body, outs, scratch=(), smem=1, cost=5, parts=0, part=0):
    def run(*args):
        specs = [
            pl.BlockSpec(memory_space=pltpu.SMEM if place < smem else pltpu.VMEM)
            for place in range(len(args) - parts)
        ]
        specs += [
            pl.BlockSpec((arg.shape[0], 2 * LANE), lambda step: (0, part)) for arg in args[len(args) - parts :]
        ]
        return pl.pallas_call(
            body,
            grid=(1,),
            in_specs=specs,
            out_specs=[pl.BlockSpec(memory_space=pltpu.VMEM)] * len(outs),
            out_shape=[jax.ShapeDtypeStruct(shape, kind) for shape, kind in outs],
            scratch_shapes=[pltpu.VMEM(shape, kind) for shape, kind in scratch],
            cost_estimate=pl.CostEstimate(
                flops=int(cost * 1e9), bytes_accessed=int(cost * 3.6e6), transcendentals=0
            ),
        )(*args)

    return run


def place_of(entry, kind):
    if kind == "col":
        entry = (entry & 1) * 2 + (entry // 2) % 2 + (entry // 4) * 4
    return entry % 2, (entry // 2) * 2


def stages_of(kind):
    far = [("col", step) for step in steps_of("col") if step > 1]
    row = [("row", 1)]
    return row + far if kind == "row" else far[:1] + row + far[1:]


def after(value, *marks):
    return lax.optimization_barrier((value,) + marks)[0]


def grow(stack, axis, step):
    return jnp.concatenate([stack, swap(stack, axis, step)], axis=0)


def add_low(kept, moved):
    return (kept.astype(WIDE) + moved.astype(WIDE)).astype(LOW)


def join(kept, moved):
    half = kept.shape[0] // 2
    return add_low(kept[:half], moved[:half]), add_low(kept[half:], moved[half:])


class DataSum:
    def __init__(self, part):
        self.index = lax.axis_index("dp")
        steps = steps_of("dp")
        self.todo = [(True, step) for step in steps] + [(False, step) for step in reversed(steps)]
        self.part = part
        self.start()

    def start(self):
        down, step = self.todo[0]
        self.bit = (self.index // step) % 2
        if down:
            self.halves = self.part.reshape((2, self.part.shape[0] // 2) + self.part.shape[1:])
            self.moved = swap(pick(self.halves, 1 - self.bit), "dp", step)
        else:
            self.moved = swap(self.part, "dp", step)

    def finish(self, *marks):
        moved = after(self.moved, *marks) if marks else self.moved
        down, _ = self.todo.pop(0)
        if down:
            self.part = add_low(pick(self.halves, self.bit), moved)
        else:
            self.part = jnp.where(
                self.bit == 0,
                jnp.concatenate([self.part, moved], axis=0),
                jnp.concatenate([moved, self.part], axis=0),
            )
        if self.todo:
            self.start()
        return self.part

    def rest(self, *marks):
        while self.todo:
            self.finish(*marks)
        return self.part


class FlatSum:
    def __init__(self, flat):
        self.todo = [("col", 1), ("row", 1)] + [("col", step) for step in steps_of("col") if step > 1]
        self.todo += [("dp", step) for step in steps_of("dp")]
        self.low = flat
        self.start()

    def start(self):
        self.moved = swap(self.low, *self.todo[0])

    def finish(self, *marks):
        moved = after(self.moved, *marks) if marks else self.moved
        self.todo.pop(0)
        self.low = add_low(self.low, moved)
        if self.todo:
            self.start()
        return self.low


def assemble_pieces(here, pieces, full, parts, size):
    for (dr, dc), piece in pieces:
        row = here[0] ^ dr
        col = here[1] ^ dc
        for part in range(parts):
            full[part, row, pl.ds(pl.multiple_of(col * size, 16), size), :] = piece[
                part * size : (part + 1) * size, :
            ]


def assemble(here, stacks, kind, full, parts, size, start):
    for core, stack in enumerate(stacks):

        def one(entry, carry):
            dr, dc = place_of(entry, kind)
            row = here[0] ^ dr
            col = here[1] ^ (dc + core)
            for part in range(parts):
                full[part, row, pl.ds(pl.multiple_of(col * size, 16), size), :] = stack[
                    entry, start + part * size : start + (part + 1) * size, :
                ]
            return carry

        lax.fori_loop(0, stack.shape[0], one, 0)


def cut(here, full, outs, kind, parts, size, start):
    for core, out in enumerate(outs):

        def one(entry, carry):
            dr, dc = place_of(entry, kind)
            row = here[0] ^ dr
            col = here[1] ^ (dc + core)
            for part in range(parts):
                out[entry, start + part * size : start + (part + 1) * size, :] = full[
                    part, row, pl.ds(pl.multiple_of(col * size, 16), size), :
                ]
            return carry

        lax.fori_loop(0, out.shape[0], one, 0)


def two(left, right):
    return jnp.concatenate([left, right], axis=1)


def half_pair(value):
    return value[:, : value.shape[1] // 2], value[:, value.shape[1] // 2 :]


def project_kernel(keys, here, own, other, bias, *rest):
    weights, rest = rest[: len(keys)], rest[len(keys) :]
    query, pairs, w_full = rest
    size = (weights[0].shape[0] - DOC_ROWS) // 3
    block_len = own.shape[0]
    assemble_pieces(here, list(zip(keys, weights)), w_full, 3, size)
    for slot, source in enumerate((own, other)):
        left, right = half_pair(source[...])
        rows = pl.ds(slot * block_len, block_len)

        def product(part):
            return mm(left, w_full[part, 0], NT) + mm(right, w_full[part, 1], NT)

        query[rows, :] = (product(0) + bias[0:1, :]).astype(LOW)
        key_low = product(1).astype(LOW)
        value_low = (product(2) + bias[1:2, :]).astype(LOW)
        for index in range(PAIRS):
            lanes = slice(index * LANE, (index + 1) * LANE)
            pairs[rows, 2 * index * LANE : 2 * (index + 1) * LANE] = two(key_low[:, lanes], value_low[:, lanes])


def tile_lanes(mask, times):
    return jnp.concatenate([mask] * times, axis=1)


def split_low(values):
    high = values.astype(LOW)
    return high, (values - high.astype(WIDE)).astype(LOW)


def fill_wide(wide, slot, low_rim, source, high_rim):
    block_len = source.shape[0]
    wide[slot, 0:RIM, :] = low_rim[slot].astype(WIDE)
    wide[slot, RIM : RIM + block_len, :] = source[...].astype(WIDE)
    wide[slot, RIM + block_len : RIM + block_len + RIM, :] = high_rim[slot].astype(WIDE)


def same_doc(docs, slot, offset, block_len):
    start = RIM - KERNEL // 2 + offset
    return docs[slot, start : start + block_len, :] == docs[slot, RIM : RIM + block_len, :]


def spread_heads():
    head = lax.broadcasted_iota(jnp.int32, (2 * LANE, ATT), 0) % LANE
    lane = lax.broadcasted_iota(jnp.int32, (2 * LANE, ATT), 1)
    return jnp.where(lane // HEAD == head, 1.0, 0.0).astype(LOW)


def take_rims(keys, here, pieces, start, cols, low_rim, high_rim):
    for rims, step, edge, first in ((low_rim, -1, 0, 0), (high_rim, 1, cols - 1, 2 * RIM)):
        source = here[1] ^ ((here[1] + step + cols) % cols)
        turn = jnp.where(here[1] == edge, 1, 0)
        for (dr, dc), piece in zip(keys, pieces):
            if dr == 0 and dc > 0:

                @pl.when(source == dc)
                def _():
                    rows = piece[start : start + 8 * RIM, :].astype(WIDE)
                    for slot in range(2):
                        place = first + slot * RIM
                        left = rows[place : place + RIM, :]
                        right = rows[4 * RIM + place : 4 * RIM + place + RIM, :]
                        rims[slot ^ turn] = two(left, right).astype(LOW)


def branch_kernel(
    keys, size, cols, here, own, other, docs, depth_gain, bias, tap_weight, tap_bias, query, *rest
):
    weights, rest = rest[: len(keys)], rest[len(keys) :]
    (
        context,
        depth_low,
        value_wide,
        key_conv,
        conv_attn,
        conv_weights,
        w_full,
        low_rim,
        high_rim,
        wide,
    ) = rest
    take_rims(keys, here, weights, 2 * size, cols, low_rim, high_rim)
    block_len = own.shape[0]
    start = RIM - KERNEL // 2
    assemble_pieces(here, list(zip(keys, weights)), w_full, 2, size)
    spread = spread_heads()
    for slot, source in enumerate((own, other)):
        rows = slice(slot * block_len, (slot + 1) * block_len)
        fill_wide(wide, slot, low_rim, source, high_rim)
        for block in range(wide.shape[2] // LANE):
            lanes = slice(block * LANE, (block + 1) * LANE)
            total = jnp.zeros((block_len, LANE), WIDE)
            for offset in range(KERNEL):
                piece = wide[slot, start + offset : start + offset + block_len, lanes]
                piece = jnp.where(same_doc(docs, slot, offset, block_len), piece, 0.0)
                total = total + piece * depth_gain[offset : offset + 1, lanes]
            depth_low[rows, lanes] = total.astype(LOW)
        left, right = half_pair(wide[slot].astype(LOW))
        value = (mm(left, w_full[0, 0], NT) + mm(right, w_full[0, 1], NT) + bias[2:3, :]).astype(LOW)
        value_wide[slot] = value.astype(WIDE)
        left, right = half_pair(depth_low[rows, :])
        key_here = mm(left, w_full[1, 0], NT) + mm(right, w_full[1, 1], NT) + bias[3:4, :]
        key_conv[rows, :] = key_here
        attn = (query[rows, :].astype(WIDE) * key_here).astype(LOW)
        conv_attn[rows, :] = attn
        conv_weights[rows, :] = mm(attn, tap_weight[...], NN) + tap_bias[...]
        top = jnp.full((block_len, LANE), MASKED, WIDE)
        for offset in range(KERNEL):
            lanes = slice(offset * LANE, (offset + 1) * LANE)
            top = jnp.maximum(
                top,
                jnp.where(
                    same_doc(docs, slot, offset, block_len), conv_weights[rows, lanes], MASKED
                ),
            )
        total = jnp.zeros((block_len, LANE), WIDE)
        for offset in range(KERNEL):
            lanes = slice(offset * LANE, (offset + 1) * LANE)
            mask = same_doc(docs, slot, offset, block_len)
            term = jnp.where(
                mask, jnp.exp(jnp.where(mask, conv_weights[rows, lanes], MASKED) - top), 0.0
            )
            conv_weights[rows, lanes] = term
            total = total + term
        scale = 1.0 / total
        mixed = jnp.zeros((block_len, ATT), WIDE)
        for offset in range(KERNEL):
            lanes = slice(offset * LANE, (offset + 1) * LANE)
            weight = conv_weights[rows, lanes] * scale
            conv_weights[rows, lanes] = weight
            wide_weight = mm(two(*split_low(weight)), spread, NN)
            mixed = mixed + wide_weight * value_wide[slot, start + offset : start + offset + block_len, :]
        context[rows, :] = mixed.astype(LOW)


def head_queries(values, head):
    lane = lax.broadcasted_iota(jnp.int32, values.shape, 1)
    return jnp.where(lane // HEAD == head, values, jnp.zeros_like(values))


def blocks_overlap(bounds, slot, block):
    return (bounds[block, 0] <= bounds[slot, 1]) & (bounds[block, 1] >= bounds[slot, 0])


def attend_kernel(count, index, bounds, query, doc_query, doc_key, *rest):
    stacks, rest = rest[:count], rest[count:]
    out, stats, scores, top, total, mixed = rest
    pair_lanes = slice(index * LANE, (index + 1) * LANE)
    tokens_here = query.shape[0]
    block_len = tokens_here // 2
    score_scale = HEAD ** (-0.5)
    for slot in range(2):
        rows = slice(slot * block_len, (slot + 1) * block_len)
        scaled = query[rows, pair_lanes] * jnp.asarray(score_scale, LOW)
        queries = [head_queries(scaled, head) for head in range(2)]
        doc_here = doc_query[slot : slot + 1, :]
        top[...] = jnp.full(top.shape, MASKED, WIDE)
        total[...] = jnp.zeros(total.shape, WIDE)
        mixed[...] = jnp.zeros(mixed.shape, WIDE)

        def each(body):
            for place, stack in enumerate(stacks):

                def one(step, carry):
                    block = place * 2 + step

                    @pl.when(blocks_overlap(bounds, slot, block))
                    def _():
                        keys = pl.ds(pl.multiple_of(step * block_len, 16), block_len)
                        body(stack, keys, block)

                    return carry

                lax.fori_loop(0, 2, one, 0)

        def first(stack, keys, block):
            key_rows = stack[keys, :LANE]
            doc_rows = doc_key[block]
            allowed = tile_lanes(doc_rows, block_len // LANE) == doc_here
            for head in range(2):
                score = jnp.where(allowed, mm(key_rows, queries[head], NT), MASKED)
                scores[block, head] = score
                top[head] = jnp.maximum(top[head], jnp.max(score, axis=0, keepdims=True))

        each(first)

        def second(stack, keys, block):
            value_rows = stack[keys, LANE:]
            for head in range(2):
                term = jnp.exp(scores[block, head] - top[head, 0:1, :])
                total[head] = total[head] + jnp.sum(term, axis=0, keepdims=True)
                mixed[head] = mixed[head] + mm(value_rows, term.astype(LOW), TN)

        each(second)
        parts = []
        for head in range(2):
            scale = 1.0 / total[head, 0:1, :]
            parts.append(mixed[head, head * HEAD : (head + 1) * HEAD, :] * scale)
            stats[slot, head : head + 1, :] = top[head, 0:1, :] + jnp.log(total[head, 0:1, :])
        out[rows, :] = jnp.concatenate(parts, axis=0).T.astype(LOW)


def attend_back_kernel(count, index, bounds, query, doc_query, doc_key, attended, grad, stats, *rest):
    stacks, rest = rest[:count], rest[count:]
    grad_query, grad_own, grad_far, bias_grad, delta, grad_kv = rest
    pair_lanes = slice(index * LANE, (index + 1) * LANE)
    tokens_here = query.shape[0]
    block_len = tokens_here // 2
    score_scale = HEAD ** (-0.5)
    head_row = lax.broadcasted_iota(jnp.int32, (8, LANE), 0)
    head_lane = lax.broadcasted_iota(jnp.int32, (8, LANE), 1) // HEAD
    chosen = jnp.where(head_row == head_lane, 1.0, 0.0).astype(LOW)
    for slot in range(2):
        rows = slice(slot * block_len, (slot + 1) * block_len)
        both = attended[rows, :].astype(WIDE) * grad[rows, :].astype(WIDE)
        high, low = split_low(both)
        delta[slot] = mm(chosen, high, NT) + mm(chosen, low, NT)
    grad_query[...] = jnp.zeros(grad_query.shape, WIDE)
    bias_grad[...] = jnp.zeros(bias_grad.shape, WIDE)

    for place, stack in enumerate(stacks):
        out = (grad_own, grad_far)[2 * place // count]
        entry = place % (count // 2)

        def one(step, carry):
            block = place * 2 + step
            keys = pl.ds(pl.multiple_of(step * block_len, 16), block_len)
            grad_kv[...] = jnp.zeros(grad_kv.shape, WIDE)
            for slot in range(2):

                @pl.when(blocks_overlap(bounds, slot, block))
                def _():
                    rows = slice(slot * block_len, (slot + 1) * block_len)
                    key_rows = stack[keys, :LANE]
                    value_rows = stack[keys, LANE:]
                    scaled = query[rows, pair_lanes] * jnp.asarray(score_scale, LOW)
                    allowed = tile_lanes(doc_key[block], block_len // LANE) == doc_query[slot : slot + 1, :]
                    for head in range(2):
                        query_here = head_queries(scaled, head)
                        grad_here = head_queries(grad[rows, :], head)
                        score = mm(key_rows, query_here, NT)
                        probs = jnp.where(
                            allowed, jnp.exp(score - stats[slot, head : head + 1, :]), 0.0
                        )
                        g_probs = mm(value_rows, grad_here, NT)
                        g_score = (probs * (g_probs - delta[slot, head : head + 1, :])).astype(LOW)
                        key_here = head_queries(key_rows, head)
                        grad_query[rows, :] += mm(g_score, key_here, TN)
                        grad_kv[:, :LANE] += mm(g_score, query_here, NN)
                        grad_kv[:, LANE:] += mm(probs.astype(LOW), grad_here, NN)

            bias_grad[1:2, :] += column_sum(grad_kv[:, LANE:])
            out[entry, keys, :] = grad_kv[...].astype(LOW)
            return carry

        lax.fori_loop(0, 2, one, 0)
    grad_query[...] = grad_query[...] * score_scale
    bias_grad[0:1, :] = column_sum(grad_query[...])


def norm_stats(values):
    mean = jnp.mean(values, axis=-1, keepdims=True)
    centred = values - mean
    spread = jnp.mean(centred * centred, axis=-1, keepdims=True)
    scale = lax.rsqrt(spread + EPSILON)
    return centred * scale, scale


def norm_back(normal, scale, grad):
    return scale * (
        grad
        - jnp.mean(grad, axis=-1, keepdims=True)
        - normal * jnp.mean(grad * normal, axis=-1, keepdims=True)
    )


def column_sum(values):
    return jnp.sum(values, axis=0, keepdims=True)


def middle_kernel(
    here,
    own,
    other,
    cot_pair,
    cot_other,
    att_0,
    att_1,
    att_2,
    conv_context,
    inner_own,
    inner_far,
    tail_own,
    tail_far,
    vectors,
    inner_bias,
    out_own,
    out_other,
    resid_grad,
    g_att_0,
    g_att_1,
    g_att_2,
    g_conv,
    d_inner_own,
    d_inner_far,
    d_tail_own,
    d_tail_far,
    vector_grads,
    inner_bias_grad,
    w_out,
    context,
    normal_1,
    scale_1,
    hidden_low,
    active,
    slope,
    ffn_sum,
    grad_2,
    ffn_grad,
    attn_grad,
    d_out,
):
    block_len = own.shape[0]
    tokens_here = 2 * block_len
    inner_size = inner_own.shape[1]
    out_size = tail_own.shape[1] - inner_size
    half_width = inner_own.shape[2]
    cols = inner_own.shape[0]
    assemble(here, (tail_own, tail_far), "col", w_out, 1, out_size, inner_size)
    bias_out, gain_1, shift_1 = vectors[0:1, :], vectors[1:2, :], vectors[2:3, :]
    bias_outer, gain_2, shift_2 = vectors[3:4, :], vectors[4:5, :], vectors[5:6, :]
    context[0] = jnp.concatenate([att_0[...], att_1[...], att_2[...]], axis=1)
    context[1] = conv_context[...]
    sources = ((own, cot_pair.at[here[0]], out_own), (other, cot_other, out_other))
    for slot, (source, _, _) in enumerate(sources):
        rows = slice(slot * block_len, (slot + 1) * block_len)
        attn = (
            mm(context[0, rows, :], w_out[0, 0], NT)
            + mm(context[1, rows, :], w_out[0, 1], NT)
            + bias_out
        )
        normal, scale = norm_stats(source[...].astype(WIDE) + attn)
        normal_1[rows, :] = normal
        scale_1[rows, :] = jnp.broadcast_to(scale, (block_len, LANE))
        hidden = normal * gain_1 + shift_1
        left, right = half_pair(hidden.astype(LOW))
        hidden_low[0, rows, :] = left
        hidden_low[1, rows, :] = right
    ffn_sum[...] = jnp.zeros(ffn_sum.shape, WIDE)

    def each(body):
        for core, (inner, tail) in enumerate(((inner_own, tail_own), (inner_far, tail_far))):

            def one(entry, carry):
                dr, dc = place_of(entry, "row")
                entry_tail = (entry % 2) * 2 + (entry // 2) % 2 + (entry // 4) * 4
                group = here[0] ^ dr
                spot = group * (2 * cols // 2) + (here[1] ^ (dc + core))
                body(core, entry, entry_tail, group, spot, inner, tail)
                return carry

            lax.fori_loop(0, cols, one, 0)

    def forward(core, entry, entry_tail, group, spot, inner, tail):
        for slot in range(2):
            rows = slice(slot * block_len, (slot + 1) * block_len)
            pre = mm(hidden_low[group, rows, :], inner[entry], NT) + inner_bias[spot]
            half = 0.5 * (1.0 + lax.erf(pre * (0.5**0.5)))
            low = (pre * half).astype(LOW)
            active[core * cols + entry, rows, :] = low
            slope[core * cols + entry, rows, :] = half + pre * jnp.exp(-0.5 * pre * pre) * (
                0.3989422804014327
            )
            ffn_sum[group, rows, :] += mm(low, tail[entry_tail, :inner_size, :], NN)

    each(forward)
    vector_grads[...] = jnp.zeros(vector_grads.shape, WIDE)
    for slot, (_, cot, out) in enumerate(sources):
        rows = slice(slot * block_len, (slot + 1) * block_len)
        hidden = normal_1[rows, :] * gain_1 + shift_1
        resid = hidden + (two(ffn_sum[0, rows, :], ffn_sum[1, rows, :]) + bias_outer)
        normal, scale = norm_stats(resid)
        out[...] = (normal * gain_2 + shift_2).astype(LOW)
        cot_wide = cot[...].astype(WIDE)
        vector_grads[0:1, :] += column_sum(cot_wide * normal)
        vector_grads[1:2, :] += column_sum(cot_wide)
        grad = norm_back(normal, scale, cot_wide * gain_2)
        grad_2[rows, :] = grad
        low = grad.astype(LOW)
        vector_grads[2:3, :] += column_sum(low.astype(WIDE))
        left, right = half_pair(low)
        ffn_grad[0, rows, :] = left
        ffn_grad[1, rows, :] = right
    ffn_sum[...] = jnp.zeros(ffn_sum.shape, WIDE)

    def backward(core, entry, entry_tail, group, spot, inner, tail):
        d_inner = (d_inner_own, d_inner_far)[core]
        d_tail = (d_tail_own, d_tail_far)[core]
        where = core * cols + entry
        lows = []
        for slot in range(2):
            rows = slice(slot * block_len, (slot + 1) * block_len)
            g_active = mm(ffn_grad[group, rows, :], tail[entry_tail, :inner_size, :], NT)
            low = (g_active * slope[where, rows, :]).astype(LOW)
            lows.append(low)
            ffn_sum[group, rows, :] += mm(low, inner[entry], NN)
        g_inner = jnp.concatenate(lows, axis=0)
        inner_bias_grad[spot] = column_sum(g_inner.astype(WIDE))
        d_inner[entry] = mm(g_inner, hidden_low[group], TN).astype(LOW)
        d_tail[entry_tail, :inner_size, :] = mm(active[where], ffn_grad[group], TN).astype(LOW)

    each(backward)
    for slot in range(2):
        rows = slice(slot * block_len, (slot + 1) * block_len)
        grad = grad_2[rows, :] + two(ffn_sum[0, rows, :], ffn_sum[1, rows, :])
        normal = normal_1[rows, :]
        vector_grads[3:4, :] += column_sum(grad * normal)
        vector_grads[4:5, :] += column_sum(grad)
        grad = norm_back(normal, scale_1[rows, 0:1], grad * gain_1)
        resid_grad[rows, :] = grad
        low = grad.astype(LOW)
        vector_grads[5:6, :] += column_sum(low.astype(WIDE))
        attn_grad[rows, :] = low
        g_att = mm(low, w_out[0, 0], NN).astype(LOW)
        for index, out in enumerate((g_att_0, g_att_1, g_att_2)):
            out[rows, :] = g_att[:, index * LANE : (index + 1) * LANE]
        g_conv[rows, :] = mm(low, w_out[0, 1], NN).astype(LOW)
    for half in range(2):
        d_out[0, half] = mm(attn_grad[...], context[half], TN).astype(LOW)
    cut(here, d_out, (d_tail_own, d_tail_far), "col", 1, out_size, inner_size)


def branch_back_kernel(
    own,
    other,
    low_rim,
    high_rim,
    docs,
    w_full,
    depth_gain,
    tap_weight,
    query,
    g_conv,
    value_wide,
    key_conv,
    conv_attn,
    conv_weights,
    g_key_conv,
    g_query,
    d_tap_weight,
    d_tap_bias,
    d_depth,
    bias_grad,
    g_ext_value,
    g_ext_tokens,
    first_rim,
    last_rim,
    wide,
    weight_grad,
    low_grad,
    tap_sum,
    tap_bias_sum,
):
    block_len = own.shape[0]
    start = RIM - KERNEL // 2
    spread = spread_heads()
    tap_sum[...] = jnp.zeros(tap_sum.shape, WIDE)
    tap_bias_sum[...] = jnp.zeros(tap_bias_sum.shape, WIDE)
    d_depth[...] = jnp.zeros(d_depth.shape, WIDE)
    bias_grad[...] = jnp.zeros(bias_grad.shape, WIDE)
    g_ext_value[...] = jnp.zeros(g_ext_value.shape, WIDE)
    g_ext_tokens[...] = jnp.zeros(g_ext_tokens.shape, WIDE)
    for slot, source in enumerate((own, other)):
        rows = slice(slot * block_len, (slot + 1) * block_len)
        fill_wide(wide, slot, low_rim, source, high_rim)
        grad = g_conv[rows, :].astype(WIDE)
        mean = jnp.zeros((block_len, LANE), WIDE)
        for offset in range(KERNEL):
            lanes = slice(offset * LANE, (offset + 1) * LANE)
            place = slice(start + offset, start + offset + block_len)
            high, low = split_low(grad * value_wide[slot, place, :])
            back = mm(high, spread[:LANE], NT) + mm(low, spread[:LANE], NT)
            weight_grad[:, lanes] = back
            mean = mean + conv_weights[rows, lanes] * back
        for offset in range(KERNEL):
            lanes = slice(offset * LANE, (offset + 1) * LANE)
            place = slice(start + offset, start + offset + block_len)
            weight = conv_weights[rows, lanes]
            low_grad[:, lanes] = (weight * (weight_grad[:, lanes] - mean)).astype(LOW)
            g_ext_value[slot, place, :] += mm(two(*split_low(weight)), spread, NN) * grad
        tap_sum[...] += mm(conv_attn[rows, :], low_grad[...], TN)
        tap_bias_sum[0:1, :] += column_sum(low_grad[...].astype(WIDE))
        g_attn = mm(low_grad[...], tap_weight[...], NT)
        g_key = (g_attn * query[rows, :].astype(WIDE)).astype(LOW)
        g_key_conv[rows, :] = g_key
        bias_grad[0:1, :] += column_sum(g_ext_value[slot])
        bias_grad[1:2, :] += column_sum(g_key.astype(WIDE))
        g_query[rows, :] = g_attn * key_conv[rows, :]
        bias_grad[2:3, :] += column_sum(g_query[rows, :])
        for half in range(2):
            g_depth = mm(g_key, w_full[1, half], NN)
            for block in range(g_depth.shape[1] // LANE):
                column = half * g_depth.shape[1] + block * LANE
                lanes = slice(column, column + LANE)
                piece = g_depth[:, block * LANE : (block + 1) * LANE]
                for offset in range(KERNEL):
                    place = slice(start + offset, start + offset + block_len)
                    masked = jnp.where(same_doc(docs, slot, offset, block_len), piece, 0.0)
                    d_depth[offset : offset + 1, lanes] += column_sum(masked * wide[slot, place, lanes])
                    g_ext_tokens[slot, place, lanes] += masked * depth_gain[offset : offset + 1, lanes]
        for rim, place in ((first_rim, slice(0, RIM)), (last_rim, slice(RIM + block_len, 2 * RIM + block_len))):
            rim[slot] = two(g_ext_value[slot, place, :], g_ext_tokens[slot, place, :]).astype(LOW)
    source = lax.broadcasted_iota(jnp.int32, (KERNEL * LANE, LANE), 0)
    target = lax.broadcasted_iota(jnp.int32, (KERNEL * LANE, LANE), 1)
    chosen = (source % LANE < HEADS) & (source % LANE * KERNEL + source // LANE == target)
    chosen = jnp.where(chosen, 1.0, 0.0).astype(LOW)
    high, low = split_low(tap_sum[...])
    d_tap_weight[...] = mm(chosen, high, NT_ROWS) + mm(chosen, low, NT_ROWS)
    high, low = split_low(tap_bias_sum[...])
    d_tap_bias[...] = mm(high, chosen, NN) + mm(low, chosen, NN)


def pack(out, grads):
    vector_grads, inner_bias_grad, d_depth, d_tap_weight, d_tap_bias, branch_bias, biases = grads
    width = out.shape[1]
    out[...] = jnp.zeros(out.shape, WIDE)
    row = 0
    for source, count in ((vector_grads, 6), (d_depth, KERNEL)):
        for index in range(count):
            for half in range(2):
                out[row : row + 1, :] = source[index : index + 1, half * width : (half + 1) * width]
                row += 1
    taps = HEADS * KERNEL
    out[row : row + taps, :] = d_tap_weight[0:taps, :]
    row += taps
    out[row : row + 1, :LANE] = d_tap_bias[0:1, :]
    query_bias = jnp.concatenate([grads[0:1, :] for grads in biases], axis=1)
    value_bias = jnp.concatenate([grads[1:2, :] for grads in biases], axis=1)
    out[row + 1 : row + 2, :] = query_bias + branch_bias[2:3, :]
    out[row + 2 : row + 3, :] = value_bias
    out[row + 3 : row + 5, :] = branch_bias[0:2, :]
    row += 5
    for index in range(inner_bias_grad.shape[0]):
        out[row : row + 1, : inner_bias_grad.shape[2]] = inner_bias_grad[index]
        row += 1


def branch_weights_kernel(
    here,
    own,
    other,
    w_full,
    depth_low,
    g_key_conv,
    g_ext_value,
    g_ext_tokens,
    after,
    before,
    resid_grad,
    vector_grads,
    inner_bias_grad,
    d_depth,
    d_tap_weight,
    d_tap_bias,
    branch_bias,
    bias_0,
    bias_1,
    bias_2,
    d_own,
    d_far,
    token_grad,
    packed,
    ext,
    d_full,
    tokens,
    value_grad,
    rows_wide,
):
    pack(
        rows_wide,
        (vector_grads, inner_bias_grad, d_depth, d_tap_weight, d_tap_bias, branch_bias, (bias_0, bias_1, bias_2)),
    )
    packed[...] = rows_wide[...].astype(LOW)
    block_len = own.shape[0]
    size = d_own.shape[1] // 2
    for slot, source in enumerate((own, other)):
        rows = slice(slot * block_len, (slot + 1) * block_len)
        tokens[rows, :] = source[...]
        for grads, lanes in ((g_ext_value, slice(0, ATT)), (g_ext_tokens, slice(ATT, ext.shape[1]))):
            ext[:, lanes] = grads[slot, RIM : RIM + block_len, :]
        ext[0:RIM, :] += before[slot].astype(WIDE)
        ext[block_len - RIM :, :] += after[slot].astype(WIDE)
        low = ext[:, :ATT].astype(LOW)
        value_grad[rows, :] = low
        token_grad[rows, :] = (
            resid_grad[rows, :]
            + ext[:, ATT:]
            + two(mm(low, w_full[0, 0], NN), mm(low, w_full[0, 1], NN))
        )
    for half in range(2):
        lanes = slice(half * d_own.shape[2], (half + 1) * d_own.shape[2])
        d_full[0, half] = mm(value_grad[...], tokens[:, lanes], TN).astype(LOW)
        d_full[1, half] = mm(g_key_conv[...], depth_low[:, lanes], TN).astype(LOW)
    cut(here, d_full, (d_own, d_far), "col", 2, size, 0)


def first_weights_kernel(
    here,
    own,
    other,
    grad_0,
    grad_1,
    grad_2,
    g_query,
    kept_0,
    moved_0,
    kept_1,
    moved_1,
    kept_2,
    moved_2,
    d_own,
    d_far,
    lows,
    d_full,
    tokens,
):
    block_len = own.shape[0]
    size = d_own.shape[1] // 3
    pairs = ((kept_0, moved_0), (kept_1, moved_1), (kept_2, moved_2))
    for slot, source in enumerate((own, other)):
        tokens[slot * block_len : (slot + 1) * block_len, :] = source[...]
    lows[0] = (
        jnp.concatenate([grad_0[...], grad_1[...], grad_2[...]], axis=1) + g_query[...]
    ).astype(LOW)
    for part in range(2):
        lows[1 + part] = jnp.concatenate(
            [
                add_low(kept[0, :, part * LANE : (part + 1) * LANE], moved[0, :, part * LANE : (part + 1) * LANE])
                for kept, moved in pairs
            ],
            axis=1,
        )
    for part in range(3):
        for half in range(2):
            lanes = slice(half * d_own.shape[2], (half + 1) * d_own.shape[2])
            d_full[part, half] = mm(lows[part], tokens[:, lanes], TN).astype(LOW)
    cut(here, d_full, (d_own, d_far), "row", 3, size, 0)


def token_kernel(w_full, lows, token_in, token_own, token_other):
    block_len = token_own.shape[0]
    for slot, out in enumerate((token_own, token_other)):
        rows = slice(slot * block_len, (slot + 1) * block_len)
        total = token_in[rows, :]
        for part in range(3):
            low = lows[part, rows, :]
            total = total + two(mm(low, w_full[part, 0], NN), mm(low, w_full[part, 1], NN))
        out[...] = total.astype(out.dtype)


def local(
    tokens,
    cotangent,
    doc_ids,
    proj_weight,
    out_weight,
    inner_weight,
    outer_weight,
    depth_weight,
    proj_bias,
    kernel_weight,
    kernel_bias,
    out_bias,
    norm1_gain,
    norm1_shift,
    inner_bias,
    outer_bias,
    norm2_gain,
    norm2_shift,
):
    block_len = tokens.shape[1]
    model_width = tokens.shape[2]
    margin = KERNEL // 2
    col_count = lax.axis_size("col")
    row_count = lax.axis_size("row")
    row_here = lax.axis_index("row")
    col_here = lax.axis_index("col")
    here = jnp.stack([row_here, col_here]).astype(jnp.int32)
    tokens_here = 2 * block_len
    entries = col_count // 2 * row_count
    pair_entries = col_count // 2
    cut_proj = proj_weight.shape[2]
    cut_out = out_weight.shape[1]
    cut_inner = inner_weight.shape[2]
    lanes = proj_weight.shape[1]

    far_steps = [step for step in steps_of("col") if step > 1]

    proj_t = jnp.transpose(proj_weight, (0, 2, 1))
    doc_slab = jnp.pad(
        doc_ids[:, 0].astype(LOW), ((0, DOC_ROWS - doc_ids.shape[0]), (0, lanes - block_len))
    )
    first = {(0, 0): jnp.concatenate([proj_t[:3].reshape(-1, lanes), doc_slab], axis=0)}

    def spread_row(held):
        for dr, dc in list(held):
            held[(1, dc)] = swap(held[(dr, dc)], "row", 1)

    def spread_col(held, step):
        for dr, dc in list(held):
            held[(dr, dc ^ step)] = swap(held[(dr, dc)], "col", step)

    def trade(pair, *marks):
        sent = pick(pair, 1 - row_here)
        if marks:
            sent = after(sent, *marks)
        return pick(pair, row_here), swap(sent, "row", 1)

    spread_row(first)
    first_row = first[(1, 0)]
    for step in far_steps:
        spread_col(first, step)
    own, other = trade(tokens, first_row)
    for dr, dc in list(first):
        first[(dr, dc ^ 1)] = swap(first[(dr, dc)], "col", 1)
    edges = jnp.concatenate([own[block_len - RIM :], other[block_len - RIM :], own[:RIM], other[:RIM]], axis=0)
    branch_parts = [proj_t[3:].reshape(-1, lanes), edges[:, :lanes], edges[:, lanes:]]
    inner = inner_weight[0].T
    branch_low = after(jnp.concatenate(branch_parts, axis=0), first[(1, far_steps[-1])])
    branch_rows = branch_low.shape[0]
    branch = {(0, 0): branch_low}
    for step in far_steps:
        spread_col(branch, step)
    sent = {key: value for key, value in branch.items() if key != (0, 0)}
    branch[(1, 0)] = swap(jnp.concatenate([branch_low, inner], axis=0), "row", 1)
    spread_row(sent)
    branch.update(sent)
    inner_moved = branch[(1, 0)][branch_rows:][None]
    inner = inner[None]
    for dr, dc in list(branch):
        branch[(dr, dc ^ 1)] = swap(branch[(dr, dc)], "col", 1)

    def wrapped(block, step):
        moved = shift(block, "col", step)
        edge = 0 if step > 0 else col_count - 1
        return jnp.where(col_here == edge, moved[::-1], moved)

    tail = grow(
        after(
            jnp.concatenate([outer_weight[0], out_weight.T], axis=0), branch[(0, far_steps[-1])]
        )[None],
        "col",
        far_steps[0],
    )

    wide_bias = proj_bias.astype(WIDE)
    tap_weight = jnp.pad(
        kernel_weight.reshape(ATT, HEADS, KERNEL).transpose(0, 2, 1),
        ((0, 0), (0, 0), (0, LANE - HEADS)),
    ).reshape(ATT, KERNEL * LANE)
    tap_bias = (
        jnp.pad(kernel_bias.reshape(HEADS, KERNEL).T, ((0, 0), (0, LANE - HEADS)))
        .reshape(1, KERNEL * LANE)
        .astype(WIDE)
    )
    depth_gain = jnp.pad(depth_weight.astype(WIDE), ((0, 16 - KERNEL), (0, 0)))
    vectors = jnp.stack(
        [out_bias, norm1_gain, norm1_shift, outer_bias, norm2_gain, norm2_shift, norm2_shift, norm2_shift]
    ).astype(WIDE)

    first_keys = sorted(first, key=lambda key: (key[1] & 1, key[1], key[0]))
    query, pairs, w_first = kernel_call(
        functools.partial(project_kernel, first_keys),
        [
            ((tokens_here, ATT), LOW),
            ((tokens_here, 2 * ATT), LOW),
            ((3, row_count, ATT, lanes), LOW),
        ],
        cost=0.05,
    )(here, own, other, wide_bias, *[first[key] for key in first_keys])

    gathered = [pairs]
    for step in far_steps:
        gathered = gathered + [swap(piece, "col", step) for piece in gathered]
    tail = after(tail, query)
    tail_moved = swap(tail, "row", 1)

    doc_blocks = jnp.stack(
        [
            lax.dynamic_slice(first[key], (3 * cut_proj + row_here, 0), (1, block_len))[0]
            for key in first_keys
        ]
    ).astype(jnp.int32)
    bounds = jnp.stack([doc_blocks[:, 0], doc_blocks[:, -1]], axis=1)
    doc_key = jnp.broadcast_to(doc_blocks[:, :, None], doc_blocks.shape + (LANE,))

    def doc_rim(slot, step):
        position = (row_here ^ slot) * col_count + col_here + step
        inside = (position >= 0) & (position < row_count * col_count)
        position = jnp.clip(position, 0, row_count * col_count - 1)
        dr = (position // col_count) ^ row_here
        dc = (position % col_count) ^ col_here
        return jnp.where(inside, pick(doc_blocks, (dc % 2) * entries + (dc // 2) * 2 + dr), -1)

    doc_ext = jnp.stack(
        [
            jnp.concatenate(
                [doc_rim(slot, -1)[block_len - RIM :], doc_blocks[slot], doc_rim(slot, 1)[:RIM]]
            )
            for slot in range(2)
        ]
    )
    doc_rows = jnp.broadcast_to(doc_ext[:, :, None], doc_ext.shape + (LANE,))

    ext_len = block_len + 2 * RIM
    branch_keys = list(branch)
    conv_context, depth_low, value_wide, key_conv, conv_attn, conv_weights, w_branch, low_rim, high_rim = kernel_call(
        functools.partial(branch_kernel, branch_keys, cut_proj, col_count),
        [
            ((tokens_here, ATT), LOW),
            ((tokens_here, model_width), LOW),
            ((2, ext_len, ATT), WIDE),
            ((tokens_here, ATT), WIDE),
            ((tokens_here, ATT), LOW),
            ((tokens_here, KERNEL * LANE), WIDE),
            ((2, row_count, ATT, lanes), LOW),
            ((2, RIM, model_width), LOW),
            ((2, RIM, model_width), LOW),
        ],
        [((2, ext_len, model_width), WIDE)],
        cost=11,
    )(
        here,
        own,
        other,
        doc_rows,
        depth_gain,
        wide_bias,
        tap_weight,
        tap_bias,
        query,
        *[branch[key] for key in branch_keys],
    )

    gathered.append(swap(pairs, "col", 1))
    for piece in gathered[1 : col_count // 2]:
        gathered.append(swap(after(piece, conv_context), "col", 1))
    inner = jnp.concatenate([inner, after(inner_moved, conv_context)], axis=0)
    for step in far_steps[:-1]:
        inner = grow(inner, "col", step)
    inner_far_moved = swap(inner, "col", far_steps[-1])
    _, cot_other = trade(cotangent, conv_context)

    doc_query = doc_blocks[:2]
    attended = []
    stats = []
    for index in range(PAIRS):
        out, stat = kernel_call(
            functools.partial(attend_kernel, col_count, index),
            [((tokens_here, LANE), LOW), ((2, 8, block_len), WIDE)],
            [
                ((2 * col_count, 2, block_len, block_len), WIDE),
                ((2, 1, block_len), WIDE),
                ((2, 1, block_len), WIDE),
                ((2, LANE, block_len), WIDE),
            ],
            cost=8,
            parts=col_count,
            part=index,
        )(bounds, after(query, conv_context), doc_query, doc_key, *gathered)
        attended.append(out)
        stats.append(stat)

    tail = jnp.concatenate([tail, after(tail_moved, conv_context)], axis=0)
    for step in far_steps[1:]:
        tail = grow(tail, "col", step)
    inner = jnp.concatenate([inner, after(inner_far_moved, attended[0])], axis=0)
    inner_own, inner_far = inner, swap(inner, "col", 1)
    tail_own, tail_far = tail, swap(tail, "col", 1)

    (
        out_own,
        out_other,
        resid_grad,
        *g_att,
        g_conv,
        d_inner_own,
        d_inner_far,
        d_tail_own,
        d_tail_far,
        vector_grads,
        inner_bias_grad,
    ) = kernel_call(
        middle_kernel,
        [
            ((block_len, model_width), LOW),
            ((block_len, model_width), LOW),
            ((tokens_here, model_width), WIDE),
        ]
        + [((tokens_here, LANE), LOW)] * PAIRS
        + [((tokens_here, ATT), LOW)]
        + [((entries, cut_inner, lanes), LOW)] * 2
        + [((entries, cut_inner + cut_out, lanes), LOW)] * 2
        + [((8, model_width), WIDE), ((2 * entries, 1, cut_inner), WIDE)],
        [
            ((1, row_count, model_width, lanes), LOW),
            ((row_count, tokens_here, lanes), LOW),
            ((tokens_here, model_width), WIDE),
            ((tokens_here, LANE), WIDE),
            ((row_count, tokens_here, lanes), LOW),
            ((2 * entries, tokens_here, cut_inner), LOW),
            ((2 * entries, tokens_here, cut_inner), WIDE),
            ((row_count, tokens_here, lanes), WIDE),
            ((tokens_here, model_width), WIDE),
            ((row_count, tokens_here, lanes), LOW),
            ((tokens_here, model_width), LOW),
            ((1, row_count, model_width, lanes), LOW),
        ],
        cost=30,
    )(
        here,
        own,
        other,
        cotangent,
        cot_other,
        *attended,
        conv_context,
        inner_own,
        inner_far,
        tail_own,
        tail_far,
        vectors,
        inner_bias.astype(WIDE).reshape(2 * entries, 1, cut_inner),
    )

    row_stages = [("row", 1)] + [("col", step) for step in far_steps]
    col_stages = [("col", far_steps[0]), ("row", 1)] + [("col", step) for step in far_steps[1:]]
    row_stages.reverse()
    col_stages.reverse()

    class GridSum:
        def __init__(self, kept, sent, stages):
            self.kept = kept
            self.moved = swap(sent, "col", 1)
            self.todo = list(stages)

        def finish(self, *marks):
            moved = after(self.moved, *marks) if marks else self.moved
            if not self.todo:
                self.kept = add_low(self.kept, moved)
                return self.kept
            self.kept, sent = join(self.kept, moved)
            axis, step = self.todo.pop(0)
            self.moved = swap(sent, axis, step)
            return sent

        def rest(self, *marks):
            while self.todo:
                self.finish(*marks)
            return self.finish(*marks)[0]

        def terms(self, *marks):
            while self.todo:
                self.finish(*marks)
            return self.kept, self.moved

    inner_sum = GridSum(d_inner_own, d_inner_far, row_stages)
    tail_sum = GridSum(d_tail_own, d_tail_far, col_stages)
    query_grads = []
    bias_grads = []
    pair_sums = []

    def attend_back(index, *marks):
        grad_query, grad_own, grad_far, bias_grad = kernel_call(
            functools.partial(attend_back_kernel, col_count, index),
            [
                ((tokens_here, LANE), WIDE),
                ((pair_entries, tokens_here, 2 * LANE), LOW),
                ((pair_entries, tokens_here, 2 * LANE), LOW),
                ((8, LANE), WIDE),
            ],
            [((2, 8, block_len), WIDE), ((block_len, 2 * LANE), WIDE)],
            cost=13,
            parts=col_count,
            part=index,
        )(
            bounds,
            after(query, *marks) if marks else query,
            doc_query,
            doc_key,
            attended[index],
            g_att[index],
            stats[index],
            *gathered,
        )
        query_grads.append(grad_query)
        bias_grads.append(bias_grad)
        pair_sums.append(GridSum(grad_own, grad_far, [("col", step) for step in reversed(far_steps)]))
        return grad_query

    done = attend_back(0)
    marks = [inner_sum.finish(done), tail_sum.finish(done)]
    (
        g_key_conv,
        g_query,
        d_tap_weight,
        d_tap_bias,
        d_depth,
        branch_bias,
        g_ext_value,
        g_ext_tokens,
        first_rim,
        last_rim,
    ) = kernel_call(
        branch_back_kernel,
        [
            ((tokens_here, ATT), LOW),
            ((tokens_here, ATT), WIDE),
            ((LANE, ATT), WIDE),
            ((8, LANE), WIDE),
            ((16, model_width), WIDE),
            ((8, ATT), WIDE),
            ((2, ext_len, ATT), WIDE),
            ((2, ext_len, model_width), WIDE),
            ((2, RIM, ATT + model_width), LOW),
            ((2, RIM, ATT + model_width), LOW),
        ],
        [
            ((2, ext_len, model_width), WIDE),
            ((block_len, KERNEL * LANE), WIDE),
            ((block_len, KERNEL * LANE), LOW),
            ((ATT, KERNEL * LANE), WIDE),
            ((8, KERNEL * LANE), WIDE),
        ],
        smem=0,
        cost=16,
    )(
        own,
        other,
        low_rim,
        high_rim,
        doc_rows,
        w_branch,
        depth_gain,
        tap_weight,
        query,
        after(g_conv, *marks),
        value_wide,
        key_conv,
        conv_attn,
        conv_weights,
    )
    marks = [pair_sums[0].finish(g_query), inner_sum.finish(g_query), tail_sum.finish(g_query)]
    done = attend_back(1, *marks)
    from_after = wrapped(after(first_rim, done), -1)
    from_before = wrapped(after(last_rim, done), 1)
    wide_part = jnp.concatenate([inner_sum.rest(done), tail_sum.rest(done)], axis=0)
    wide_sum = DataSum(wide_part)
    done = attend_back(2, wide_part, pair_sums[1].finish())
    marks = [pair_sums[2].finish(), wide_sum.finish(done)]
    inner_rows = inner_bias_grad.shape[0]
    packed_rows = 2 * (6 + KERNEL) + HEADS * KERNEL + 5 + inner_rows
    packed_rows += -packed_rows % 16
    d_branch_own, d_branch_far, token_grad, packed = kernel_call(
        branch_weights_kernel,
        [((entries, 2 * cut_proj, lanes), LOW)] * 2
        + [((tokens_here, model_width), WIDE), ((packed_rows, lanes), LOW)],
        [
            ((block_len, ATT + model_width), WIDE),
            ((2, row_count, ATT, lanes), LOW),
            ((tokens_here, model_width), LOW),
            ((tokens_here, ATT), LOW),
            ((packed_rows, lanes), WIDE),
        ],
        cost=6,
    )(
        here,
        own,
        other,
        w_branch,
        depth_low,
        after(g_key_conv, done, *marks),
        g_ext_value,
        g_ext_tokens,
        from_after,
        from_before,
        resid_grad,
        vector_grads,
        inner_bias_grad,
        d_depth,
        d_tap_weight,
        d_tap_bias,
        branch_bias,
        *bias_grads,
    )
    flat_sum = FlatSum(packed)
    branch_sum = GridSum(d_branch_own, d_branch_far, col_stages)
    terms = [term for pair in pair_sums for term in pair.terms(token_grad)]
    wide_stage = wide_sum.finish(token_grad)
    d_first_own, d_first_far, lows = kernel_call(
        first_weights_kernel,
        [((entries, 3 * cut_proj, lanes), LOW)] * 2
        + [((3, tokens_here, ATT), LOW)],
        [((3, row_count, ATT, lanes), LOW), ((tokens_here, model_width), LOW)],
        cost=0.05,
    )(here, own, other, *query_grads, after(g_query, wide_stage), *terms)
    first_sum = GridSum(d_first_own, d_first_far, row_stages)

    flat_stage = flat_sum.finish(lows)
    branch_stage = branch_sum.finish(lows)
    first_stage = first_sum.finish()
    token_own, token_other = kernel_call(
        token_kernel,
        [((block_len, model_width), WIDE), ((block_len, model_width), LOW)],
        smem=0,
        cost=0.05,
    )(w_first, lows, after(token_grad, first_stage, branch_stage, flat_stage))
    first_stage = first_sum.finish(token_own)
    branch_stage = branch_sum.finish(token_own)
    wide_stage = wide_sum.finish(token_own)
    flat_sum.finish(first_stage, branch_stage, wide_stage)
    token_other = after(token_other, first_stage)
    first_part = first_sum.rest()
    branch_part = branch_sum.rest(first_stage)
    proj_sum = DataSum(jnp.concatenate([first_part, branch_part], axis=0))
    while len(flat_sum.todo) > 1:
        flat_sum.finish(first_part)
    proj_stage = proj_sum.finish()
    wide_sum = wide_sum.rest(proj_stage).astype(WIDE)
    flat_sum.finish(proj_stage)
    proj_stage = proj_sum.finish()
    proj_sum = proj_sum.rest().astype(WIDE)
    flat = flat_sum.low.astype(WIDE)
    finals = []
    start = 0
    for count in (12, 2 * KERNEL, HEADS * KERNEL, 1, 4, inner_rows):
        finals.append(flat[start : start + count])
        start += count
    vector_sum, depth_sum, tap_weight_sum, tap_bias_sum, bias_sum, inner_bias_sum = finals
    vector_sum = vector_sum.reshape(6, -1)

    def give_back(here_rows, there_rows, *marks):
        moved = swap(there_rows, "row", 1).astype(here_rows.dtype)
        if marks:
            moved = after(moved, *marks)
        return jnp.where(
            row_here == 0, jnp.stack([here_rows, moved]), jnp.stack([moved, here_rows])
        )

    return (
        give_back(out_own, out_other, first_stage),
        give_back(token_own, token_other, proj_stage),
        jnp.transpose(proj_sum.reshape(5, cut_proj, lanes), (0, 2, 1)),
        wide_sum[2 * cut_inner :].T,
        wide_sum[:cut_inner].T[None],
        wide_sum[cut_inner : 2 * cut_inner][None],
        depth_sum.reshape(KERNEL, -1),
        bias_sum,
        tap_weight_sum.T,
        tap_bias_sum[0, : HEADS * KERNEL],
        vector_sum[5],
        vector_sum[3],
        vector_sum[4],
        inner_bias_sum[:, :cut_inner].reshape(-1),
        vector_sum[2],
        vector_sum[0],
        vector_sum[1],
    )


def solution(mesh):
    return jax.shard_map(
        local,
        mesh=mesh,
        in_specs=(
            P(None, ("dp", "row", "col"), None),
            P(None, ("dp", "row", "col"), None),
            P(None, "dp", ("row", "col")),
            P(None, "row", "col"),
            P("row", "col"),
            P("row", None, "col"),
            P("row", "col", None),
        )
        + (P(),) * 11,
        out_specs=(
            P(None, ("dp", "row", "col"), None),
            P(None, ("dp", "row", "col"), None),
            P(None, "row", "col"),
            P("row", "col"),
            P("row", None, "col"),
            P("row", "col", None),
        )
        + (P(),) * 11,
        check_vma=False,
    )
```

```python
import functools

import jax
import jax.numpy as jnp
from jax import lax
from jax.experimental import pallas as pl
from jax.experimental.pallas import tpu as pltpu
from jax.sharding import PartitionSpec as P

HEADS = 6
HEAD = 64
KERNEL = 9
FF = 3072
ATT = 384
PAIRS = HEADS // 2
LANE = 128
RIM = 8
DOC_ROWS = 16

EPSILON = 1e-12
MASKED = -1e30
LOW = jnp.bfloat16
WIDE = jnp.float32


def swap(block, axis, step):
    count = lax.axis_size(axis)
    return lax.ppermute(block, axis, [(i, i ^ step) for i in range(count)])


def shift(block, axis, step):
    count = lax.axis_size(axis)
    return lax.ppermute(block, axis, [(i, (i + step) % count) for i in range(count)])


def steps_of(axis):
    steps = []
    step = 1
    while step < lax.axis_size(axis):
        steps.append(step)
        step *= 2
    return steps


def pick(block, index):
    return lax.dynamic_index_in_dim(block, index, 0, keepdims=False)


NT = (((1,), (1,)), ((), ()))
NN = (((1,), (0,)), ((), ()))
TN = (((0,), (0,)), ((), ()))
NT_ROWS = (((0,), (1,)), ((), ()))


def mm(left, right, how):
    return lax.dot_general(left, right, how, preferred_element_type=WIDE)


def kernel_call(body, outs, scratch=(), smem=1, cost=5, parts=0, part=0):
    def run(*args):
        specs = [
            pl.BlockSpec(memory_space=pltpu.SMEM if place < smem else pltpu.VMEM)
            for place in range(len(args) - parts)
        ]
        specs += [
            pl.BlockSpec((arg.shape[0], 2 * LANE), lambda step: (0, part)) for arg in args[len(args) - parts :]
        ]
        return pl.pallas_call(
            body,
            grid=(1,),
            in_specs=specs,
            out_specs=[pl.BlockSpec(memory_space=pltpu.VMEM)] * len(outs),
            out_shape=[jax.ShapeDtypeStruct(shape, kind) for shape, kind in outs],
            scratch_shapes=[pltpu.VMEM(shape, kind) for shape, kind in scratch],
            cost_estimate=pl.CostEstimate(
                flops=int(cost * 1e9), bytes_accessed=int(cost * 3.6e6), transcendentals=0
            ),
        )(*args)

    return run


def place_of(entry, kind):
    if kind == "col":
        entry = (entry & 1) * 2 + (entry // 2) % 2 + (entry // 4) * 4
    return entry % 2, (entry // 2) * 2


def stages_of(kind):
    far = [("col", step) for step in steps_of("col") if step > 1]
    row = [("row", 1)]
    return row + far if kind == "row" else far[:1] + row + far[1:]


def after(value, *marks):
    return lax.optimization_barrier((value,) + marks)[0]


def grow(stack, axis, step):
    return jnp.concatenate([stack, swap(stack, axis, step)], axis=0)


def add_low(kept, moved):
    return (kept.astype(WIDE) + moved.astype(WIDE)).astype(LOW)


def join(kept, moved):
    half = kept.shape[0] // 2
    return add_low(kept[:half], moved[:half]), add_low(kept[half:], moved[half:])


class DataSum:
    def __init__(self, part):
        self.index = lax.axis_index("dp")
        steps = steps_of("dp")
        self.todo = [(True, step) for step in steps] + [(False, step) for step in reversed(steps)]
        self.part = part
        self.start()

    def start(self):
        down, step = self.todo[0]
        self.bit = (self.index // step) % 2
        if down:
            self.halves = self.part.reshape((2, self.part.shape[0] // 2) + self.part.shape[1:])
            self.moved = swap(pick(self.halves, 1 - self.bit), "dp", step)
        else:
            self.moved = swap(self.part, "dp", step)

    def finish(self, *marks):
        moved = after(self.moved, *marks) if marks else self.moved
        down, _ = self.todo.pop(0)
        if down:
            self.part = add_low(pick(self.halves, self.bit), moved)
        else:
            self.part = jnp.where(
                self.bit == 0,
                jnp.concatenate([self.part, moved], axis=0),
                jnp.concatenate([moved, self.part], axis=0),
            )
        if self.todo:
            self.start()
        return self.part

    def rest(self, *marks):
        while self.todo:
            self.finish(*marks)
        return self.part


class FlatSum:
    def __init__(self, flat):
        self.todo = [("col", 1), ("row", 1)] + [("col", step) for step in steps_of("col") if step > 1]
        self.todo += [("dp", step) for step in steps_of("dp")]
        self.low = flat
        self.start()

    def start(self):
        self.moved = swap(self.low, *self.todo[0])

    def finish(self, *marks):
        moved = after(self.moved, *marks) if marks else self.moved
        self.todo.pop(0)
        self.low = add_low(self.low, moved)
        if self.todo:
            self.start()
        return self.low


def assemble_pieces(here, pieces, full, parts, size):
    for (dr, dc), piece in pieces:
        row = here[0] ^ dr
        col = here[1] ^ dc
        for part in range(parts):
            full[part, row, pl.ds(pl.multiple_of(col * size, 16), size), :] = piece[
                part * size : (part + 1) * size, :
            ]


def assemble(here, stacks, kind, full, parts, size, start):
    for core, stack in enumerate(stacks):

        def one(entry, carry):
            dr, dc = place_of(entry, kind)
            row = here[0] ^ dr
            col = here[1] ^ (dc + core)
            for part in range(parts):
                full[part, row, pl.ds(pl.multiple_of(col * size, 16), size), :] = stack[
                    entry, start + part * size : start + (part + 1) * size, :
                ]
            return carry

        lax.fori_loop(0, stack.shape[0], one, 0)


def cut(here, full, outs, kind, parts, size, start):
    for core, out in enumerate(outs):

        def one(entry, carry):
            dr, dc = place_of(entry, kind)
            row = here[0] ^ dr
            col = here[1] ^ (dc + core)
            for part in range(parts):
                out[entry, start + part * size : start + (part + 1) * size, :] = full[
                    part, row, pl.ds(pl.multiple_of(col * size, 16), size), :
                ]
            return carry

        lax.fori_loop(0, out.shape[0], one, 0)


def two(left, right):
    return jnp.concatenate([left, right], axis=1)


def half_pair(value):
    return value[:, : value.shape[1] // 2], value[:, value.shape[1] // 2 :]


def project_kernel(keys, here, own, other, bias, *rest):
    weights, rest = rest[: len(keys)], rest[len(keys) :]
    query, pairs, w_full = rest
    size = (weights[0].shape[0] - DOC_ROWS) // 3
    block_len = own.shape[0]
    assemble_pieces(here, list(zip(keys, weights)), w_full, 3, size)
    for slot, source in enumerate((own, other)):
        left, right = half_pair(source[...])
        rows = pl.ds(slot * block_len, block_len)

        def product(part):
            return mm(left, w_full[part, 0], NT) + mm(right, w_full[part, 1], NT)

        query[rows, :] = (product(0) + bias[0:1, :]).astype(LOW)
        key_low = product(1).astype(LOW)
        value_low = (product(2) + bias[1:2, :]).astype(LOW)
        for index in range(PAIRS):
            lanes = slice(index * LANE, (index + 1) * LANE)
            pairs[rows, 2 * index * LANE : 2 * (index + 1) * LANE] = two(key_low[:, lanes], value_low[:, lanes])


def tile_lanes(mask, times):
    return jnp.concatenate([mask] * times, axis=1)


def split_low(values):
    high = values.astype(LOW)
    return high, (values - high.astype(WIDE)).astype(LOW)


def fill_wide(wide, slot, low_rim, source, high_rim):
    block_len = source.shape[0]
    wide[slot, 0:RIM, :] = low_rim[slot].astype(WIDE)
    wide[slot, RIM : RIM + block_len, :] = source[...].astype(WIDE)
    wide[slot, RIM + block_len : RIM + block_len + RIM, :] = high_rim[slot].astype(WIDE)


def same_doc(docs, slot, offset, block_len):
    start = RIM - KERNEL // 2 + offset
    return docs[slot, start : start + block_len, :] == docs[slot, RIM : RIM + block_len, :]


def spread_heads():
    head = lax.broadcasted_iota(jnp.int32, (2 * LANE, ATT), 0) % LANE
    lane = lax.broadcasted_iota(jnp.int32, (2 * LANE, ATT), 1)
    return jnp.where(lane // HEAD == head, 1.0, 0.0).astype(LOW)


def take_rims(keys, here, pieces, start, cols, low_rim, high_rim):
    for rims, step, edge, first in ((low_rim, -1, 0, 0), (high_rim, 1, cols - 1, 2 * RIM)):
        source = here[1] ^ ((here[1] + step + cols) % cols)
        turn = jnp.where(here[1] == edge, 1, 0)
        for (dr, dc), piece in zip(keys, pieces):
            if dr == 0 and dc > 0:

                @pl.when(source == dc)
                def _():
                    rows = piece[start : start + 8 * RIM, :].astype(WIDE)
                    for slot in range(2):
                        place = first + slot * RIM
                        left = rows[place : place + RIM, :]
                        right = rows[4 * RIM + place : 4 * RIM + place + RIM, :]
                        rims[slot ^ turn] = two(left, right).astype(LOW)


def branch_kernel(
    keys, size, cols, here, own, other, docs, depth_gain, bias, tap_weight, tap_bias, query, *rest
):
    weights, rest = rest[: len(keys)], rest[len(keys) :]
    (
        context,
        depth_low,
        value_wide,
        key_conv,
        conv_attn,
        conv_weights,
        w_full,
        low_rim,
        high_rim,
        wide,
    ) = rest
    take_rims(keys, here, weights, 2 * size, cols, low_rim, high_rim)
    block_len = own.shape[0]
    start = RIM - KERNEL // 2
    assemble_pieces(here, list(zip(keys, weights)), w_full, 2, size)
    spread = spread_heads()
    for slot, source in enumerate((own, other)):
        rows = slice(slot * block_len, (slot + 1) * block_len)
        fill_wide(wide, slot, low_rim, source, high_rim)
        for block in range(wide.shape[2] // LANE):
            lanes = slice(block * LANE, (block + 1) * LANE)
            total = jnp.zeros((block_len, LANE), WIDE)
            for offset in range(KERNEL):
                piece = wide[slot, start + offset : start + offset + block_len, lanes]
                piece = jnp.where(same_doc(docs, slot, offset, block_len), piece, 0.0)
                total = total + piece * depth_gain[offset : offset + 1, lanes]
            depth_low[rows, lanes] = total.astype(LOW)
        left, right = half_pair(wide[slot].astype(LOW))
        value = (mm(left, w_full[0, 0], NT) + mm(right, w_full[0, 1], NT) + bias[2:3, :]).astype(LOW)
        value_wide[slot] = value.astype(WIDE)
        left, right = half_pair(depth_low[rows, :])
        key_here = mm(left, w_full[1, 0], NT) + mm(right, w_full[1, 1], NT) + bias[3:4, :]
        key_conv[rows, :] = key_here
        attn = (query[rows, :].astype(WIDE) * key_here).astype(LOW)
        conv_attn[rows, :] = attn
        conv_weights[rows, :] = mm(attn, tap_weight[...], NN) + tap_bias[...]
        top = jnp.full((block_len, LANE), MASKED, WIDE)
        for offset in range(KERNEL):
            lanes = slice(offset * LANE, (offset + 1) * LANE)
            top = jnp.maximum(
                top,
                jnp.where(
                    same_doc(docs, slot, offset, block_len), conv_weights[rows, lanes], MASKED
                ),
            )
        total = jnp.zeros((block_len, LANE), WIDE)
        for offset in range(KERNEL):
            lanes = slice(offset * LANE, (offset + 1) * LANE)
            mask = same_doc(docs, slot, offset, block_len)
            term = jnp.where(
                mask, jnp.exp(jnp.where(mask, conv_weights[rows, lanes], MASKED) - top), 0.0
            )
            conv_weights[rows, lanes] = term
            total = total + term
        scale = 1.0 / total
        mixed = jnp.zeros((block_len, ATT), WIDE)
        for offset in range(KERNEL):
            lanes = slice(offset * LANE, (offset + 1) * LANE)
            weight = conv_weights[rows, lanes] * scale
            conv_weights[rows, lanes] = weight
            wide_weight = mm(two(*split_low(weight)), spread, NN)
            mixed = mixed + wide_weight * value_wide[slot, start + offset : start + offset + block_len, :]
        context[rows, :] = mixed.astype(LOW)


def head_queries(values, head):
    lane = lax.broadcasted_iota(jnp.int32, values.shape, 1)
    return jnp.where(lane // HEAD == head, values, jnp.zeros_like(values))


def blocks_overlap(bounds, slot, block):
    return (bounds[block, 0] <= bounds[slot, 1]) & (bounds[block, 1] >= bounds[slot, 0])


def attend_kernel(count, index, bounds, query, doc_query, doc_key, *rest):
    stacks, rest = rest[:count], rest[count:]
    out, stats, scores, top, total, mixed = rest
    pair_lanes = slice(index * LANE, (index + 1) * LANE)
    tokens_here = query.shape[0]
    block_len = tokens_here // 2
    score_scale = HEAD ** (-0.5)
    for slot in range(2):
        rows = slice(slot * block_len, (slot + 1) * block_len)
        scaled = query[rows, pair_lanes] * jnp.asarray(score_scale, LOW)
        queries = [head_queries(scaled, head) for head in range(2)]
        doc_here = doc_query[slot : slot + 1, :]
        top[...] = jnp.full(top.shape, MASKED, WIDE)
        total[...] = jnp.zeros(total.shape, WIDE)
        mixed[...] = jnp.zeros(mixed.shape, WIDE)

        def each(body):
            for place, stack in enumerate(stacks):

                def one(step, carry):
                    block = place * 2 + step

                    @pl.when(blocks_overlap(bounds, slot, block))
                    def _():
                        keys = pl.ds(pl.multiple_of(step * block_len, 16), block_len)
                        body(stack, keys, block)

                    return carry

                lax.fori_loop(0, 2, one, 0)

        def first(stack, keys, block):
            key_rows = stack[keys, :LANE]
            doc_rows = doc_key[block]
            allowed = tile_lanes(doc_rows, block_len // LANE) == doc_here
            for head in range(2):
                score = jnp.where(allowed, mm(key_rows, queries[head], NT), MASKED)
                scores[block, head] = score
                top[head] = jnp.maximum(top[head], jnp.max(score, axis=0, keepdims=True))

        each(first)

        def second(stack, keys, block):
            value_rows = stack[keys, LANE:]
            for head in range(2):
                term = jnp.exp(scores[block, head] - top[head, 0:1, :])
                total[head] = total[head] + jnp.sum(term, axis=0, keepdims=True)
                mixed[head] = mixed[head] + mm(value_rows, term.astype(LOW), TN)

        each(second)
        parts = []
        for head in range(2):
            scale = 1.0 / total[head, 0:1, :]
            parts.append(mixed[head, head * HEAD : (head + 1) * HEAD, :] * scale)
            stats[slot, head : head + 1, :] = top[head, 0:1, :] + jnp.log(total[head, 0:1, :])
        out[rows, :] = jnp.concatenate(parts, axis=0).T.astype(LOW)


def attend_back_kernel(count, index, bounds, query, doc_query, doc_key, attended, grad, stats, *rest):
    stacks, rest = rest[:count], rest[count:]
    grad_query, grad_own, grad_far, bias_grad, delta, grad_kv = rest
    pair_lanes = slice(index * LANE, (index + 1) * LANE)
    tokens_here = query.shape[0]
    block_len = tokens_here // 2
    score_scale = HEAD ** (-0.5)
    head_row = lax.broadcasted_iota(jnp.int32, (8, LANE), 0)
    head_lane = lax.broadcasted_iota(jnp.int32, (8, LANE), 1) // HEAD
    chosen = jnp.where(head_row == head_lane, 1.0, 0.0).astype(LOW)
    for slot in range(2):
        rows = slice(slot * block_len, (slot + 1) * block_len)
        both = attended[rows, :].astype(WIDE) * grad[rows, :].astype(WIDE)
        high, low = split_low(both)
        delta[slot] = mm(chosen, high, NT) + mm(chosen, low, NT)
    grad_query[...] = jnp.zeros(grad_query.shape, WIDE)
    bias_grad[...] = jnp.zeros(bias_grad.shape, WIDE)

    for place, stack in enumerate(stacks):
        out = (grad_own, grad_far)[2 * place // count]
        entry = place % (count // 2)

        def one(step, carry):
            block = place * 2 + step
            keys = pl.ds(pl.multiple_of(step * block_len, 16), block_len)
            grad_kv[...] = jnp.zeros(grad_kv.shape, WIDE)
            for slot in range(2):

                @pl.when(blocks_overlap(bounds, slot, block))
                def _():
                    rows = slice(slot * block_len, (slot + 1) * block_len)
                    key_rows = stack[keys, :LANE]
                    value_rows = stack[keys, LANE:]
                    scaled = query[rows, pair_lanes] * jnp.asarray(score_scale, LOW)
                    allowed = tile_lanes(doc_key[block], block_len // LANE) == doc_query[slot : slot + 1, :]
                    for head in range(2):
                        query_here = head_queries(scaled, head)
                        grad_here = head_queries(grad[rows, :], head)
                        score = mm(key_rows, query_here, NT)
                        probs = jnp.where(
                            allowed, jnp.exp(score - stats[slot, head : head + 1, :]), 0.0
                        )
                        g_probs = mm(value_rows, grad_here, NT)
                        g_score = (probs * (g_probs - delta[slot, head : head + 1, :])).astype(LOW)
                        key_here = head_queries(key_rows, head)
                        grad_query[rows, :] += mm(g_score, key_here, TN)
                        grad_kv[:, :LANE] += mm(g_score, query_here, NN)
                        grad_kv[:, LANE:] += mm(probs.astype(LOW), grad_here, NN)

            bias_grad[1:2, :] += column_sum(grad_kv[:, LANE:])
            out[entry, keys, :] = grad_kv[...].astype(LOW)
            return carry

        lax.fori_loop(0, 2, one, 0)
    grad_query[...] = grad_query[...] * score_scale
    bias_grad[0:1, :] = column_sum(grad_query[...])


def norm_stats(values):
    mean = jnp.mean(values, axis=-1, keepdims=True)
    centred = values - mean
    spread = jnp.mean(centred * centred, axis=-1, keepdims=True)
    scale = lax.rsqrt(spread + EPSILON)
    return centred * scale, scale


def norm_back(normal, scale, grad):
    return scale * (
        grad
        - jnp.mean(grad, axis=-1, keepdims=True)
        - normal * jnp.mean(grad * normal, axis=-1, keepdims=True)
    )


def column_sum(values):
    return jnp.sum(values, axis=0, keepdims=True)


def middle_kernel(
    here,
    own,
    other,
    cot_pair,
    cot_other,
    att_0,
    att_1,
    att_2,
    conv_context,
    inner_own,
    inner_far,
    tail_own,
    tail_far,
    vectors,
    inner_bias,
    out_own,
    out_other,
    resid_grad,
    g_att_0,
    g_att_1,
    g_att_2,
    g_conv,
    d_inner_own,
    d_inner_far,
    d_tail_own,
    d_tail_far,
    vector_grads,
    inner_bias_grad,
    w_out,
    context,
    normal_1,
    scale_1,
    hidden_low,
    active,
    slope,
    ffn_sum,
    grad_2,
    ffn_grad,
    attn_grad,
    d_out,
):
    block_len = own.shape[0]
    tokens_here = 2 * block_len
    inner_size = inner_own.shape[1]
    out_size = tail_own.shape[1] - inner_size
    half_width = inner_own.shape[2]
    cols = inner_own.shape[0]
    assemble(here, (tail_own, tail_far), "col", w_out, 1, out_size, inner_size)
    bias_out, gain_1, shift_1 = vectors[0:1, :], vectors[1:2, :], vectors[2:3, :]
    bias_outer, gain_2, shift_2 = vectors[3:4, :], vectors[4:5, :], vectors[5:6, :]
    context[0] = jnp.concatenate([att_0[...], att_1[...], att_2[...]], axis=1)
    context[1] = conv_context[...]
    sources = ((own, cot_pair.at[here[0]], out_own), (other, cot_other, out_other))
    for slot, (source, _, _) in enumerate(sources):
        rows = slice(slot * block_len, (slot + 1) * block_len)
        attn = (
            mm(context[0, rows, :], w_out[0, 0], NT)
            + mm(context[1, rows, :], w_out[0, 1], NT)
            + bias_out
        )
        normal, scale = norm_stats(source[...].astype(WIDE) + attn)
        normal_1[rows, :] = normal
        scale_1[rows, :] = jnp.broadcast_to(scale, (block_len, LANE))
        hidden = normal * gain_1 + shift_1
        left, right = half_pair(hidden.astype(LOW))
        hidden_low[0, rows, :] = left
        hidden_low[1, rows, :] = right
    ffn_sum[...] = jnp.zeros(ffn_sum.shape, WIDE)

    def each(body):
        for core, (inner, tail) in enumerate(((inner_own, tail_own), (inner_far, tail_far))):

            def one(entry, carry):
                dr, dc = place_of(entry, "row")
                entry_tail = (entry % 2) * 2 + (entry // 2) % 2 + (entry // 4) * 4
                group = here[0] ^ dr
                spot = group * (2 * cols // 2) + (here[1] ^ (dc + core))
                body(core, entry, entry_tail, group, spot, inner, tail)
                return carry

            lax.fori_loop(0, cols, one, 0)

    def forward(core, entry, entry_tail, group, spot, inner, tail):
        for slot in range(2):
            rows = slice(slot * block_len, (slot + 1) * block_len)
            pre = mm(hidden_low[group, rows, :], inner[entry], NT) + inner_bias[spot]
            half = 0.5 * (1.0 + lax.erf(pre * (0.5**0.5)))
            low = (pre * half).astype(LOW)
            active[core * cols + entry, rows, :] = low
            slope[core * cols + entry, rows, :] = half + pre * jnp.exp(-0.5 * pre * pre) * (
                0.3989422804014327
            )
            ffn_sum[group, rows, :] += mm(low, tail[entry_tail, :inner_size, :], NN)

    each(forward)
    vector_grads[...] = jnp.zeros(vector_grads.shape, WIDE)
    for slot, (_, cot, out) in enumerate(sources):
        rows = slice(slot * block_len, (slot + 1) * block_len)
        hidden = normal_1[rows, :] * gain_1 + shift_1
        resid = hidden + (two(ffn_sum[0, rows, :], ffn_sum[1, rows, :]) + bias_outer)
        normal, scale = norm_stats(resid)
        out[...] = (normal * gain_2 + shift_2).astype(LOW)
        cot_wide = cot[...].astype(WIDE)
        vector_grads[0:1, :] += column_sum(cot_wide * normal)
        vector_grads[1:2, :] += column_sum(cot_wide)
        grad = norm_back(normal, scale, cot_wide * gain_2)
        grad_2[rows, :] = grad
        low = grad.astype(LOW)
        vector_grads[2:3, :] += column_sum(low.astype(WIDE))
        left, right = half_pair(low)
        ffn_grad[0, rows, :] = left
        ffn_grad[1, rows, :] = right
    ffn_sum[...] = jnp.zeros(ffn_sum.shape, WIDE)

    def backward(core, entry, entry_tail, group, spot, inner, tail):
        d_inner = (d_inner_own, d_inner_far)[core]
        d_tail = (d_tail_own, d_tail_far)[core]
        where = core * cols + entry
        lows = []
        for slot in range(2):
            rows = slice(slot * block_len, (slot + 1) * block_len)
            g_active = mm(ffn_grad[group, rows, :], tail[entry_tail, :inner_size, :], NT)
            low = (g_active * slope[where, rows, :]).astype(LOW)
            lows.append(low)
            ffn_sum[group, rows, :] += mm(low, inner[entry], NN)
        g_inner = jnp.concatenate(lows, axis=0)
        inner_bias_grad[spot] = column_sum(g_inner.astype(WIDE))
        d_inner[entry] = mm(g_inner, hidden_low[group], TN).astype(LOW)
        d_tail[entry_tail, :inner_size, :] = mm(active[where], ffn_grad[group], TN).astype(LOW)

    each(backward)
    for slot in range(2):
        rows = slice(slot * block_len, (slot + 1) * block_len)
        grad = grad_2[rows, :] + two(ffn_sum[0, rows, :], ffn_sum[1, rows, :])
        normal = normal_1[rows, :]
        vector_grads[3:4, :] += column_sum(grad * normal)
        vector_grads[4:5, :] += column_sum(grad)
        grad = norm_back(normal, scale_1[rows, 0:1], grad * gain_1)
        resid_grad[rows, :] = grad
        low = grad.astype(LOW)
        vector_grads[5:6, :] += column_sum(low.astype(WIDE))
        attn_grad[rows, :] = low
        g_att = mm(low, w_out[0, 0], NN).astype(LOW)
        for index, out in enumerate((g_att_0, g_att_1, g_att_2)):
            out[rows, :] = g_att[:, index * LANE : (index + 1) * LANE]
        g_conv[rows, :] = mm(low, w_out[0, 1], NN).astype(LOW)
    for half in range(2):
        d_out[0, half] = mm(attn_grad[...], context[half], TN).astype(LOW)
    cut(here, d_out, (d_tail_own, d_tail_far), "col", 1, out_size, inner_size)


def branch_back_kernel(
    own,
    other,
    low_rim,
    high_rim,
    docs,
    w_full,
    depth_gain,
    tap_weight,
    query,
    g_conv,
    value_wide,
    key_conv,
    conv_attn,
    conv_weights,
    g_key_conv,
    g_query,
    d_tap_weight,
    d_tap_bias,
    d_depth,
    bias_grad,
    g_ext_value,
    g_ext_tokens,
    first_rim,
    last_rim,
    wide,
    weight_grad,
    low_grad,
    tap_sum,
    tap_bias_sum,
):
    block_len = own.shape[0]
    start = RIM - KERNEL // 2
    spread = spread_heads()
    tap_sum[...] = jnp.zeros(tap_sum.shape, WIDE)
    tap_bias_sum[...] = jnp.zeros(tap_bias_sum.shape, WIDE)
    d_depth[...] = jnp.zeros(d_depth.shape, WIDE)
    bias_grad[...] = jnp.zeros(bias_grad.shape, WIDE)
    g_ext_value[...] = jnp.zeros(g_ext_value.shape, WIDE)
    g_ext_tokens[...] = jnp.zeros(g_ext_tokens.shape, WIDE)
    for slot, source in enumerate((own, other)):
        rows = slice(slot * block_len, (slot + 1) * block_len)
        fill_wide(wide, slot, low_rim, source, high_rim)
        grad = g_conv[rows, :].astype(WIDE)
        mean = jnp.zeros((block_len, LANE), WIDE)
        for offset in range(KERNEL):
            lanes = slice(offset * LANE, (offset + 1) * LANE)
            place = slice(start + offset, start + offset + block_len)
            high, low = split_low(grad * value_wide[slot, place, :])
            back = mm(high, spread[:LANE], NT) + mm(low, spread[:LANE], NT)
            weight_grad[:, lanes] = back
            mean = mean + conv_weights[rows, lanes] * back
        for offset in range(KERNEL):
            lanes = slice(offset * LANE, (offset + 1) * LANE)
            place = slice(start + offset, start + offset + block_len)
            weight = conv_weights[rows, lanes]
            low_grad[:, lanes] = (weight * (weight_grad[:, lanes] - mean)).astype(LOW)
            g_ext_value[slot, place, :] += mm(two(*split_low(weight)), spread, NN) * grad
        tap_sum[...] += mm(conv_attn[rows, :], low_grad[...], TN)
        tap_bias_sum[0:1, :] += column_sum(low_grad[...].astype(WIDE))
        g_attn = mm(low_grad[...], tap_weight[...], NT)
        g_key = (g_attn * query[rows, :].astype(WIDE)).astype(LOW)
        g_key_conv[rows, :] = g_key
        bias_grad[0:1, :] += column_sum(g_ext_value[slot])
        bias_grad[1:2, :] += column_sum(g_key.astype(WIDE))
        g_query[rows, :] = g_attn * key_conv[rows, :]
        bias_grad[2:3, :] += column_sum(g_query[rows, :])
        for half in range(2):
            g_depth = mm(g_key, w_full[1, half], NN)
            for block in range(g_depth.shape[1] // LANE):
                column = half * g_depth.shape[1] + block * LANE
                lanes = slice(column, column + LANE)
                piece = g_depth[:, block * LANE : (block + 1) * LANE]
                for offset in range(KERNEL):
                    place = slice(start + offset, start + offset + block_len)
                    masked = jnp.where(same_doc(docs, slot, offset, block_len), piece, 0.0)
                    d_depth[offset : offset + 1, lanes] += column_sum(masked * wide[slot, place, lanes])
                    g_ext_tokens[slot, place, lanes] += masked * depth_gain[offset : offset + 1, lanes]
        for rim, place in ((first_rim, slice(0, RIM)), (last_rim, slice(RIM + block_len, 2 * RIM + block_len))):
            rim[slot] = two(g_ext_value[slot, place, :], g_ext_tokens[slot, place, :]).astype(LOW)
    source = lax.broadcasted_iota(jnp.int32, (KERNEL * LANE, LANE), 0)
    target = lax.broadcasted_iota(jnp.int32, (KERNEL * LANE, LANE), 1)
    chosen = (source % LANE < HEADS) & (source % LANE * KERNEL + source // LANE == target)
    chosen = jnp.where(chosen, 1.0, 0.0).astype(LOW)
    high, low = split_low(tap_sum[...])
    d_tap_weight[...] = mm(chosen, high, NT_ROWS) + mm(chosen, low, NT_ROWS)
    high, low = split_low(tap_bias_sum[...])
    d_tap_bias[...] = mm(high, chosen, NN) + mm(low, chosen, NN)


def pack(out, grads):
    vector_grads, inner_bias_grad, d_depth, d_tap_weight, d_tap_bias, branch_bias, biases = grads
    width = out.shape[1]
    out[...] = jnp.zeros(out.shape, WIDE)
    row = 0
    for source, count in ((vector_grads, 6), (d_depth, KERNEL)):
        for index in range(count):
            for half in range(2):
                out[row : row + 1, :] = source[index : index + 1, half * width : (half + 1) * width]
                row += 1
    taps = HEADS * KERNEL
    out[row : row + taps, :] = d_tap_weight[0:taps, :]
    row += taps
    out[row : row + 1, :LANE] = d_tap_bias[0:1, :]
    query_bias = jnp.concatenate([grads[0:1, :] for grads in biases], axis=1)
    value_bias = jnp.concatenate([grads[1:2, :] for grads in biases], axis=1)
    out[row + 1 : row + 2, :] = query_bias + branch_bias[2:3, :]
    out[row + 2 : row + 3, :] = value_bias
    out[row + 3 : row + 5, :] = branch_bias[0:2, :]
    row += 5
    for index in range(inner_bias_grad.shape[0]):
        out[row : row + 1, : inner_bias_grad.shape[2]] = inner_bias_grad[index]
        row += 1


def branch_weights_kernel(
    here,
    own,
    other,
    w_full,
    depth_low,
    g_key_conv,
    g_ext_value,
    g_ext_tokens,
    after,
    before,
    resid_grad,
    vector_grads,
    inner_bias_grad,
    d_depth,
    d_tap_weight,
    d_tap_bias,
    branch_bias,
    bias_0,
    bias_1,
    bias_2,
    d_own,
    d_far,
    token_grad,
    packed,
    ext,
    d_full,
    tokens,
    value_grad,
    rows_wide,
):
    pack(
        rows_wide,
        (vector_grads, inner_bias_grad, d_depth, d_tap_weight, d_tap_bias, branch_bias, (bias_0, bias_1, bias_2)),
    )
    packed[...] = rows_wide[...].astype(LOW)
    block_len = own.shape[0]
    size = d_own.shape[1] // 2
    for slot, source in enumerate((own, other)):
        rows = slice(slot * block_len, (slot + 1) * block_len)
        tokens[rows, :] = source[...]
        for grads, lanes in ((g_ext_value, slice(0, ATT)), (g_ext_tokens, slice(ATT, ext.shape[1]))):
            ext[:, lanes] = grads[slot, RIM : RIM + block_len, :]
        ext[0:RIM, :] += before[slot].astype(WIDE)
        ext[block_len - RIM :, :] += after[slot].astype(WIDE)
        low = ext[:, :ATT].astype(LOW)
        value_grad[rows, :] = low
        token_grad[rows, :] = (
            resid_grad[rows, :]
            + ext[:, ATT:]
            + two(mm(low, w_full[0, 0], NN), mm(low, w_full[0, 1], NN))
        )
    for half in range(2):
        lanes = slice(half * d_own.shape[2], (half + 1) * d_own.shape[2])
        d_full[0, half] = mm(value_grad[...], tokens[:, lanes], TN).astype(LOW)
        d_full[1, half] = mm(g_key_conv[...], depth_low[:, lanes], TN).astype(LOW)
    cut(here, d_full, (d_own, d_far), "col", 2, size, 0)


def first_weights_kernel(
    here,
    own,
    other,
    grad_0,
    grad_1,
    grad_2,
    g_query,
    kept_0,
    moved_0,
    kept_1,
    moved_1,
    kept_2,
    moved_2,
    d_own,
    d_far,
    lows,
    d_full,
    tokens,
):
    block_len = own.shape[0]
    size = d_own.shape[1] // 3
    pairs = ((kept_0, moved_0), (kept_1, moved_1), (kept_2, moved_2))
    for slot, source in enumerate((own, other)):
        tokens[slot * block_len : (slot + 1) * block_len, :] = source[...]
    lows[0] = (
        jnp.concatenate([grad_0[...], grad_1[...], grad_2[...]], axis=1) + g_query[...]
    ).astype(LOW)
    for part in range(2):
        lows[1 + part] = jnp.concatenate(
            [
                add_low(kept[0, :, part * LANE : (part + 1) * LANE], moved[0, :, part * LANE : (part + 1) * LANE])
                for kept, moved in pairs
            ],
            axis=1,
        )
    for part in range(3):
        for half in range(2):
            lanes = slice(half * d_own.shape[2], (half + 1) * d_own.shape[2])
            d_full[part, half] = mm(lows[part], tokens[:, lanes], TN).astype(LOW)
    cut(here, d_full, (d_own, d_far), "row", 3, size, 0)


def token_kernel(w_full, lows, token_in, token_own, token_other):
    block_len = token_own.shape[0]
    for slot, out in enumerate((token_own, token_other)):
        rows = slice(slot * block_len, (slot + 1) * block_len)
        total = token_in[rows, :]
        for part in range(3):
            low = lows[part, rows, :]
            total = total + two(mm(low, w_full[part, 0], NN), mm(low, w_full[part, 1], NN))
        out[...] = total.astype(out.dtype)


def local(
    tokens,
    cotangent,
    doc_ids,
    proj_weight,
    out_weight,
    inner_weight,
    outer_weight,
    depth_weight,
    proj_bias,
    kernel_weight,
    kernel_bias,
    out_bias,
    norm1_gain,
    norm1_shift,
    inner_bias,
    outer_bias,
    norm2_gain,
    norm2_shift,
):
    block_len = tokens.shape[1]
    model_width = tokens.shape[2]
    margin = KERNEL // 2
    col_count = lax.axis_size("col")
    row_count = lax.axis_size("row")
    row_here = lax.axis_index("row")
    col_here = lax.axis_index("col")
    here = jnp.stack([row_here, col_here]).astype(jnp.int32)
    tokens_here = 2 * block_len
    entries = col_count // 2 * row_count
    pair_entries = col_count // 2
    cut_proj = proj_weight.shape[2]
    cut_out = out_weight.shape[1]
    cut_inner = inner_weight.shape[2]
    lanes = proj_weight.shape[1]

    far_steps = [step for step in steps_of("col") if step > 1]

    proj_t = jnp.transpose(proj_weight, (0, 2, 1))
    doc_slab = jnp.pad(
        doc_ids[:, 0].astype(LOW), ((0, DOC_ROWS - doc_ids.shape[0]), (0, lanes - block_len))
    )
    first = {(0, 0): jnp.concatenate([proj_t[:3].reshape(-1, lanes), doc_slab], axis=0)}

    def spread_row(held):
        for dr, dc in list(held):
            held[(1, dc)] = swap(held[(dr, dc)], "row", 1)

    def spread_col(held, step):
        for dr, dc in list(held):
            held[(dr, dc ^ step)] = swap(held[(dr, dc)], "col", step)

    def trade(pair, mark):
        sent = after(pick(pair, 1 - row_here), mark)
        return pick(pair, row_here), swap(sent, "row", 1)

    spread_row(first)
    first_row = first[(1, 0)]
    for step in far_steps:
        spread_col(first, step)
    own, other = trade(tokens, first_row)
    for dr, dc in list(first):
        first[(dr, dc ^ 1)] = swap(first[(dr, dc)], "col", 1)
    edges = jnp.concatenate([own[block_len - RIM :], other[block_len - RIM :], own[:RIM], other[:RIM]], axis=0)
    branch_parts = [proj_t[3:].reshape(-1, lanes), edges[:, :lanes], edges[:, lanes:]]
    inner = inner_weight[0].T
    branch_low = after(jnp.concatenate(branch_parts, axis=0), first[(1, far_steps[-1])])
    branch_rows = branch_low.shape[0]
    branch = {(0, 0): branch_low}
    for step in far_steps:
        spread_col(branch, step)
    sent = {key: value for key, value in branch.items() if key != (0, 0)}
    branch[(1, 0)] = swap(jnp.concatenate([branch_low, inner], axis=0), "row", 1)
    spread_row(sent)
    branch.update(sent)
    inner_moved = branch[(1, 0)][branch_rows:][None]
    inner = inner[None]
    for dr, dc in list(branch):
        branch[(dr, dc ^ 1)] = swap(branch[(dr, dc)], "col", 1)

    def wrapped(block, step):
        moved = shift(block, "col", step)
        edge = 0 if step > 0 else col_count - 1
        return jnp.where(col_here == edge, moved[::-1], moved)

    tail = grow(
        after(
            jnp.concatenate([outer_weight[0], out_weight.T], axis=0), branch[(0, far_steps[-1])]
        )[None],
        "col",
        far_steps[0],
    )

    wide_bias = proj_bias.astype(WIDE)
    tap_weight = jnp.pad(
        kernel_weight.reshape(ATT, HEADS, KERNEL).transpose(0, 2, 1),
        ((0, 0), (0, 0), (0, LANE - HEADS)),
    ).reshape(ATT, KERNEL * LANE)
    tap_bias = (
        jnp.pad(kernel_bias.reshape(HEADS, KERNEL).T, ((0, 0), (0, LANE - HEADS)))
        .reshape(1, KERNEL * LANE)
        .astype(WIDE)
    )
    depth_gain = jnp.pad(depth_weight.astype(WIDE), ((0, 16 - KERNEL), (0, 0)))
    vectors = jnp.stack(
        [out_bias, norm1_gain, norm1_shift, outer_bias, norm2_gain, norm2_shift, norm2_shift, norm2_shift]
    ).astype(WIDE)

    first_keys = sorted(first, key=lambda key: (key[1] & 1, key[1], key[0]))
    query, pairs, w_first = kernel_call(
        functools.partial(project_kernel, first_keys),
        [
            ((tokens_here, ATT), LOW),
            ((tokens_here, 2 * ATT), LOW),
            ((3, row_count, ATT, lanes), LOW),
        ],
        cost=0.05,
    )(here, own, other, wide_bias, *[first[key] for key in first_keys])

    gathered = [pairs]
    for step in far_steps:
        gathered = gathered + [swap(piece, "col", step) for piece in gathered]
    tail = after(tail, query)
    tail_moved = swap(tail, "row", 1)

    doc_blocks = jnp.stack(
        [
            lax.dynamic_slice(first[key], (3 * cut_proj + row_here, 0), (1, block_len))[0]
            for key in first_keys
        ]
    ).astype(jnp.int32)
    bounds = jnp.stack([doc_blocks[:, 0], doc_blocks[:, -1]], axis=1)
    doc_key = jnp.broadcast_to(doc_blocks[:, :, None], doc_blocks.shape + (LANE,))

    def doc_rim(slot, step):
        position = (row_here ^ slot) * col_count + col_here + step
        inside = (position >= 0) & (position < row_count * col_count)
        position = jnp.clip(position, 0, row_count * col_count - 1)
        dr = (position // col_count) ^ row_here
        dc = (position % col_count) ^ col_here
        return jnp.where(inside, pick(doc_blocks, (dc % 2) * entries + (dc // 2) * 2 + dr), -1)

    doc_ext = jnp.stack(
        [
            jnp.concatenate(
                [doc_rim(slot, -1)[block_len - RIM :], doc_blocks[slot], doc_rim(slot, 1)[:RIM]]
            )
            for slot in range(2)
        ]
    )
    doc_rows = jnp.broadcast_to(doc_ext[:, :, None], doc_ext.shape + (LANE,))

    ext_len = block_len + 2 * RIM
    branch_keys = list(branch)
    conv_context, depth_low, value_wide, key_conv, conv_attn, conv_weights, w_branch, low_rim, high_rim = kernel_call(
        functools.partial(branch_kernel, branch_keys, cut_proj, col_count),
        [
            ((tokens_here, ATT), LOW),
            ((tokens_here, model_width), LOW),
            ((2, ext_len, ATT), WIDE),
            ((tokens_here, ATT), WIDE),
            ((tokens_here, ATT), LOW),
            ((tokens_here, KERNEL * LANE), WIDE),
            ((2, row_count, ATT, lanes), LOW),
            ((2, RIM, model_width), LOW),
            ((2, RIM, model_width), LOW),
        ],
        [((2, ext_len, model_width), WIDE)],
        cost=11,
    )(
        here,
        own,
        other,
        doc_rows,
        depth_gain,
        wide_bias,
        tap_weight,
        tap_bias,
        query,
        *[branch[key] for key in branch_keys],
    )

    gathered.append(swap(pairs, "col", 1))
    inner = jnp.concatenate([inner, after(inner_moved, conv_context)], axis=0)
    cot_sent = pick(cotangent, 1 - row_here)
    for piece in gathered[1 : col_count // 2]:
        gathered.append(swap(after(piece, conv_context, inner, cot_sent), "col", 1))
    for step in far_steps[:-1]:
        inner = grow(inner, "col", step)
    inner_far_moved = swap(inner, "col", far_steps[-1])
    cot_other = swap(after(cot_sent, conv_context), "row", 1)

    doc_query = doc_blocks[:2]
    attended = []
    stats = []
    for index in range(PAIRS):
        out, stat = kernel_call(
            functools.partial(attend_kernel, col_count, index),
            [((tokens_here, LANE), LOW), ((2, 8, block_len), WIDE)],
            [
                ((2 * col_count, 2, block_len, block_len), WIDE),
                ((2, 1, block_len), WIDE),
                ((2, 1, block_len), WIDE),
                ((2, LANE, block_len), WIDE),
            ],
            cost=8,
            parts=col_count,
            part=index,
        )(bounds, after(query, conv_context), doc_query, doc_key, *gathered)
        attended.append(out)
        stats.append(stat)

    tail = jnp.concatenate([tail, after(tail_moved, conv_context)], axis=0)
    for step in far_steps[1:]:
        tail = grow(tail, "col", step)
    inner = jnp.concatenate([inner, after(inner_far_moved, attended[0])], axis=0)
    inner_own, inner_far = inner, swap(inner, "col", 1)
    tail_own, tail_far = tail, swap(tail, "col", 1)

    (
        out_own,
        out_other,
        resid_grad,
        *g_att,
        g_conv,
        d_inner_own,
        d_inner_far,
        d_tail_own,
        d_tail_far,
        vector_grads,
        inner_bias_grad,
    ) = kernel_call(
        middle_kernel,
        [
            ((block_len, model_width), LOW),
            ((block_len, model_width), LOW),
            ((tokens_here, model_width), WIDE),
        ]
        + [((tokens_here, LANE), LOW)] * PAIRS
        + [((tokens_here, ATT), LOW)]
        + [((entries, cut_inner, lanes), LOW)] * 2
        + [((entries, cut_inner + cut_out, lanes), LOW)] * 2
        + [((8, model_width), WIDE), ((2 * entries, 1, cut_inner), WIDE)],
        [
            ((1, row_count, model_width, lanes), LOW),
            ((row_count, tokens_here, lanes), LOW),
            ((tokens_here, model_width), WIDE),
            ((tokens_here, LANE), WIDE),
            ((row_count, tokens_here, lanes), LOW),
            ((2 * entries, tokens_here, cut_inner), LOW),
            ((2 * entries, tokens_here, cut_inner), WIDE),
            ((row_count, tokens_here, lanes), WIDE),
            ((tokens_here, model_width), WIDE),
            ((row_count, tokens_here, lanes), LOW),
            ((tokens_here, model_width), LOW),
            ((1, row_count, model_width, lanes), LOW),
        ],
        cost=30,
    )(
        here,
        own,
        other,
        cotangent,
        cot_other,
        *attended,
        conv_context,
        inner_own,
        inner_far,
        tail_own,
        tail_far,
        vectors,
        inner_bias.astype(WIDE).reshape(2 * entries, 1, cut_inner),
    )

    row_stages = [("row", 1)] + [("col", step) for step in far_steps]
    col_stages = [("col", far_steps[0]), ("row", 1)] + [("col", step) for step in far_steps[1:]]
    row_stages.reverse()
    col_stages.reverse()

    class GridSum:
        def __init__(self, kept, sent, stages):
            self.kept = kept
            self.moved = swap(sent, "col", 1)
            self.todo = list(stages)

        def finish(self, *marks):
            moved = after(self.moved, *marks) if marks else self.moved
            if not self.todo:
                self.kept = add_low(self.kept, moved)
                return self.kept
            self.kept, sent = join(self.kept, moved)
            axis, step = self.todo.pop(0)
            self.moved = swap(sent, axis, step)
            return sent

        def rest(self, *marks):
            while self.todo:
                self.finish(*marks)
            return self.finish(*marks)[0]

        def terms(self, *marks):
            while self.todo:
                self.finish(*marks)
            return self.kept, self.moved

    inner_sum = GridSum(d_inner_own, d_inner_far, row_stages)
    tail_sum = GridSum(d_tail_own, d_tail_far, col_stages)
    query_grads = []
    bias_grads = []
    pair_sums = []

    def attend_back(index, *marks):
        grad_query, grad_own, grad_far, bias_grad = kernel_call(
            functools.partial(attend_back_kernel, col_count, index),
            [
                ((tokens_here, LANE), WIDE),
                ((pair_entries, tokens_here, 2 * LANE), LOW),
                ((pair_entries, tokens_here, 2 * LANE), LOW),
                ((8, LANE), WIDE),
            ],
            [((2, 8, block_len), WIDE), ((block_len, 2 * LANE), WIDE)],
            cost=13,
            parts=col_count,
            part=index,
        )(
            bounds,
            after(query, *marks) if marks else query,
            doc_query,
            doc_key,
            attended[index],
            g_att[index],
            stats[index],
            *gathered,
        )
        query_grads.append(grad_query)
        bias_grads.append(bias_grad)
        pair_sums.append(GridSum(grad_own, grad_far, [("col", step) for step in reversed(far_steps)]))
        return grad_query

    done = attend_back(0)
    marks = [inner_sum.finish(done), tail_sum.finish(done)]
    (
        g_key_conv,
        g_query,
        d_tap_weight,
        d_tap_bias,
        d_depth,
        branch_bias,
        g_ext_value,
        g_ext_tokens,
        first_rim,
        last_rim,
    ) = kernel_call(
        branch_back_kernel,
        [
            ((tokens_here, ATT), LOW),
            ((tokens_here, ATT), WIDE),
            ((LANE, ATT), WIDE),
            ((8, LANE), WIDE),
            ((16, model_width), WIDE),
            ((8, ATT), WIDE),
            ((2, ext_len, ATT), WIDE),
            ((2, ext_len, model_width), WIDE),
            ((2, RIM, ATT + model_width), LOW),
            ((2, RIM, ATT + model_width), LOW),
        ],
        [
            ((2, ext_len, model_width), WIDE),
            ((block_len, KERNEL * LANE), WIDE),
            ((block_len, KERNEL * LANE), LOW),
            ((ATT, KERNEL * LANE), WIDE),
            ((8, KERNEL * LANE), WIDE),
        ],
        smem=0,
        cost=16,
    )(
        own,
        other,
        low_rim,
        high_rim,
        doc_rows,
        w_branch,
        depth_gain,
        tap_weight,
        query,
        after(g_conv, *marks),
        value_wide,
        key_conv,
        conv_attn,
        conv_weights,
    )
    marks = [pair_sums[0].finish(g_query), inner_sum.finish(g_query), tail_sum.finish(g_query)]
    done = attend_back(1, *marks)
    from_after = wrapped(after(first_rim, done), -1)
    from_before = wrapped(after(last_rim, done), 1)
    wide_part = jnp.concatenate([inner_sum.rest(done), tail_sum.rest(done)], axis=0)
    wide_sum = DataSum(wide_part)
    done = attend_back(2, wide_part, pair_sums[1].finish())
    marks = [pair_sums[2].finish(), wide_sum.finish(done)]
    inner_rows = inner_bias_grad.shape[0]
    packed_rows = 2 * (6 + KERNEL) + HEADS * KERNEL + 5 + inner_rows
    packed_rows += -packed_rows % 16
    d_branch_own, d_branch_far, token_grad, packed = kernel_call(
        branch_weights_kernel,
        [((entries, 2 * cut_proj, lanes), LOW)] * 2
        + [((tokens_here, model_width), WIDE), ((packed_rows, lanes), LOW)],
        [
            ((block_len, ATT + model_width), WIDE),
            ((2, row_count, ATT, lanes), LOW),
            ((tokens_here, model_width), LOW),
            ((tokens_here, ATT), LOW),
            ((packed_rows, lanes), WIDE),
        ],
        cost=6,
    )(
        here,
        own,
        other,
        w_branch,
        depth_low,
        after(g_key_conv, done, *marks),
        g_ext_value,
        g_ext_tokens,
        from_after,
        from_before,
        resid_grad,
        vector_grads,
        inner_bias_grad,
        d_depth,
        d_tap_weight,
        d_tap_bias,
        branch_bias,
        *bias_grads,
    )
    flat_sum = FlatSum(packed)
    branch_sum = GridSum(d_branch_own, d_branch_far, col_stages)
    terms = [term for pair in pair_sums for term in pair.terms(token_grad)]
    wide_stage = wide_sum.finish(token_grad)
    d_first_own, d_first_far, lows = kernel_call(
        first_weights_kernel,
        [((entries, 3 * cut_proj, lanes), LOW)] * 2
        + [((3, tokens_here, ATT), LOW)],
        [((3, row_count, ATT, lanes), LOW), ((tokens_here, model_width), LOW)],
        cost=0.05,
    )(here, own, other, *query_grads, after(g_query, wide_stage), *terms)
    first_sum = GridSum(d_first_own, d_first_far, row_stages)

    flat_stage = flat_sum.finish(lows)
    branch_stage = branch_sum.finish(lows)
    first_stage = first_sum.finish()
    token_own, token_other = kernel_call(
        token_kernel,
        [((block_len, model_width), WIDE), ((block_len, model_width), LOW)],
        smem=0,
        cost=0.05,
    )(w_first, lows, after(token_grad, first_stage, branch_stage, flat_stage))
    first_stage = first_sum.finish(token_own)
    branch_stage = branch_sum.finish(token_own)
    wide_stage = wide_sum.finish(token_own)
    flat_sum.finish(first_stage, branch_stage, wide_stage)
    token_other = after(token_other, first_stage)
    first_part = first_sum.rest()
    branch_part = branch_sum.rest(first_stage)
    proj_sum = DataSum(jnp.concatenate([first_part, branch_part], axis=0))
    while len(flat_sum.todo) > 1:
        flat_sum.finish(first_part)
    proj_stage = proj_sum.finish()
    wide_sum = wide_sum.rest(proj_stage).astype(WIDE)
    flat_sum.finish(proj_stage)
    flat = flat_sum.low.astype(WIDE)
    finals = []
    start = 0
    for count in (12, 2 * KERNEL, HEADS * KERNEL, 1, 4, inner_rows):
        finals.append(flat[start : start + count])
        start += count
    vector_sum, depth_sum, tap_weight_sum, tap_bias_sum, bias_sum, inner_bias_sum = finals
    vector_sum = vector_sum.reshape(6, -1)
    vectors_out = [vector_sum[row] for row in (5, 3, 4)]
    vectors_out.append(inner_bias_sum[:, :cut_inner].reshape(-1))
    vectors_out += [vector_sum[row] for row in (2, 0, 1)]
    small_out = [
        depth_sum.reshape(KERNEL, -1),
        bias_sum,
        tap_weight_sum.T,
        tap_bias_sum[0, : HEADS * KERNEL],
    ]
    proj_stage = proj_sum.finish(*small_out)

    def give_back(here_rows, there_rows, *marks):
        moved = swap(there_rows, "row", 1).astype(here_rows.dtype)
        if marks:
            moved = after(moved, *marks)
        return jnp.where(
            row_here == 0, jnp.stack([here_rows, moved]), jnp.stack([moved, here_rows])
        )

    token_grad = give_back(token_own, token_other, proj_stage)
    wide_grads = (
        wide_sum[2 * cut_inner :].T,
        wide_sum[:cut_inner].T[None],
        wide_sum[cut_inner : 2 * cut_inner][None],
    )
    while len(proj_sum.todo) > 1:
        proj_sum.finish(*vectors_out)
    proj_sum = proj_sum.finish(token_grad, *wide_grads).astype(WIDE)

    return (
        give_back(out_own, out_other, first_stage),
        token_grad,
        jnp.transpose(proj_sum.reshape(5, cut_proj, lanes), (0, 2, 1)),
        *wide_grads,
        *small_out,
        *vectors_out,
    )


def solution(mesh):
    return jax.shard_map(
        local,
        mesh=mesh,
        in_specs=(
            P(None, ("dp", "row", "col"), None),
            P(None, ("dp", "row", "col"), None),
            P(None, "dp", ("row", "col")),
            P(None, "row", "col"),
            P("row", "col"),
            P("row", None, "col"),
            P("row", "col", None),
        )
        + (P(),) * 11,
        out_specs=(
            P(None, ("dp", "row", "col"), None),
            P(None, ("dp", "row", "col"), None),
            P(None, "row", "col"),
            P("row", "col"),
            P("row", None, "col"),
            P("row", "col", None),
        )
        + (P(),) * 11,
        check_vma=False,
    )
```
